32 devices in a mesh: dp: 4 (over x, core), seq: 8 (over z, y).
Axes of the slice: x: 2, y: 2, z: 4, core: 2. Of those that a mesh axis runs over, the one named last changes fastest.
Arguments:
- inputs: bfloat16 [4, 1024, 2048], P('dp', 'seq'), may hold values from -6 to 6
- attention_gain: bfloat16 [2048], P(('dp', 'seq')), may hold values from 0.5 to 1.5
- query_weight: bfloat16 [2048, 2048], P(('dp', 'seq')), may hold values from -0.125 to 0.125
- key_weight: bfloat16 [2048, 256], P(('dp', 'seq')), may hold values from -0.125 to 0.125
- value_weight: bfloat16 [2048, 256], P(('dp', 'seq')), may hold values from -0.125 to 0.125
- output_weight: bfloat16 [2048, 2048], P(('dp', 'seq')), may hold values from -0.5 to 0.5
- feedforward_gain: bfloat16 [2048], P(('dp', 'seq')), may hold values from 0.5 to 1.5
- gate_weight: bfloat16 [2048, 5632], P(('dp', 'seq')), may hold values from -0.125 to 0.125
- up_weight: bfloat16 [2048, 5632], P(('dp', 'seq')), may hold values from -0.125 to 0.125
- down_weight: bfloat16 [5632, 2048], P(('dp', 'seq')), may hold values from -0.078125 to 0.078125
- cotangent: bfloat16 [4, 1024, 2048], P('dp', 'seq'), may hold values from -6 to 6
Outputs:
- layer_output: bfloat16 [4, 1024, 2048], P('dp', 'seq')
- input_grad: float32 [4, 1024, 2048], P('dp', 'seq')
- attention_gain_grad: float32 [2048], P(('dp', 'seq'))
- query_grad: float32 [2048, 2048], P(('dp', 'seq'))
- key_grad: float32 [2048, 256], P(('dp', 'seq'))
- value_grad: float32 [2048, 256], P(('dp', 'seq'))
- output_grad: float32 [2048, 2048], P(('dp', 'seq'))
- feedforward_gain_grad: float32 [2048], P(('dp', 'seq'))
- gate_grad: float32 [2048, 5632], P(('dp', 'seq'))
- up_grad: float32 [2048, 5632], P(('dp', 'seq'))
- down_grad: float32 [5632, 2048], P(('dp', 'seq'))
The draws below stay inside these ranges and needn't reach their ends.
All inputs are finite; a program needn't handle non-finite values.
Results may differ from the reference program's by a relative error of at most 0.02.
Values may be sent and summed in bfloat16 or wider, within the bound.
A program may use at most 384 MiB of HBM per device.

```python
import jax
import jax.numpy as jnp
from jax import lax

D = 2048
H = 32
KV = 4
HEAD = 64
FF = 5632
SEQ_LEN = 1024
SEQS = 4
N_SEQ = 8


def steps_of(key, shape, cuts, low, largest):
    def one(position, parts):
        draws = jax.random.uniform(jax.random.fold_in(jax.random.fold_in(key, 6), position), (parts,), jnp.float32, low / len(cuts), largest / len(cuts))
        return jnp.repeat(jnp.exp(draws), shape[position] // parts).reshape((-1,) + (1,) * (len(shape) - position - 1))

    factor_of = one(*cuts[0])
    for cut in cuts[1:]:
        factor_of = factor_of * one(*cut)
    return factor_of


def gaussian(stream_key, dims, scale, limit, pieces=(), kind=jnp.bfloat16):
    array = scale * jax.random.normal(stream_key, dims, jnp.float32)
    if pieces:
        array = array * steps_of(stream_key, dims, pieces, -0.22, 0.18)
    return jnp.clip(array, -limit, limit).astype(kind)


def setup_inputs(seed: int = 0) -> dict:
    streams_of = jax.random.split(jax.random.key(seed), 12)
    inputs = gaussian(streams_of[0], (SEQS, SEQ_LEN, D), 1.0, 6.0, ((0, 4), (1, 8)))
    attention_gain = jnp.clip(1.0 + 0.1 * jax.random.normal(streams_of[1], (D,), jnp.float32), 0.5, 1.5).astype(jnp.bfloat16)
    query_weight = gaussian(streams_of[2], (D, D), D ** -0.5, 0.125, ((0, 32),))
    key_weight = gaussian(streams_of[3], (D, KV * HEAD), D ** -0.5, 0.125, ((0, 32),))
    value_weight = gaussian(streams_of[4], (D, KV * HEAD), D ** -0.5, 0.125, ((0, 32),))
    output_weight = gaussian(streams_of[5], (D, D), (max(1, D * 64 // SEQ_LEN)) ** -0.5, 0.5, ((0, 32),))
    feedforward_gain = jnp.clip(1.0 + 0.1 * jax.random.normal(streams_of[6], (D,), jnp.float32), 0.5, 1.5).astype(jnp.bfloat16)
    gate_weight = gaussian(streams_of[7], (D, FF), D ** -0.5, 0.125, ((0, 32),))
    up_weight = gaussian(streams_of[8], (D, FF), D ** -0.5, 0.125, ((0, 32),))
    down_weight = gaussian(streams_of[9], (FF, D), FF ** -0.5, 0.078125, ((0, 32),))
    cotangent = gaussian(streams_of[10], (SEQS, SEQ_LEN, D), 1.0, 6.0, ((0, 4), (1, 8)))
    return {"inputs": inputs, "attention_gain": attention_gain, "query_weight": query_weight, "key_weight": key_weight, "value_weight": value_weight, "output_weight": output_weight, "feedforward_gain": feedforward_gain, "gate_weight": gate_weight, "up_weight": up_weight, "down_weight": down_weight, "cotangent": cotangent}


epsilon = 1e-05
masked = -1e+30

@jax.custom_vjp
def low(v):
    return lax.optimization_barrier(v.astype(jnp.bfloat16)).astype(jnp.float32)

@jax.custom_vjp
def low_back(v):
    return v

def low_keep(v):
    return (low(v), None)

def low_pass(kept, grad):
    return (grad,)

def back_keep(v):
    return (v, None)

def back_low(kept, grad):
    return (low(grad),)
low.defvjp(low_keep, low_pass)
low_back.defvjp(back_keep, back_low)

def matmul(left_side, right_side):
    return jnp.dot(left_side, right_side, precision=lax.Precision.HIGHEST, preferred_element_type=jnp.float32)

def rope_tables(positions):
    half_width = HEAD // 2
    frequency = 10000.0 ** (-(jnp.arange(half_width, dtype=jnp.float32) * 2.0) / HEAD)
    angles = positions[:, None] * frequency[None, :]
    return (jnp.cos(angles), jnp.sin(angles))

def rotate(values, cosine_part, sine_part):
    half_width = HEAD // 2
    front_half = values[..., :half_width]
    back_half = values[..., half_width:]
    cosine_part = cosine_part[:, None, :]
    sine_part = sine_part[:, None, :]
    return jnp.concatenate([front_half * cosine_part - back_half * sine_part, back_half * cosine_part + front_half * sine_part], axis=-1)

def rms_scale(values):
    return lax.rsqrt(lax.optimization_barrier(jnp.mean(values * values, axis=-1, keepdims=True)) + epsilon)

def head_attention(items):
    query_head, key_head, value_head = items
    length = query_head.shape[0]
    scores = low_back(matmul(query_head, key_head.T) * HEAD ** (-0.5))
    visible = jnp.arange(length)[None, :] <= jnp.arange(length)[:, None]
    scores = jnp.where(visible, scores, masked)
    probabilities = jax.nn.softmax(scores, axis=-1)
    return matmul(low(probabilities), value_head)

def layer_forward(flattened, gain_one, query_weight, key_weight, value_weight, output_weight, gain_two, gate_weight, up_weight, down_weight):
    length = flattened.shape[0]
    heads_dev = H // N_SEQ
    repeats = N_SEQ // KV
    cosine_part, sine_part = rope_tables(jnp.arange(length).astype(jnp.float32))
    normed_one = low(flattened * rms_scale(flattened) * gain_one)
    query_raw = low_back(matmul(normed_one, query_weight)).reshape(length, H, HEAD)
    key_raw = low_back(matmul(normed_one, key_weight)).reshape(length, KV, HEAD)
    value_part = low_back(low(matmul(normed_one, value_weight))).reshape(length, KV, HEAD)
    queries = low_back(low(rotate(query_raw, cosine_part, sine_part)))
    key_rotated = low(rotate(key_raw, cosine_part, sine_part))
    key_copies = low_back(jnp.repeat(key_rotated, repeats, axis=1))
    value_copies = low_back(jnp.repeat(value_part, repeats, axis=1))
    key_heads = jnp.repeat(key_copies, heads_dev, axis=1)
    value_heads = jnp.repeat(value_copies, heads_dev, axis=1)
    attended = lax.map(jax.checkpoint(head_attention), (jnp.transpose(queries, (1, 0, 2)), jnp.transpose(key_heads, (1, 0, 2)), jnp.transpose(value_heads, (1, 0, 2))))
    attended = low_back(low(jnp.transpose(attended, (1, 0, 2)).reshape(length, H * HEAD)))
    middle = flattened + low_back(matmul(attended, output_weight))
    normed_two = low(middle * rms_scale(middle) * gain_two)
    gate_values = low_back(matmul(normed_two, gate_weight))
    up_values = low_back(matmul(normed_two, up_weight))
    hidden = low(jax.nn.silu(gate_values) * up_values)
    return middle + matmul(hidden, down_weight)

def reference(inputs, attention_gain, query_weight, key_weight, value_weight, output_weight, feedforward_gain, gate_weight, up_weight, down_weight, cotangent):
    params = (attention_gain.astype(jnp.float32), query_weight.astype(jnp.float32), key_weight.astype(jnp.float32), value_weight.astype(jnp.float32), output_weight.astype(jnp.float32), feedforward_gain.astype(jnp.float32), gate_weight.astype(jnp.float32), up_weight.astype(jnp.float32), down_weight.astype(jnp.float32))

    def one_sequence(carry, item):
        sequence_in, sequence_cot = item
        result, pullback = jax.vjp(layer_forward, sequence_in.astype(jnp.float32), *params)
        grads = pullback(sequence_cot.astype(jnp.float32))
        carry = tuple((running + piece_grad for running, piece_grad in zip(carry, grads[1:])))
        return (carry, (result.astype(jnp.bfloat16), grads[0]))
    zeros = tuple((jnp.zeros(param.shape, jnp.float32) for param in params))
    sums, (outputs, input_grads) = lax.scan(one_sequence, zeros, (inputs, cotangent))
    return (outputs, input_grads, sums[0], sums[1], sums[2], sums[3], sums[4], sums[5], sums[6], sums[7], sums[8])
```

```python
import jax
import jax.numpy as jnp
from jax import lax
from jax.sharding import PartitionSpec as P

H = 32
KV = 4
HEAD = 64

epsilon = 1e-05
masked = -1e30
f32 = jnp.float32
bf16 = jnp.bfloat16


def rope_tables(length):
    half_width = HEAD // 2
    frequency = 10000.0 ** (-(jnp.arange(half_width, dtype=f32) * 2.0) / HEAD)
    angles = jnp.arange(length, dtype=f32)[:, None] * frequency[None, :]
    return (jnp.cos(angles)[:, None, :], jnp.sin(angles)[:, None, :])


def rotate(values, cosine, sine):
    front, back = values[..., : HEAD // 2], values[..., HEAD // 2 :]
    return jnp.concatenate([front * cosine - back * sine, back * cosine + front * sine], axis=-1)


def rms_scale(values):
    return lax.rsqrt(jnp.mean(values * values, axis=-1, keepdims=True) + epsilon)


def mm(a, b):
    return lax.dot_general(a, b, (((1,), (0,)), ((), ())), preferred_element_type=f32)


def mm_nt(a, b):
    return lax.dot_general(a, b, (((1,), (1,)), ((), ())), preferred_element_type=f32)


def mm_tn(a, b):
    return lax.dot_general(a, b, (((0,), (0,)), ((), ())), preferred_element_type=f32)


def gather_seq(rows):
    return lax.all_gather(rows, "seq", axis=0, tiled=True)


def scatter_seq(rows):
    return lax.psum_scatter(rows, "seq", scatter_dimension=0, tiled=True).astype(f32)


def gather_dp(rows):
    return lax.all_gather(rows, "dp", axis=0, tiled=True)


def scatter_dp(rows):
    return lax.psum_scatter(rows, "dp", scatter_dimension=0, tiled=True)


def exchange_seq(pieces):
    return lax.all_to_all(pieces, "seq", split_axis=0, concat_axis=0, tiled=True)


def causal_mask(offset, block_rows, block_end):
    return jnp.arange(block_end)[None, :] <= (offset + jnp.arange(block_rows))[:, None]


def attention_forward(queries, keys, values, block_rows):
    outputs, totals = [], []
    for offset in range(0, queries.shape[1], block_rows):
        end = offset + block_rows
        scores = jnp.einsum(
            "hqd,kd->hqk", queries[:, offset:end], keys[:end], preferred_element_type=f32
        ) * HEAD ** (-0.5)
        scores = jnp.where(causal_mask(offset, block_rows, end), scores, masked)
        row_max = jnp.max(scores, axis=-1, keepdims=True)
        total = row_max + jnp.log(jnp.sum(jnp.exp(scores - row_max), axis=-1, keepdims=True))
        probs_low = jnp.exp(scores - total).astype(bf16)
        outputs.append(
            jnp.einsum("hqk,kd->hqd", probs_low, values[:end], preferred_element_type=f32).astype(
                bf16
            )
        )
        totals.append(total)
    return jnp.concatenate(outputs, axis=1), jnp.concatenate(totals, axis=1)


def attention_backward(queries, keys, values, grads, totals, block_rows):
    length = keys.shape[0]
    scale = HEAD ** (-0.5)
    key_sum = jnp.zeros((length, HEAD), f32)
    value_sum = jnp.zeros((length, HEAD), f32)
    query_parts = []
    for offset in range(0, length, block_rows):
        end = offset + block_rows
        query_block, grad_block = queries[:, offset:end], grads[:, offset:end]
        key_block, value_block = keys[:end], values[:end]
        scores = (
            jnp.einsum("hqd,kd->hqk", query_block, key_block, preferred_element_type=f32) * scale
        )
        scores = jnp.where(causal_mask(offset, block_rows, end), scores, masked)
        probs = jnp.exp(scores - totals[:, offset:end])
        probs_low = probs.astype(bf16)
        grad_probs = jnp.einsum(
            "hqd,kd->hqk", grad_block, value_block, preferred_element_type=f32
        )
        inner = jnp.sum(probs * grad_probs, axis=-1, keepdims=True)
        grad_scores = (probs * (grad_probs - inner)).astype(bf16)
        query_parts.append(
            jnp.einsum("hqk,kd->hqd", grad_scores, key_block, preferred_element_type=f32) * scale
        )
        padding = ((0, length - end), (0, 0))
        key_sum = key_sum + jnp.pad(
            jnp.einsum("hqk,hqd->kd", grad_scores, query_block, preferred_element_type=f32)
            * scale,
            padding,
        )
        value_sum = value_sum + jnp.pad(
            jnp.einsum("hqk,hqd->kd", probs_low, grad_block, preferred_element_type=f32), padding
        )
    return jnp.concatenate(query_parts, axis=1), key_sum, value_sum


def heads_first(flat, heads):
    return jnp.transpose(flat.reshape(flat.shape[0], heads, HEAD), (1, 0, 2))


def heads_last(stacked):
    return jnp.transpose(stacked, (1, 0, 2)).reshape(stacked.shape[1], -1)


def shards(
    inputs,
    attention_gain,
    query_weight,
    key_weight,
    value_weight,
    output_weight,
    feedforward_gain,
    gate_weight,
    up_weight,
    down_weight,
    cotangent,
):
    S, Dp = lax.axis_size("seq"), lax.axis_size("dp")
    sequences, tokens, width = inputs.shape
    length = tokens * S
    rows = query_weight.shape[0]
    heads = H // S
    q_cols = heads * HEAD
    repeats = S // KV
    down_rows = down_weight.shape[0]
    hidden = down_rows * Dp
    block_rows = min(length, max(512, length // 8))

    gain_one = attention_gain.astype(f32)[:, None]
    gain_two = feedforward_gain.astype(f32)[:, None]

    def folded(weight, gain):
        return (weight.astype(f32) * gain).astype(bf16)

    def per_group_kv(weight):
        return jnp.repeat(weight.reshape(rows, KV, HEAD), repeats, axis=1)

    def per_group_hidden(weight):
        return jnp.transpose(weight.reshape(rows, Dp, S, down_rows), (2, 0, 1, 3)).reshape(
            S, rows, hidden
        )

    packed = jnp.concatenate(
        [
            folded(query_weight, gain_one).reshape(rows, S, q_cols),
            per_group_kv(folded(key_weight, gain_one)),
            per_group_kv(folded(value_weight, gain_one)),
        ],
        axis=2,
    )
    packed = jnp.transpose(packed, (1, 0, 2))
    w_qkv = gather_dp(exchange_seq(packed).reshape(S * rows, q_cols + 2 * HEAD))
    forward_perm = [(Dp * s + d, d * S + s) for s in range(S) for d in range(Dp)]
    backward_perm = [(b, a) for a, b in forward_perm]
    w_o = gather_dp(lax.ppermute(output_weight, ("dp", "seq"), forward_perm))
    packed = jnp.concatenate(
        [
            per_group_hidden(folded(gate_weight, gain_two)),
            per_group_hidden(folded(up_weight, gain_two)),
        ],
        axis=2,
    )
    w_gu = gather_dp(exchange_seq(packed).reshape(S * rows, 2 * hidden))
    w_d = gather_dp(down_weight)

    flat = inputs.reshape(tokens, width).astype(f32)
    r1 = rms_scale(flat)
    s1 = flat * r1
    s1_all = gather_seq(s1.astype(bf16))
    cosine, sine = rope_tables(length)
    qkv = mm(s1_all, w_qkv)
    queries = rotate(qkv[:, :q_cols].reshape(length, heads, HEAD), cosine, sine).astype(bf16)
    queries = jnp.transpose(queries, (1, 0, 2))
    keys = rotate(qkv[:, None, q_cols : q_cols + HEAD], cosine, sine).astype(bf16)[:, 0]
    values = qkv[:, q_cols + HEAD :].astype(bf16)
    attended, totals = attention_forward(queries, keys, values, block_rows)
    attended = heads_last(attended)
    middle = flat + scatter_seq(mm(attended, w_o).astype(bf16))
    r2 = rms_scale(middle)
    s2 = middle * r2
    s2_all = gather_seq(s2.astype(bf16))
    gate_up = mm(s2_all, w_gu)
    gate, up = gate_up[:, :hidden], gate_up[:, hidden:]
    sig = jax.nn.sigmoid(gate)
    hid = (gate * sig * up).astype(bf16)
    output = (middle + scatter_seq(mm(hid, w_d).astype(bf16))).astype(bf16)

    dy = cotangent.reshape(tokens, width)
    dy_all = gather_seq(dy)
    d_hid = mm_nt(dy_all, w_d)
    d_gate = (d_hid * up * sig * (1.0 + gate * (1.0 - sig))).astype(bf16)
    d_up = (d_hid * (gate * sig)).astype(bf16)
    d_gu = jnp.concatenate([d_gate, d_up], axis=1)
    e2 = scatter_seq(mm_nt(d_gu, w_gu).astype(bf16))
    d_middle = dy.astype(f32) + r2 * (e2 - s2 * jnp.mean(e2 * s2, axis=-1, keepdims=True))
    dm_all = gather_seq(d_middle.astype(bf16))
    d_att = heads_first(mm_nt(dm_all, w_o).astype(bf16), heads)
    d_q, d_k, d_v = attention_backward(queries, keys, values, d_att, totals, block_rows)
    d_q = jnp.transpose(d_q, (1, 0, 2))
    d_qkv = jnp.concatenate(
        [
            rotate(d_q, cosine, -sine).reshape(length, q_cols).astype(bf16),
            rotate(d_k[:, None], cosine, -sine)[:, 0].astype(bf16),
            d_v.astype(bf16),
        ],
        axis=1,
    )
    e1 = scatter_seq(mm_nt(d_qkv, w_qkv).astype(bf16))
    input_grad = d_middle + r1 * (e1 - s1 * jnp.mean(e1 * s1, axis=-1, keepdims=True))

    down_grad = scatter_dp(mm_tn(hid, dy_all).astype(bf16)).astype(f32)
    g_gu = scatter_dp(mm_tn(s2_all, d_gu).astype(bf16))
    output_grad = lax.ppermute(
        scatter_dp(mm_tn(attended, dm_all).astype(bf16)), ("dp", "seq"), backward_perm
    ).astype(f32)
    g_qkv = scatter_dp(mm_tn(s1_all, d_qkv).astype(bf16))

    g_gu = exchange_seq(g_gu.reshape(S, rows, 2 * hidden)).astype(f32)
    g_qkv = exchange_seq(g_qkv.reshape(S, rows, q_cols + 2 * HEAD)).astype(f32)

    def back_hidden(part):
        return jnp.transpose(part.reshape(S, rows, Dp, down_rows), (1, 2, 0, 3)).reshape(rows, -1)

    def back_kv(part):
        part = jnp.sum(part.reshape(KV, repeats, rows, HEAD), axis=1)
        return jnp.transpose(part, (1, 0, 2)).reshape(rows, KV * HEAD)

    g_gate, g_up = back_hidden(g_gu[..., :hidden]), back_hidden(g_gu[..., hidden:])
    g_query = jnp.transpose(g_qkv[..., :q_cols], (1, 0, 2)).reshape(rows, width)
    g_key = back_kv(g_qkv[..., q_cols : q_cols + HEAD])
    g_value = back_kv(g_qkv[..., q_cols + HEAD :])

    def row_dot(weight, grad):
        return jnp.sum(weight.astype(f32) * grad, axis=1)

    gain_two_grad = row_dot(gate_weight, g_gate) + row_dot(up_weight, g_up)
    gain_one_grad = (
        row_dot(query_weight, g_query) + row_dot(key_weight, g_key) + row_dot(value_weight, g_value)
    )
    return (
        output.reshape(sequences, tokens, width),
        input_grad.reshape(sequences, tokens, width),
        gain_one_grad,
        g_query * gain_one,
        g_key * gain_one,
        g_value * gain_one,
        output_grad,
        gain_two_grad,
        g_gate * gain_two,
        g_up * gain_two,
        down_grad,
    )


def solution(mesh):
    both = ("dp", "seq")
    tok, vec, mat = P("dp", "seq", None), P(both), P(both, None)
    in_specs = (tok, vec, mat, mat, mat, mat, vec, mat, mat, mat, tok)
    out_specs = (tok, tok, vec, mat, mat, mat, mat, vec, mat, mat, mat)
    return jax.shard_map(shards, mesh=mesh, in_specs=in_specs, out_specs=out_specs, check_vma=False)
```

```python
import functools

import jax
import jax.numpy as jnp
from jax import lax
from jax.experimental import pallas as pl
from jax.experimental.pallas import tpu as pltpu
from jax.sharding import PartitionSpec as P

H = 32
KV = 4
HEAD = 64

epsilon = 1e-05
masked = -1e30
f32 = jnp.float32
bf16 = jnp.bfloat16


def rope_tables(length):
    half_width = HEAD // 2
    frequency = 10000.0 ** (-(jnp.arange(half_width, dtype=f32) * 2.0) / HEAD)
    angles = jnp.arange(length, dtype=f32)[:, None] * frequency[None, :]
    return (jnp.cos(angles)[:, None, :], jnp.sin(angles)[:, None, :])


def rotate(values, cosine, sine):
    front, back = values[..., : HEAD // 2], values[..., HEAD // 2 :]
    return jnp.concatenate([front * cosine - back * sine, back * cosine + front * sine], axis=-1)


def rms_scale(values):
    return lax.rsqrt(jnp.mean(values * values, axis=-1, keepdims=True) + epsilon)


def mm(a, b):
    return lax.dot_general(a, b, (((1,), (0,)), ((), ())), preferred_element_type=f32)


def mm_nt(a, b):
    return lax.dot_general(a, b, (((1,), (1,)), ((), ())), preferred_element_type=f32)


def mm_tn(a, b):
    return lax.dot_general(a, b, (((0,), (0,)), ((), ())), preferred_element_type=f32)


def seq_place():
    me = lax.axis_index("seq")
    return me // 2, me % 2

def greet(z, y, Z):
    barrier = pltpu.get_barrier_semaphore()
    def hello(peer):
        pl.semaphore_signal(barrier, inc=1, device_id={"seq": peer}, device_id_type=pl.DeviceIdType.MESH)
    hello(z * 2 + 1 - y)
    @pl.when(z > 0)
    def _(): hello(z * 2 + y - 2)
    @pl.when(z < Z - 1)
    def _(): hello(z * 2 + y + 2)
    pl.semaphore_wait(barrier, 1 + (z + Z - 1) // Z + (2 * Z - 2 - z) // Z)

def send(src, dst, ssem, rsem, peer):
    return pltpu.make_async_remote_copy(src_ref=src, dst_ref=dst, send_sem=ssem, recv_sem=rsem,
        device_id={"seq": peer}, device_id_type=pl.DeviceIdType.MESH)

def gather_kernel(Z, T, x_ref, out_ref, up_sem, dn_sem, y_sem, recv_sem, own_sem):
    z, y = seq_place()
    greet(z, y, Z)
    def block(zz, yy):
        return out_ref.at[pl.ds(pl.multiple_of((zz * 2 + yy) * T, T), T)]
    def copy(src, zz, sem, peer):
        return send(src, block(zz, y), sem.at[zz], recv_sem.at[zz * 2 + y], peer)
    own = pltpu.make_async_copy(x_ref, block(z, y), own_sem)
    own.start()
    peer_y, peer_up, peer_dn = z * 2 + 1 - y, z * 2 + y + 2, z * 2 + y - 2
    copy(x_ref, z, y_sem, peer_y).start()
    @pl.when(z < Z - 1)
    def _(): copy(x_ref, z, up_sem, peer_up).start()
    @pl.when(z > 0)
    def _(): copy(x_ref, z, dn_sem, peer_dn).start()
    for h in range(1, Z):
        @pl.when(z >= h)
        def _():
            zz = z - h
            copy(block(zz, y), zz, y_sem, peer_y).wait_recv()
            @pl.when(z < Z - 1)
            def _(): copy(block(zz, y), zz, up_sem, peer_up).start()
            copy(block(zz, y), zz, y_sem, peer_y).start()
        @pl.when(z + h < Z)
        def _():
            zz = z + h
            copy(block(zz, y), zz, y_sem, peer_y).wait_recv()
            @pl.when(z > 0)
            def _(): copy(block(zz, y), zz, dn_sem, peer_dn).start()
            copy(block(zz, y), zz, y_sem, peer_y).start()
    own.wait()
    for zz in range(Z):
        b = block(zz, 1 - y)
        send(b, b, y_sem.at[zz], recv_sem.at[zz * 2 + 1 - y], peer_y).wait_recv()
        c = copy(block(zz, y), zz, y_sem, peer_y)
        c.wait_send()
        @pl.when((zz <= z) & (z < Z - 1))
        def _(): copy(block(zz, y), zz, up_sem, peer_up).wait_send()
        @pl.when((zz >= z) & (z > 0))
        def _(): copy(block(zz, y), zz, dn_sem, peer_dn).wait_send()

def gather_line(x, cid=1):
    S = lax.axis_size("seq"); Z = S // 2
    T, D = x.shape
    return pl.pallas_call(
        functools.partial(gather_kernel, Z, T),
        out_shape=jax.ShapeDtypeStruct((S * T, D), x.dtype),
        in_specs=[pl.BlockSpec(memory_space=pltpu.VMEM)],
        out_specs=pl.BlockSpec(memory_space=pl.ANY),
        scratch_shapes=[pltpu.SemaphoreType.DMA((Z,))] * 3 + [pltpu.SemaphoreType.DMA((S,)), pltpu.SemaphoreType.DMA],
        compiler_params=pltpu.CompilerParams(collective_id=cid, has_side_effects=True),
        name="gather_seq",
    )(x)

def scatter_kernel(Z, T, p_ref, out_ref, ybuf, upbuf, dnbuf, upst, dnst, up_s, dn_s, y_s, up_r, dn_r, y_r):
    z, y = seq_place()
    greet(z, y, Z)
    peer_y, peer_up, peer_dn = z * 2 + 1 - y, z * 2 + y + 2, z * 2 + y - 2
    def mine(zz, yy):
        return p_ref.at[pl.ds(pl.multiple_of((zz * 2 + yy) * T, T), T)]
    def y_copy(zz):
        return send(mine(zz, 1 - y), ybuf.at[zz], y_s.at[zz], y_r.at[zz], peer_y)
    def up_copy(zz):
        return send(upst.at[zz], upbuf.at[zz], up_s.at[zz], up_r.at[zz], peer_up)
    def dn_copy(zz):
        return send(dnst.at[zz], dnbuf.at[zz], dn_s.at[zz], dn_r.at[zz], peer_dn)
    for h in range(Z - 1, 0, -1):
        @pl.when(z + h < Z)
        def _(): y_copy(z + h).start()
        @pl.when(z - h >= 0)
        def _(): y_copy(z - h).start()
    y_copy(z).start()
    for h in range(Z - 1, 0, -1):
        @pl.when(z + h < Z)
        def _():
            d = z + h
            y_copy(d).wait_recv()
            upst[d] = (mine(d, y)[...].astype(f32) + ybuf[d].astype(f32)).astype(bf16)
            @pl.when(z > 0)
            def _():
                up_copy(d).wait_recv()
                upst[d] = (mine(d, y)[...].astype(f32) + ybuf[d].astype(f32) + upbuf[d].astype(f32)).astype(bf16)
            up_copy(d).start()
        @pl.when(z - h >= 0)
        def _():
            d = z - h
            y_copy(d).wait_recv()
            dnst[d] = (mine(d, y)[...].astype(f32) + ybuf[d].astype(f32)).astype(bf16)
            @pl.when(z < Z - 1)
            def _():
                dn_copy(d).wait_recv()
                dnst[d] = (mine(d, y)[...].astype(f32) + ybuf[d].astype(f32) + dnbuf[d].astype(f32)).astype(bf16)
            dn_copy(d).start()
    y_copy(z).wait_recv()
    out_ref[...] = mine(z, y)[...].astype(f32) + ybuf[z].astype(f32)
    @pl.when(z > 0)
    def _():
        up_copy(z).wait_recv()
        out_ref[...] += upbuf[z].astype(f32)
    @pl.when(z < Z - 1)
    def _():
        dn_copy(z).wait_recv()
        out_ref[...] += dnbuf[z].astype(f32)
    for zz in range(Z):
        y_copy(zz).wait_send()
        @pl.when(zz > z)
        def _(): up_copy(zz).wait_send()
        @pl.when(zz < z)
        def _(): dn_copy(zz).wait_send()

def scatter_line(p, cid=2):
    S = lax.axis_size("seq"); Z = S // 2
    L, D = p.shape; T = L // S
    return pl.pallas_call(
        functools.partial(scatter_kernel, Z, T),
        out_shape=jax.ShapeDtypeStruct((T, D), f32),
        in_specs=[pl.BlockSpec(memory_space=pltpu.VMEM)],
        out_specs=pl.BlockSpec(memory_space=pltpu.VMEM),
        scratch_shapes=[pltpu.VMEM((Z, T, D), bf16)] * 5 + [pltpu.SemaphoreType.DMA((Z,))] * 6,
        compiler_params=pltpu.CompilerParams(collective_id=cid, has_side_effects=True, vmem_limit_bytes=60 << 20),
        name="scatter_seq",
    )(p)


def gather_seq(rows):
    if lax.axis_size("seq") == 8:
        return gather_line(rows)
    return lax.all_gather(rows, "seq", axis=0, tiled=True)


def scatter_seq(rows):
    if lax.axis_size("seq") == 8:
        return scatter_line(rows)
    return lax.psum_scatter(rows, "seq", scatter_dimension=0, tiled=True).astype(f32)


def gather_dp(rows):
    return lax.all_gather(rows, "dp", axis=0, tiled=True)


def scatter_dp(rows):
    return lax.psum_scatter(rows, "dp", scatter_dimension=0, tiled=True)


def exchange_seq(pieces):
    return lax.all_to_all(pieces, "seq", split_axis=0, concat_axis=0, tiled=True)


def causal_mask(offset, block_rows, block_end):
    return jnp.arange(block_end)[None, :] <= (offset + jnp.arange(block_rows))[:, None]


def attention_forward(queries, keys, values, block_rows):
    outputs, totals = [], []
    for offset in range(0, queries.shape[1], block_rows):
        end = offset + block_rows
        scores = jnp.einsum(
            "hqd,kd->hqk", queries[:, offset:end], keys[:end], preferred_element_type=f32
        ) * HEAD ** (-0.5)
        scores = jnp.where(causal_mask(offset, block_rows, end), scores, masked)
        row_max = jnp.max(scores, axis=-1, keepdims=True)
        total = row_max + jnp.log(jnp.sum(jnp.exp(scores - row_max), axis=-1, keepdims=True))
        probs_low = jnp.exp(scores - total).astype(bf16)
        outputs.append(
            jnp.einsum("hqk,kd->hqd", probs_low, values[:end], preferred_element_type=f32).astype(
                bf16
            )
        )
        totals.append(total)
    return jnp.concatenate(outputs, axis=1), jnp.concatenate(totals, axis=1)


def attention_backward(queries, keys, values, grads, totals, block_rows):
    length = keys.shape[0]
    scale = HEAD ** (-0.5)
    key_sum = jnp.zeros((length, HEAD), f32)
    value_sum = jnp.zeros((length, HEAD), f32)
    query_parts = []
    for offset in range(0, length, block_rows):
        end = offset + block_rows
        query_block, grad_block = queries[:, offset:end], grads[:, offset:end]
        key_block, value_block = keys[:end], values[:end]
        scores = (
            jnp.einsum("hqd,kd->hqk", query_block, key_block, preferred_element_type=f32) * scale
        )
        scores = jnp.where(causal_mask(offset, block_rows, end), scores, masked)
        probs = jnp.exp(scores - totals[:, offset:end])
        probs_low = probs.astype(bf16)
        grad_probs = jnp.einsum(
            "hqd,kd->hqk", grad_block, value_block, preferred_element_type=f32
        )
        inner = jnp.sum(probs * grad_probs, axis=-1, keepdims=True)
        grad_scores = (probs * (grad_probs - inner)).astype(bf16)
        query_parts.append(
            jnp.einsum("hqk,kd->hqd", grad_scores, key_block, preferred_element_type=f32) * scale
        )
        padding = ((0, length - end), (0, 0))
        key_sum = key_sum + jnp.pad(
            jnp.einsum("hqk,hqd->kd", grad_scores, query_block, preferred_element_type=f32)
            * scale,
            padding,
        )
        value_sum = value_sum + jnp.pad(
            jnp.einsum("hqk,hqd->kd", probs_low, grad_block, preferred_element_type=f32), padding
        )
    return jnp.concatenate(query_parts, axis=1), key_sum, value_sum


def heads_first(flat, heads):
    return jnp.transpose(flat.reshape(flat.shape[0], heads, HEAD), (1, 0, 2))


def heads_last(stacked):
    return jnp.transpose(stacked, (1, 0, 2)).reshape(stacked.shape[1], -1)


def shards(
    inputs,
    attention_gain,
    query_weight,
    key_weight,
    value_weight,
    output_weight,
    feedforward_gain,
    gate_weight,
    up_weight,
    down_weight,
    cotangent,
):
    S, Dp = lax.axis_size("seq"), lax.axis_size("dp")
    sequences, tokens, width = inputs.shape
    length = tokens * S
    rows = query_weight.shape[0]
    heads = H // S
    q_cols = heads * HEAD
    repeats = S // KV
    down_rows = down_weight.shape[0]
    hidden = down_rows * Dp
    block_rows = min(length, max(512, length // 8))

    gain_one = attention_gain.astype(f32)[:, None]
    gain_two = feedforward_gain.astype(f32)[:, None]

    def folded(weight, gain):
        return (weight.astype(f32) * gain).astype(bf16)

    def per_group_kv(weight):
        return jnp.repeat(weight.reshape(rows, KV, HEAD), repeats, axis=1)

    def per_group_hidden(weight):
        return jnp.transpose(weight.reshape(rows, Dp, S, down_rows), (2, 0, 1, 3)).reshape(
            S, rows, hidden
        )

    packed = jnp.concatenate(
        [
            folded(query_weight, gain_one).reshape(rows, S, q_cols),
            per_group_kv(folded(key_weight, gain_one)),
            per_group_kv(folded(value_weight, gain_one)),
        ],
        axis=2,
    )
    packed = jnp.transpose(packed, (1, 0, 2))
    w_qkv = gather_dp(exchange_seq(packed).reshape(S * rows, q_cols + 2 * HEAD))
    forward_perm = [(Dp * s + d, d * S + s) for s in range(S) for d in range(Dp)]
    backward_perm = [(b, a) for a, b in forward_perm]
    w_o = gather_dp(lax.ppermute(output_weight, ("dp", "seq"), forward_perm))
    packed = jnp.concatenate(
        [
            per_group_hidden(folded(gate_weight, gain_two)),
            per_group_hidden(folded(up_weight, gain_two)),
        ],
        axis=2,
    )
    w_gu = gather_dp(exchange_seq(packed).reshape(S * rows, 2 * hidden))
    w_d = gather_dp(down_weight)

    flat = inputs.reshape(tokens, width).astype(f32)
    r1 = rms_scale(flat)
    s1 = flat * r1
    s1_all = gather_seq(s1.astype(bf16))
    cosine, sine = rope_tables(length)
    qkv = mm(s1_all, w_qkv)
    queries = rotate(qkv[:, :q_cols].reshape(length, heads, HEAD), cosine, sine).astype(bf16)
    queries = jnp.transpose(queries, (1, 0, 2))
    keys = rotate(qkv[:, None, q_cols : q_cols + HEAD], cosine, sine).astype(bf16)[:, 0]
    values = qkv[:, q_cols + HEAD :].astype(bf16)
    attended, totals = attention_forward(queries, keys, values, block_rows)
    attended = heads_last(attended)
    middle = flat + scatter_seq(mm(attended, w_o).astype(bf16))
    r2 = rms_scale(middle)
    s2 = middle * r2
    s2_all = gather_seq(s2.astype(bf16))
    gate_up = mm(s2_all, w_gu)
    gate, up = gate_up[:, :hidden], gate_up[:, hidden:]
    sig = jax.nn.sigmoid(gate)
    hid = (gate * sig * up).astype(bf16)
    output = (middle + scatter_seq(mm(hid, w_d).astype(bf16))).astype(bf16)

    dy = cotangent.reshape(tokens, width)
    dy_all = gather_seq(dy)
    d_hid = mm_nt(dy_all, w_d)
    d_gate = (d_hid * up * sig * (1.0 + gate * (1.0 - sig))).astype(bf16)
    d_up = (d_hid * (gate * sig)).astype(bf16)
    d_gu = jnp.concatenate([d_gate, d_up], axis=1)
    e2 = scatter_seq(mm_nt(d_gu, w_gu).astype(bf16))
    d_middle = dy.astype(f32) + r2 * (e2 - s2 * jnp.mean(e2 * s2, axis=-1, keepdims=True))
    dm_all = gather_seq(d_middle.astype(bf16))
    d_att = heads_first(mm_nt(dm_all, w_o).astype(bf16), heads)
    d_q, d_k, d_v = attention_backward(queries, keys, values, d_att, totals, block_rows)
    d_q = jnp.transpose(d_q, (1, 0, 2))
    d_qkv = jnp.concatenate(
        [
            rotate(d_q, cosine, -sine).reshape(length, q_cols).astype(bf16),
            rotate(d_k[:, None], cosine, -sine)[:, 0].astype(bf16),
            d_v.astype(bf16),
        ],
        axis=1,
    )
    e1 = scatter_seq(mm_nt(d_qkv, w_qkv).astype(bf16))
    input_grad = d_middle + r1 * (e1 - s1 * jnp.mean(e1 * s1, axis=-1, keepdims=True))

    down_grad = scatter_dp(mm_tn(hid, dy_all).astype(bf16)).astype(f32)
    g_gu = scatter_dp(mm_tn(s2_all, d_gu).astype(bf16))
    output_grad = lax.ppermute(
        scatter_dp(mm_tn(attended, dm_all).astype(bf16)), ("dp", "seq"), backward_perm
    ).astype(f32)
    g_qkv = scatter_dp(mm_tn(s1_all, d_qkv).astype(bf16))

    g_gu = exchange_seq(g_gu.reshape(S, rows, 2 * hidden)).astype(f32)
    g_qkv = exchange_seq(g_qkv.reshape(S, rows, q_cols + 2 * HEAD)).astype(f32)

    def back_hidden(part):
        return jnp.transpose(part.reshape(S, rows, Dp, down_rows), (1, 2, 0, 3)).reshape(rows, -1)

    def back_kv(part):
        part = jnp.sum(part.reshape(KV, repeats, rows, HEAD), axis=1)
        return jnp.transpose(part, (1, 0, 2)).reshape(rows, KV * HEAD)

    g_gate, g_up = back_hidden(g_gu[..., :hidden]), back_hidden(g_gu[..., hidden:])
    g_query = jnp.transpose(g_qkv[..., :q_cols], (1, 0, 2)).reshape(rows, width)
    g_key = back_kv(g_qkv[..., q_cols : q_cols + HEAD])
    g_value = back_kv(g_qkv[..., q_cols + HEAD :])

    def row_dot(weight, grad):
        return jnp.sum(weight.astype(f32) * grad, axis=1)

    gain_two_grad = row_dot(gate_weight, g_gate) + row_dot(up_weight, g_up)
    gain_one_grad = (
        row_dot(query_weight, g_query) + row_dot(key_weight, g_key) + row_dot(value_weight, g_value)
    )
    return (
        output.reshape(sequences, tokens, width),
        input_grad.reshape(sequences, tokens, width),
        gain_one_grad,
        g_query * gain_one,
        g_key * gain_one,
        g_value * gain_one,
        output_grad,
        gain_two_grad,
        g_gate * gain_two,
        g_up * gain_two,
        down_grad,
    )


def solution(mesh):
    both = ("dp", "seq")
    tok, vec, mat = P("dp", "seq", None), P(both), P(both, None)
    in_specs = (tok, vec, mat, mat, mat, mat, vec, mat, mat, mat, tok)
    out_specs = (tok, tok, vec, mat, mat, mat, mat, vec, mat, mat, mat)
    return jax.shard_map(shards, mesh=mesh, in_specs=in_specs, out_specs=out_specs, check_vma=False)
```

```python
import functools

import jax
import jax.numpy as jnp
from jax import lax
from jax.experimental import pallas as pl
from jax.experimental.pallas import tpu as pltpu
from jax.sharding import PartitionSpec as P

H = 32
KV = 4
HEAD = 64

epsilon = 1e-05
masked = -1e30
f32 = jnp.float32
bf16 = jnp.bfloat16


def rope_tables(length):
    half_width = HEAD // 2
    frequency = 10000.0 ** (-(jnp.arange(half_width, dtype=f32) * 2.0) / HEAD)
    angles = jnp.arange(length, dtype=f32)[:, None] * frequency[None, :]
    return (jnp.cos(angles)[:, None, :], jnp.sin(angles)[:, None, :])


def rotate(values, cosine, sine):
    front, back = values[..., : HEAD // 2], values[..., HEAD // 2 :]
    return jnp.concatenate([front * cosine - back * sine, back * cosine + front * sine], axis=-1)


def rms_scale(values):
    return lax.rsqrt(jnp.mean(values * values, axis=-1, keepdims=True) + epsilon)


def mm(a, b):
    return lax.dot_general(a, b, (((1,), (0,)), ((), ())), preferred_element_type=f32)


def mm_nt(a, b):
    return lax.dot_general(a, b, (((1,), (1,)), ((), ())), preferred_element_type=f32)


def mm_tn(a, b):
    return lax.dot_general(a, b, (((0,), (0,)), ((), ())), preferred_element_type=f32)


def seq_place():
    me = lax.axis_index("seq")
    return me // 2, me % 2

def greet(z, y, Z):
    barrier = pltpu.get_barrier_semaphore()
    def hello(peer):
        pl.semaphore_signal(barrier, inc=1, device_id={"seq": peer}, device_id_type=pl.DeviceIdType.MESH)
    hello(z * 2 + 1 - y)
    @pl.when(z > 0)
    def _(): hello(z * 2 + y - 2)
    @pl.when(z < Z - 1)
    def _(): hello(z * 2 + y + 2)
    pl.semaphore_wait(barrier, 1 + (z + Z - 1) // Z + (2 * Z - 2 - z) // Z)

def send(src, dst, ssem, rsem, peer):
    return pltpu.make_async_remote_copy(src_ref=src, dst_ref=dst, send_sem=ssem, recv_sem=rsem,
        device_id={"seq": peer}, device_id_type=pl.DeviceIdType.MESH)

def gather_kernel(Z, T, x_ref, out_ref, up_sem, dn_sem, y_sem, recv_sem, own_sem):
    z, y = seq_place()
    greet(z, y, Z)
    def block(zz, yy):
        return out_ref.at[pl.ds(pl.multiple_of((zz * 2 + yy) * T, T), T)]
    def copy(src, zz, sem, peer):
        return send(src, block(zz, y), sem.at[zz], recv_sem.at[zz * 2 + y], peer)
    own = pltpu.make_async_copy(x_ref, block(z, y), own_sem)
    own.start()
    peer_y, peer_up, peer_dn = z * 2 + 1 - y, z * 2 + y + 2, z * 2 + y - 2
    copy(x_ref, z, y_sem, peer_y).start()
    @pl.when(z < Z - 1)
    def _(): copy(x_ref, z, up_sem, peer_up).start()
    @pl.when(z > 0)
    def _(): copy(x_ref, z, dn_sem, peer_dn).start()
    for h in range(1, Z):
        @pl.when(z >= h)
        def _():
            zz = z - h
            copy(block(zz, y), zz, y_sem, peer_y).wait_recv()
            @pl.when(z < Z - 1)
            def _(): copy(block(zz, y), zz, up_sem, peer_up).start()
            copy(block(zz, y), zz, y_sem, peer_y).start()
        @pl.when(z + h < Z)
        def _():
            zz = z + h
            copy(block(zz, y), zz, y_sem, peer_y).wait_recv()
            @pl.when(z > 0)
            def _(): copy(block(zz, y), zz, dn_sem, peer_dn).start()
            copy(block(zz, y), zz, y_sem, peer_y).start()
    own.wait()
    for zz in range(Z):
        b = block(zz, 1 - y)
        send(b, b, y_sem.at[zz], recv_sem.at[zz * 2 + 1 - y], peer_y).wait_recv()
        c = copy(block(zz, y), zz, y_sem, peer_y)
        c.wait_send()
        @pl.when((zz <= z) & (z < Z - 1))
        def _(): copy(block(zz, y), zz, up_sem, peer_up).wait_send()
        @pl.when((zz >= z) & (z > 0))
        def _(): copy(block(zz, y), zz, dn_sem, peer_dn).wait_send()

def gather_line(x, cid=1):
    S = lax.axis_size("seq"); Z = S // 2
    T, D = x.shape
    return pl.pallas_call(
        functools.partial(gather_kernel, Z, T),
        out_shape=jax.ShapeDtypeStruct((S * T, D), x.dtype),
        in_specs=[pl.BlockSpec(memory_space=pltpu.VMEM)],
        out_specs=pl.BlockSpec(memory_space=pl.ANY),
        scratch_shapes=[pltpu.SemaphoreType.DMA((Z,))] * 3 + [pltpu.SemaphoreType.DMA((S,)), pltpu.SemaphoreType.DMA],
        compiler_params=pltpu.CompilerParams(collective_id=cid, has_side_effects=True),
        name="gather_seq",
    )(x)

def scatter_kernel(Z, T, p_ref, out_ref, ybuf, upbuf, dnbuf, upst, dnst, up_s, dn_s, y_s, up_r, dn_r, y_r):
    z, y = seq_place()
    greet(z, y, Z)
    peer_y, peer_up, peer_dn = z * 2 + 1 - y, z * 2 + y + 2, z * 2 + y - 2
    def mine(zz, yy):
        return p_ref.at[pl.ds(pl.multiple_of((zz * 2 + yy) * T, T), T)]
    def y_copy(zz):
        return send(mine(zz, 1 - y), ybuf.at[zz], y_s.at[zz], y_r.at[zz], peer_y)
    def up_copy(zz):
        return send(upst.at[zz], upbuf.at[zz], up_s.at[zz], up_r.at[zz], peer_up)
    def dn_copy(zz):
        return send(dnst.at[zz], dnbuf.at[zz], dn_s.at[zz], dn_r.at[zz], peer_dn)
    for h in range(Z - 1, 0, -1):
        @pl.when(z + h < Z)
        def _(): y_copy(z + h).start()
        @pl.when(z - h >= 0)
        def _(): y_copy(z - h).start()
    y_copy(z).start()
    for h in range(Z - 1, 0, -1):
        @pl.when(z + h < Z)
        def _():
            d = z + h
            y_copy(d).wait_recv()
            upst[d] = (mine(d, y)[...].astype(f32) + ybuf[d].astype(f32)).astype(bf16)
            @pl.when(z > 0)
            def _():
                up_copy(d).wait_recv()
                upst[d] = (mine(d, y)[...].astype(f32) + ybuf[d].astype(f32) + upbuf[d].astype(f32)).astype(bf16)
            up_copy(d).start()
        @pl.when(z - h >= 0)
        def _():
            d = z - h
            y_copy(d).wait_recv()
            dnst[d] = (mine(d, y)[...].astype(f32) + ybuf[d].astype(f32)).astype(bf16)
            @pl.when(z < Z - 1)
            def _():
                dn_copy(d).wait_recv()
                dnst[d] = (mine(d, y)[...].astype(f32) + ybuf[d].astype(f32) + dnbuf[d].astype(f32)).astype(bf16)
            dn_copy(d).start()
    y_copy(z).wait_recv()
    out_ref[...] = mine(z, y)[...].astype(f32) + ybuf[z].astype(f32)
    @pl.when(z > 0)
    def _():
        up_copy(z).wait_recv()
        out_ref[...] += upbuf[z].astype(f32)
    @pl.when(z < Z - 1)
    def _():
        dn_copy(z).wait_recv()
        out_ref[...] += dnbuf[z].astype(f32)
    for zz in range(Z):
        y_copy(zz).wait_send()
        @pl.when(zz > z)
        def _(): up_copy(zz).wait_send()
        @pl.when(zz < z)
        def _(): dn_copy(zz).wait_send()

def scatter_line(p, cid=2):
    S = lax.axis_size("seq"); Z = S // 2
    L, D = p.shape; T = L // S
    return pl.pallas_call(
        functools.partial(scatter_kernel, Z, T),
        out_shape=jax.ShapeDtypeStruct((T, D), f32),
        in_specs=[pl.BlockSpec(memory_space=pltpu.VMEM)],
        out_specs=pl.BlockSpec(memory_space=pltpu.VMEM),
        scratch_shapes=[pltpu.VMEM((Z, T, D), bf16)] * 5 + [pltpu.SemaphoreType.DMA((Z,))] * 6,
        compiler_params=pltpu.CompilerParams(collective_id=cid, has_side_effects=True, vmem_limit_bytes=60 << 20),
        name="scatter_seq",
    )(p)


def line_rank(i, z):
    upper = z // 2
    inner = (z + upper) % 2
    base = i + inner * (1 - i // 2) * (1 - 2 * i)
    return base + upper * (3 - 2 * base)


def above(d, z):
    return (d - z + 3) // 4


def rows_of(ref, start, size):
    return ref.at[pl.ds(pl.multiple_of(start, size), size)]


class Gather:
    def __init__(self, z, y, T, own, full, up_sem, dn_sem, y_sem, recv_sem, own_sem):
        self.z, self.y, self.T, self.own, self.full = z, y, T, own, full
        self.sems = {"up": up_sem, "dn": dn_sem, "y": y_sem}
        self.peers = {"up": z * 2 + y + 2, "dn": z * 2 + y - 2, "y": z * 2 + 1 - y}
        self.recv_sem, self.own_sem = recv_sem, own_sem

    def block(self, zz, yy):
        return rows_of(self.full, (zz * 2 + yy) * self.T, self.T)

    def copy(self, src, zz, way):
        return send(
            src,
            self.block(zz, self.y),
            self.sems[way].at[zz],
            self.recv_sem.at[zz * 2 + self.y],
            self.peers[way],
        )

    def start(self):
        z = self.z
        pltpu.make_async_copy(self.own, self.block(z, self.y), self.own_sem).start()
        self.copy(self.own, z, "y").start()

        @pl.when(z < 3)
        def _():
            self.copy(self.own, z, "up").start()

        @pl.when(z > 0)
        def _():
            self.copy(self.own, z, "dn").start()

    def own_ready(self):
        pltpu.make_async_copy(self.own, self.block(self.z, self.y), self.own_sem).wait()

    def hop(self, h):
        z = self.z

        @pl.when(z >= h)
        def _():
            src = self.block(z - h, self.y)
            self.copy(src, z - h, "y").wait_recv()

            @pl.when(z < 3)
            def _():
                self.copy(src, z - h, "up").start()

            self.copy(src, z - h, "y").start()

        @pl.when(z + h < 4)
        def _():
            src = self.block(z + h, self.y)
            self.copy(src, z + h, "y").wait_recv()

            @pl.when(z > 0)
            def _():
                self.copy(src, z + h, "dn").start()

            self.copy(src, z + h, "y").start()

    def pair_ready(self, zz):
        b = self.block(zz, 1 - self.y)
        send(
            b, b, self.sems["y"].at[zz], self.recv_sem.at[zz * 2 + 1 - self.y], self.peers["y"]
        ).wait_recv()

    def finish(self):
        z = self.z
        for zz in range(4):
            src = self.block(zz, self.y)
            self.copy(src, zz, "y").wait_send()

            @pl.when((zz <= z) & (z < 3))
            def _():
                self.copy(src, zz, "up").wait_send()

            @pl.when((zz >= z) & (z > 0))
            def _():
                self.copy(src, zz, "dn").wait_send()


class Scatter:
    def __init__(self, z, y, T, part, ybuf, rbuf, stage, y_s, y_r, z_s, z_r):
        self.z, self.y, self.T, self.part = z, y, T, part
        self.ybuf, self.rbuf, self.stage = ybuf, rbuf, stage
        self.y_s, self.y_r, self.z_s, self.z_r = y_s, y_r, z_s, z_r

    def rows(self, zz, yy):
        return rows_of(self.part, (zz * 2 + yy) * self.T, self.T)

    def y_copy(self, d):
        peer = self.z * 2 + 1 - self.y
        return send(
            self.rows(d, 1 - self.y), self.ybuf.at[d], self.y_s.at[d], self.y_r.at[d], peer
        )

    def z_copy(self, d, up):
        slot = d + up
        peer = self.z * 2 + self.y + 4 * up - 2
        return send(self.stage.at[d], self.rbuf.at[slot], self.z_s.at[d], self.z_r.at[slot], peer)

    def start(self, d):
        self.y_copy(d).start()

    def pass_on(self, d):
        z = self.z
        up = above(d, z)
        self.y_copy(d).wait_recv()
        total = self.rows(d, self.y)[...].astype(f32) + self.ybuf[d].astype(f32)
        inner = (z > 0) & (z < 3)

        @pl.when(inner)
        def _():
            self.z_copy(d, up).wait_recv()
            self.stage[d] = (total + self.rbuf[d + up].astype(f32)).astype(bf16)

        @pl.when(jnp.logical_not(inner))
        def _():
            self.stage[d] = total.astype(bf16)

        self.z_copy(d, up).start()

    def finish(self, out_ref):
        z = self.z
        self.y_copy(z).wait_recv()
        out_ref[...] = self.rows(z, self.y)[...].astype(f32) + self.ybuf[z].astype(f32)

        @pl.when(z > 0)
        def _():
            self.z_copy(z, 1).wait_recv()
            out_ref[...] += self.rbuf[z + 1].astype(f32)

        @pl.when(z < 3)
        def _():
            self.z_copy(z, 0).wait_recv()
            out_ref[...] += self.rbuf[z].astype(f32)

        for d in range(4):
            self.y_copy(d).wait_send()

            @pl.when(z != d)
            def _():
                self.z_copy(d, above(d, z)).wait_send()


def line_sems(n):
    return [pltpu.SemaphoreType.DMA((4,))] * 3 + [
        pltpu.SemaphoreType.DMA((8,)),
        pltpu.SemaphoreType.DMA,
    ]


def sum_scratch(T, width):
    return [
        pltpu.VMEM((4, T, width), bf16),
        pltpu.VMEM((5, T, width), bf16),
        pltpu.VMEM((4, T, width), bf16),
        pltpu.SemaphoreType.DMA((4,)),
        pltpu.SemaphoreType.DMA((4,)),
        pltpu.SemaphoreType.DMA((4,)),
        pltpu.SemaphoreType.DMA((5,)),
    ]


def feedforward_kernel(
    T, x_ref, dy_ref, wgu_ref, wd_ref, pout_ref, e2_ref, ggu_ref, gd_ref,
    full, hid, dgu, part, up_sem, dn_sem, ag_y, ag_r, own_sem,
    ybuf, rbuf, stage, y_s, y_r, z_s, z_r,
):
    z, y = seq_place()
    F = hid.shape[1]
    greet(z, y, 4)
    gather = Gather(z, y, T, x_ref, full, up_sem, dn_sem, ag_y, ag_r, own_sem)
    scatter = Scatter(z, y, T, part, ybuf, rbuf, stage, y_s, y_r, z_s, z_r)
    gather.start()
    gather.own_ready()

    def compute(i, carry):
        for h in range(1, 4):

            @pl.when(i == h - 1)
            def _():
                gather.hop(h)

        zz = line_rank(i, z)
        gather.pair_ready(zz)

        @pl.when(i == 3)
        def _():
            scatter.start(line_rank(2, z))

        r = pl.ds(pl.multiple_of(zz * 2 * T, 2 * T), 2 * T)
        gu = mm(full[r, :], wgu_ref[...])
        gate, up = gu[:, :F], gu[:, F:]
        sig = 1.0 / (1.0 + jnp.exp(-gate))
        act = gate * sig
        h = (act * up).astype(bf16)
        hid[r, :] = h
        pout_ref[r, :] = mm(h, wd_ref[...]).astype(bf16)
        dh = mm_nt(dy_ref[r, :], wd_ref[...])
        dgu[r, :F] = (dh * up * sig * (1.0 + gate * (1.0 - sig))).astype(bf16)
        dgu[r, F:] = (dh * act).astype(bf16)
        part[r, :] = mm_nt(dgu[r, :], wgu_ref[...]).astype(bf16)
        return carry

    lax.fori_loop(0, 4, compute, 0)
    for i in (3, 1, 0):
        scatter.start(line_rank(i, z))

    def gate_up_tile(i, carry):
        r = pl.ds(pl.multiple_of(i * 256, 256), 256)
        ggu_ref[r, :] = mm_tn(full[:, r], dgu[...]).astype(bf16)
        return carry

    def down_tile(i, carry):
        r = pl.ds(pl.multiple_of(i * 256, 256), 256)
        gd_ref[r, :] = mm_tn(hid[:, r], dy_ref[...]).astype(bf16)
        return carry

    lax.fori_loop(0, 4, gate_up_tile, 0)
    scatter.pass_on(line_rank(3, z))
    lax.fori_loop(4, 8, gate_up_tile, 0)
    scatter.pass_on(line_rank(2, z))
    lax.fori_loop(0, F // 256, down_tile, 0)
    scatter.pass_on(line_rank(1, z))
    scatter.finish(e2_ref)
    gather.finish()


def feedforward(x, dy_all, w_gu, w_d, cid=3):
    T, width = x.shape
    L, F = dy_all.shape[0], w_d.shape[0]
    vmem = pl.BlockSpec(memory_space=pltpu.VMEM)
    return pl.pallas_call(
        functools.partial(feedforward_kernel, T),
        out_shape=(
            jax.ShapeDtypeStruct((L, width), bf16),
            jax.ShapeDtypeStruct((T, width), f32),
            jax.ShapeDtypeStruct((width, 2 * F), bf16),
            jax.ShapeDtypeStruct((F, width), bf16),
        ),
        in_specs=[vmem] * 4,
        out_specs=(vmem,) * 4,
        scratch_shapes=[
            pltpu.VMEM((L, width), bf16),
            pltpu.VMEM((L, F), bf16),
            pltpu.VMEM((L, 2 * F), bf16),
            pltpu.VMEM((L, width), bf16),
        ]
        + line_sems(4)
        + sum_scratch(T, width),
        compiler_params=pltpu.CompilerParams(
            collective_id=cid, has_side_effects=True, vmem_limit_bytes=67000000
        ),
        name="feedforward",
    )(x, dy_all, w_gu, w_d)


def gather_seq(rows):
    if lax.axis_size("seq") == 8:
        return gather_line(rows)
    return lax.all_gather(rows, "seq", axis=0, tiled=True)


def scatter_seq(rows):
    if lax.axis_size("seq") == 8:
        return scatter_line(rows)
    return lax.psum_scatter(rows, "seq", scatter_dimension=0, tiled=True).astype(f32)


def feedforward_plain(x, dy_all, w_gu, w_d):
    hidden = w_d.shape[0]
    s2_all = gather_seq(x)
    gate_up = mm(s2_all, w_gu)
    gate, up = gate_up[:, :hidden], gate_up[:, hidden:]
    sig = jax.nn.sigmoid(gate)
    hid = (gate * sig * up).astype(bf16)
    d_hid = mm_nt(dy_all, w_d)
    d_gate = (d_hid * up * sig * (1.0 + gate * (1.0 - sig))).astype(bf16)
    d_up = (d_hid * (gate * sig)).astype(bf16)
    d_gu = jnp.concatenate([d_gate, d_up], axis=1)
    return (
        mm(hid, w_d).astype(bf16),
        scatter_seq(mm_nt(d_gu, w_gu).astype(bf16)),
        mm_tn(s2_all, d_gu).astype(bf16),
        mm_tn(hid, dy_all).astype(bf16),
    )


def gather_dp(rows):
    return lax.all_gather(rows, "dp", axis=0, tiled=True)


def scatter_dp(rows):
    return lax.psum_scatter(rows, "dp", scatter_dimension=0, tiled=True)


def exchange_seq(pieces):
    return lax.all_to_all(pieces, "seq", split_axis=0, concat_axis=0, tiled=True)


def causal_mask(offset, block_rows, block_end):
    return jnp.arange(block_end)[None, :] <= (offset + jnp.arange(block_rows))[:, None]


def attention_forward(queries, keys, values, block_rows):
    outputs, totals = [], []
    for offset in range(0, queries.shape[1], block_rows):
        end = offset + block_rows
        scores = jnp.einsum(
            "hqd,kd->hqk", queries[:, offset:end], keys[:end], preferred_element_type=f32
        ) * HEAD ** (-0.5)
        scores = jnp.where(causal_mask(offset, block_rows, end), scores, masked)
        row_max = jnp.max(scores, axis=-1, keepdims=True)
        total = row_max + jnp.log(jnp.sum(jnp.exp(scores - row_max), axis=-1, keepdims=True))
        probs_low = jnp.exp(scores - total).astype(bf16)
        outputs.append(
            jnp.einsum("hqk,kd->hqd", probs_low, values[:end], preferred_element_type=f32).astype(
                bf16
            )
        )
        totals.append(total)
    return jnp.concatenate(outputs, axis=1), jnp.concatenate(totals, axis=1)


def attention_backward(queries, keys, values, grads, totals, block_rows):
    length = keys.shape[0]
    scale = HEAD ** (-0.5)
    key_sum = jnp.zeros((length, HEAD), f32)
    value_sum = jnp.zeros((length, HEAD), f32)
    query_parts = []
    for offset in range(0, length, block_rows):
        end = offset + block_rows
        query_block, grad_block = queries[:, offset:end], grads[:, offset:end]
        key_block, value_block = keys[:end], values[:end]
        scores = (
            jnp.einsum("hqd,kd->hqk", query_block, key_block, preferred_element_type=f32) * scale
        )
        scores = jnp.where(causal_mask(offset, block_rows, end), scores, masked)
        probs = jnp.exp(scores - totals[:, offset:end])
        probs_low = probs.astype(bf16)
        grad_probs = jnp.einsum(
            "hqd,kd->hqk", grad_block, value_block, preferred_element_type=f32
        )
        inner = jnp.sum(probs * grad_probs, axis=-1, keepdims=True)
        grad_scores = (probs * (grad_probs - inner)).astype(bf16)
        query_parts.append(
            jnp.einsum("hqk,kd->hqd", grad_scores, key_block, preferred_element_type=f32) * scale
        )
        padding = ((0, length - end), (0, 0))
        key_sum = key_sum + jnp.pad(
            jnp.einsum("hqk,hqd->kd", grad_scores, query_block, preferred_element_type=f32)
            * scale,
            padding,
        )
        value_sum = value_sum + jnp.pad(
            jnp.einsum("hqk,hqd->kd", probs_low, grad_block, preferred_element_type=f32), padding
        )
    return jnp.concatenate(query_parts, axis=1), key_sum, value_sum


def heads_first(flat, heads):
    return jnp.transpose(flat.reshape(flat.shape[0], heads, HEAD), (1, 0, 2))


def heads_last(stacked):
    return jnp.transpose(stacked, (1, 0, 2)).reshape(stacked.shape[1], -1)


def shards(
    inputs,
    attention_gain,
    query_weight,
    key_weight,
    value_weight,
    output_weight,
    feedforward_gain,
    gate_weight,
    up_weight,
    down_weight,
    cotangent,
):
    S, Dp = lax.axis_size("seq"), lax.axis_size("dp")
    sequences, tokens, width = inputs.shape
    length = tokens * S
    rows = query_weight.shape[0]
    heads = H // S
    q_cols = heads * HEAD
    repeats = S // KV
    down_rows = down_weight.shape[0]
    hidden = down_rows * Dp
    block_rows = min(length, max(512, length // 8))

    gain_one = attention_gain.astype(f32)[:, None]
    gain_two = feedforward_gain.astype(f32)[:, None]

    def folded(weight, gain):
        return (weight.astype(f32) * gain).astype(bf16)

    def per_group_kv(weight):
        return jnp.repeat(weight.reshape(rows, KV, HEAD), repeats, axis=1)

    def per_group_hidden(weight):
        return jnp.transpose(weight.reshape(rows, Dp, S, down_rows), (2, 0, 1, 3)).reshape(
            S, rows, hidden
        )

    packed = jnp.concatenate(
        [
            folded(query_weight, gain_one).reshape(rows, S, q_cols),
            per_group_kv(folded(key_weight, gain_one)),
            per_group_kv(folded(value_weight, gain_one)),
        ],
        axis=2,
    )
    packed = jnp.transpose(packed, (1, 0, 2))
    w_qkv = gather_dp(exchange_seq(packed).reshape(S * rows, q_cols + 2 * HEAD))
    forward_perm = [(Dp * s + d, d * S + s) for s in range(S) for d in range(Dp)]
    backward_perm = [(b, a) for a, b in forward_perm]
    w_o = gather_dp(lax.ppermute(output_weight, ("dp", "seq"), forward_perm))
    packed = jnp.concatenate(
        [
            per_group_hidden(folded(gate_weight, gain_two)),
            per_group_hidden(folded(up_weight, gain_two)),
        ],
        axis=2,
    )
    line = S == 8
    width_f = -(-hidden // 256) * 256 if line else hidden

    def padded(part, axis):
        pads = [(0, 0)] * part.ndim
        pads[axis] = (0, width_f - hidden)
        return jnp.pad(part, pads)

    packed = exchange_seq(packed).reshape(S * rows, 2 * hidden)
    packed = jnp.concatenate(
        [padded(packed[:, :hidden], 1), padded(packed[:, hidden:], 1)], axis=1
    )
    w_gu = gather_dp(packed)
    w_d = padded(gather_dp(down_weight), 0)

    flat = inputs.reshape(tokens, width).astype(f32)
    r1 = rms_scale(flat)
    s1 = flat * r1
    s1_all = gather_seq(s1.astype(bf16))
    cosine, sine = rope_tables(length)
    qkv = mm(s1_all, w_qkv)
    queries = rotate(qkv[:, :q_cols].reshape(length, heads, HEAD), cosine, sine).astype(bf16)
    queries = jnp.transpose(queries, (1, 0, 2))
    keys = rotate(qkv[:, None, q_cols : q_cols + HEAD], cosine, sine).astype(bf16)[:, 0]
    values = qkv[:, q_cols + HEAD :].astype(bf16)
    attended, totals = attention_forward(queries, keys, values, block_rows)
    attended = heads_last(attended)
    middle = flat + scatter_seq(mm(attended, w_o).astype(bf16))
    r2 = rms_scale(middle)
    s2 = middle * r2
    dy = cotangent.reshape(tokens, width)
    dy_all = gather_seq(dy)
    block = feedforward if line else feedforward_plain
    out_part, e2, g_gu, g_down = block(s2.astype(bf16), dy_all, w_gu, w_d)
    output = (middle + scatter_seq(out_part)).astype(bf16)

    d_middle = dy.astype(f32) + r2 * (e2 - s2 * jnp.mean(e2 * s2, axis=-1, keepdims=True))
    dm_all = gather_seq(d_middle.astype(bf16))
    d_att = heads_first(mm_nt(dm_all, w_o).astype(bf16), heads)
    d_q, d_k, d_v = attention_backward(queries, keys, values, d_att, totals, block_rows)
    d_q = jnp.transpose(d_q, (1, 0, 2))
    d_qkv = jnp.concatenate(
        [
            rotate(d_q, cosine, -sine).reshape(length, q_cols).astype(bf16),
            rotate(d_k[:, None], cosine, -sine)[:, 0].astype(bf16),
            d_v.astype(bf16),
        ],
        axis=1,
    )
    e1 = scatter_seq(mm_nt(d_qkv, w_qkv).astype(bf16))
    input_grad = d_middle + r1 * (e1 - s1 * jnp.mean(e1 * s1, axis=-1, keepdims=True))

    down_grad = scatter_dp(g_down[:hidden]).astype(f32)
    g_gu = scatter_dp(g_gu)
    g_gu = jnp.concatenate([g_gu[:, :hidden], g_gu[:, width_f : width_f + hidden]], axis=1)
    output_grad = lax.ppermute(
        scatter_dp(mm_tn(attended, dm_all).astype(bf16)), ("dp", "seq"), backward_perm
    ).astype(f32)
    g_qkv = scatter_dp(mm_tn(s1_all, d_qkv).astype(bf16))

    g_gu = exchange_seq(g_gu.reshape(S, rows, 2 * hidden)).astype(f32)
    g_qkv = exchange_seq(g_qkv.reshape(S, rows, q_cols + 2 * HEAD)).astype(f32)

    def back_hidden(part):
        return jnp.transpose(part.reshape(S, rows, Dp, down_rows), (1, 2, 0, 3)).reshape(rows, -1)

    def back_kv(part):
        part = jnp.sum(part.reshape(KV, repeats, rows, HEAD), axis=1)
        return jnp.transpose(part, (1, 0, 2)).reshape(rows, KV * HEAD)

    g_gate, g_up = back_hidden(g_gu[..., :hidden]), back_hidden(g_gu[..., hidden:])
    g_query = jnp.transpose(g_qkv[..., :q_cols], (1, 0, 2)).reshape(rows, width)
    g_key = back_kv(g_qkv[..., q_cols : q_cols + HEAD])
    g_value = back_kv(g_qkv[..., q_cols + HEAD :])

    def row_dot(weight, grad):
        return jnp.sum(weight.astype(f32) * grad, axis=1)

    gain_two_grad = row_dot(gate_weight, g_gate) + row_dot(up_weight, g_up)
    gain_one_grad = (
        row_dot(query_weight, g_query) + row_dot(key_weight, g_key) + row_dot(value_weight, g_value)
    )
    return (
        output.reshape(sequences, tokens, width),
        input_grad.reshape(sequences, tokens, width),
        gain_one_grad,
        g_query * gain_one,
        g_key * gain_one,
        g_value * gain_one,
        output_grad,
        gain_two_grad,
        g_gate * gain_two,
        g_up * gain_two,
        down_grad,
    )


def solution(mesh):
    both = ("dp", "seq")
    tok, vec, mat = P("dp", "seq", None), P(both), P(both, None)
    in_specs = (tok, vec, mat, mat, mat, mat, vec, mat, mat, mat, tok)
    out_specs = (tok, tok, vec, mat, mat, mat, mat, vec, mat, mat, mat)
    return jax.shard_map(shards, mesh=mesh, in_specs=in_specs, out_specs=out_specs, check_vma=False)
```

```python
import functools

import jax
import jax.numpy as jnp
from jax import lax
from jax.experimental import pallas as pl
from jax.experimental.pallas import tpu as pltpu
from jax.sharding import PartitionSpec as P

H = 32
KV = 4
HEAD = 64

epsilon = 1e-05
masked = -1e30
f32 = jnp.float32
bf16 = jnp.bfloat16


def rope_tables(length):
    half_width = HEAD // 2
    frequency = 10000.0 ** (-(jnp.arange(half_width, dtype=f32) * 2.0) / HEAD)
    angles = jnp.arange(length, dtype=f32)[:, None] * frequency[None, :]
    return (jnp.cos(angles)[:, None, :], jnp.sin(angles)[:, None, :])


def rotate(values, cosine, sine):
    front, back = values[..., : HEAD // 2], values[..., HEAD // 2 :]
    return jnp.concatenate([front * cosine - back * sine, back * cosine + front * sine], axis=-1)


def rms_scale(values):
    return lax.rsqrt(jnp.mean(values * values, axis=-1, keepdims=True) + epsilon)


def mm(a, b):
    return lax.dot_general(a, b, (((1,), (0,)), ((), ())), preferred_element_type=f32)


def mm_nt(a, b):
    return lax.dot_general(a, b, (((1,), (1,)), ((), ())), preferred_element_type=f32)


def mm_tn(a, b):
    return lax.dot_general(a, b, (((0,), (0,)), ((), ())), preferred_element_type=f32)


def seq_place():
    me = lax.axis_index("seq")
    return me // 2, me % 2

def hello(barrier, peer, axis):
    pl.semaphore_signal(
        barrier, inc=1, device_id={axis: peer}, device_id_type=pl.DeviceIdType.MESH
    )


def greet(z, y, Z, dp=None):
    barrier = pltpu.get_barrier_semaphore()
    hello(barrier, z * 2 + 1 - y, "seq")

    @pl.when(z > 0)
    def _():
        hello(barrier, z * 2 + y - 2, "seq")

    @pl.when(z < Z - 1)
    def _():
        hello(barrier, z * 2 + y + 2, "seq")

    count = 1 + (z + Z - 1) // Z + (2 * Z - 2 - z) // Z
    if dp is not None:
        hello(barrier, dp + 1 - 2 * (dp % 2), "dp")
        hello(barrier, dp + 2 - 4 * (dp // 2), "dp")
        count = count + 2
    pl.semaphore_wait(barrier, count)


def send(src, dst, ssem, rsem, peer, axis="seq"):
    return pltpu.make_async_remote_copy(
        src_ref=src,
        dst_ref=dst,
        send_sem=ssem,
        recv_sem=rsem,
        device_id={axis: peer},
        device_id_type=pl.DeviceIdType.MESH,
    )


def gather_kernel(Z, T, x_ref, out_ref, up_sem, dn_sem, y_sem, recv_sem, own_sem):
    z, y = seq_place()
    greet(z, y, Z)
    def block(zz, yy):
        return out_ref.at[pl.ds(pl.multiple_of((zz * 2 + yy) * T, T), T)]
    def copy(src, zz, sem, peer):
        return send(src, block(zz, y), sem.at[zz], recv_sem.at[zz * 2 + y], peer)
    own = pltpu.make_async_copy(x_ref, block(z, y), own_sem)
    own.start()
    peer_y, peer_up, peer_dn = z * 2 + 1 - y, z * 2 + y + 2, z * 2 + y - 2
    copy(x_ref, z, y_sem, peer_y).start()
    @pl.when(z < Z - 1)
    def _(): copy(x_ref, z, up_sem, peer_up).start()
    @pl.when(z > 0)
    def _(): copy(x_ref, z, dn_sem, peer_dn).start()
    for h in range(1, Z):
        @pl.when(z >= h)
        def _():
            zz = z - h
            copy(block(zz, y), zz, y_sem, peer_y).wait_recv()
            @pl.when(z < Z - 1)
            def _(): copy(block(zz, y), zz, up_sem, peer_up).start()
            copy(block(zz, y), zz, y_sem, peer_y).start()
        @pl.when(z + h < Z)
        def _():
            zz = z + h
            copy(block(zz, y), zz, y_sem, peer_y).wait_recv()
            @pl.when(z > 0)
            def _(): copy(block(zz, y), zz, dn_sem, peer_dn).start()
            copy(block(zz, y), zz, y_sem, peer_y).start()
    own.wait()
    for zz in range(Z):
        b = block(zz, 1 - y)
        send(b, b, y_sem.at[zz], recv_sem.at[zz * 2 + 1 - y], peer_y).wait_recv()
        c = copy(block(zz, y), zz, y_sem, peer_y)
        c.wait_send()
        @pl.when((zz <= z) & (z < Z - 1))
        def _(): copy(block(zz, y), zz, up_sem, peer_up).wait_send()
        @pl.when((zz >= z) & (z > 0))
        def _(): copy(block(zz, y), zz, dn_sem, peer_dn).wait_send()

def gather_line(x, cid=1):
    S = lax.axis_size("seq"); Z = S // 2
    T, D = x.shape
    return pl.pallas_call(
        functools.partial(gather_kernel, Z, T),
        out_shape=jax.ShapeDtypeStruct((S * T, D), x.dtype),
        in_specs=[pl.BlockSpec(memory_space=pltpu.VMEM)],
        out_specs=pl.BlockSpec(memory_space=pl.ANY),
        scratch_shapes=[pltpu.SemaphoreType.DMA((Z,))] * 3 + [pltpu.SemaphoreType.DMA((S,)), pltpu.SemaphoreType.DMA],
        compiler_params=pltpu.CompilerParams(collective_id=cid, has_side_effects=True),
        name="gather_seq",
    )(x)

def scatter_kernel(Z, T, p_ref, out_ref, ybuf, upbuf, dnbuf, upst, dnst, up_s, dn_s, y_s, up_r, dn_r, y_r):
    z, y = seq_place()
    greet(z, y, Z)
    peer_y, peer_up, peer_dn = z * 2 + 1 - y, z * 2 + y + 2, z * 2 + y - 2
    def mine(zz, yy):
        return p_ref.at[pl.ds(pl.multiple_of((zz * 2 + yy) * T, T), T)]
    def y_copy(zz):
        return send(mine(zz, 1 - y), ybuf.at[zz], y_s.at[zz], y_r.at[zz], peer_y)
    def up_copy(zz):
        return send(upst.at[zz], upbuf.at[zz], up_s.at[zz], up_r.at[zz], peer_up)
    def dn_copy(zz):
        return send(dnst.at[zz], dnbuf.at[zz], dn_s.at[zz], dn_r.at[zz], peer_dn)
    for h in range(Z - 1, 0, -1):
        @pl.when(z + h < Z)
        def _(): y_copy(z + h).start()
        @pl.when(z - h >= 0)
        def _(): y_copy(z - h).start()
    y_copy(z).start()
    for h in range(Z - 1, 0, -1):
        @pl.when(z + h < Z)
        def _():
            d = z + h
            y_copy(d).wait_recv()
            upst[d] = (mine(d, y)[...].astype(f32) + ybuf[d].astype(f32)).astype(bf16)
            @pl.when(z > 0)
            def _():
                up_copy(d).wait_recv()
                upst[d] = (mine(d, y)[...].astype(f32) + ybuf[d].astype(f32) + upbuf[d].astype(f32)).astype(bf16)
            up_copy(d).start()
        @pl.when(z - h >= 0)
        def _():
            d = z - h
            y_copy(d).wait_recv()
            dnst[d] = (mine(d, y)[...].astype(f32) + ybuf[d].astype(f32)).astype(bf16)
            @pl.when(z < Z - 1)
            def _():
                dn_copy(d).wait_recv()
                dnst[d] = (mine(d, y)[...].astype(f32) + ybuf[d].astype(f32) + dnbuf[d].astype(f32)).astype(bf16)
            dn_copy(d).start()
    y_copy(z).wait_recv()
    out_ref[...] = mine(z, y)[...].astype(f32) + ybuf[z].astype(f32)
    @pl.when(z > 0)
    def _():
        up_copy(z).wait_recv()
        out_ref[...] += upbuf[z].astype(f32)
    @pl.when(z < Z - 1)
    def _():
        dn_copy(z).wait_recv()
        out_ref[...] += dnbuf[z].astype(f32)
    for zz in range(Z):
        y_copy(zz).wait_send()
        @pl.when(zz > z)
        def _(): up_copy(zz).wait_send()
        @pl.when(zz < z)
        def _(): dn_copy(zz).wait_send()

def scatter_line(p, cid=2):
    S = lax.axis_size("seq"); Z = S // 2
    L, D = p.shape; T = L // S
    return pl.pallas_call(
        functools.partial(scatter_kernel, Z, T),
        out_shape=jax.ShapeDtypeStruct((T, D), f32),
        in_specs=[pl.BlockSpec(memory_space=pltpu.VMEM)],
        out_specs=pl.BlockSpec(memory_space=pltpu.VMEM),
        scratch_shapes=[pltpu.VMEM((Z, T, D), bf16)] * 5 + [pltpu.SemaphoreType.DMA((Z,))] * 6,
        compiler_params=pltpu.CompilerParams(collective_id=cid, has_side_effects=True, vmem_limit_bytes=60 << 20),
        name="scatter_seq",
    )(p)


def line_rank(i, z):
    upper = z // 2
    inner = (z + upper) % 2
    base = i + inner * (1 - i // 2) * (1 - 2 * i)
    return base + upper * (3 - 2 * base)


def above(d, z):
    return (d - z + 3) // 4


def rows_of(ref, start, size):
    return ref.at[pl.ds(pl.multiple_of(start, size), size)]


def in_chunks(rows, chunk, step):
    def body(i, carry):
        step(pl.ds(pl.multiple_of(i * chunk, chunk), chunk))
        return carry

    lax.fori_loop(0, rows // chunk, body, 0)


class Gather:
    def __init__(self, z, y, T, own, full, up_sem, dn_sem, y_sem, recv_sem, own_sem):
        self.z, self.y, self.T, self.own, self.full = z, y, T, own, full
        self.sems = {"up": up_sem, "dn": dn_sem, "y": y_sem}
        self.peers = {"up": z * 2 + y + 2, "dn": z * 2 + y - 2, "y": z * 2 + 1 - y}
        self.recv_sem, self.own_sem = recv_sem, own_sem

    def block(self, zz, yy):
        return rows_of(self.full, (zz * 2 + yy) * self.T, self.T)

    def copy(self, src, zz, way):
        return send(
            src,
            self.block(zz, self.y),
            self.sems[way].at[zz],
            self.recv_sem.at[zz * 2 + self.y],
            self.peers[way],
        )

    def start(self):
        z = self.z
        pltpu.make_async_copy(self.own, self.block(z, self.y), self.own_sem).start()
        self.copy(self.own, z, "y").start()

        @pl.when(z < 3)
        def _():
            self.copy(self.own, z, "up").start()

        @pl.when(z > 0)
        def _():
            self.copy(self.own, z, "dn").start()

    def own_ready(self):
        pltpu.make_async_copy(self.own, self.block(self.z, self.y), self.own_sem).wait()

    def hop(self, h):
        z = self.z

        @pl.when(z >= h)
        def _():
            src = self.block(z - h, self.y)
            self.copy(src, z - h, "y").wait_recv()

            @pl.when(z < 3)
            def _():
                self.copy(src, z - h, "up").start()

            self.copy(src, z - h, "y").start()

        @pl.when(z + h < 4)
        def _():
            src = self.block(z + h, self.y)
            self.copy(src, z + h, "y").wait_recv()

            @pl.when(z > 0)
            def _():
                self.copy(src, z + h, "dn").start()

            self.copy(src, z + h, "y").start()

    def pair_ready(self, zz):
        b = self.block(zz, 1 - self.y)
        send(
            b, b, self.sems["y"].at[zz], self.recv_sem.at[zz * 2 + 1 - self.y], self.peers["y"]
        ).wait_recv()

    def finish(self):
        z = self.z
        for zz in range(4):
            src = self.block(zz, self.y)
            self.copy(src, zz, "y").wait_send()

            @pl.when((zz <= z) & (z < 3))
            def _():
                self.copy(src, zz, "up").wait_send()

            @pl.when((zz >= z) & (z > 0))
            def _():
                self.copy(src, zz, "dn").wait_send()


class Scatter:
    def __init__(self, z, y, T, part, ybuf, rbuf, y_s, y_r, z_s, z_r):
        self.z, self.y, self.T, self.part = z, y, T, part
        self.ybuf, self.rbuf = ybuf, rbuf
        self.y_s, self.y_r, self.z_s, self.z_r = y_s, y_r, z_s, z_r

    def rows(self, zz, yy):
        return rows_of(self.part, (zz * 2 + yy) * self.T, self.T)

    def y_copy(self, d):
        peer = self.z * 2 + 1 - self.y
        return send(
            self.rows(d, 1 - self.y), self.ybuf.at[d], self.y_s.at[d], self.y_r.at[d], peer
        )

    def z_copy(self, d, up):
        slot = d + up
        peer = self.z * 2 + self.y + 4 * up - 2
        return send(self.ybuf.at[d], self.rbuf.at[slot], self.z_s.at[d], self.z_r.at[slot], peer)

    def start(self, d):
        self.y_copy(d).start()

    def pass_on(self, d):
        z = self.z
        up = above(d, z)
        self.y_copy(d).wait_recv()
        mine, slot = self.rows(d, self.y), self.ybuf.at[d]
        inner = (z > 0) & (z < 3)

        @pl.when(inner)
        def _():
            self.z_copy(d, up).wait_recv()
            far = self.rbuf.at[d + up]

            def step(c):
                slot[c] = (
                    mine[c].astype(f32) + slot[c].astype(f32) + far[c].astype(f32)
                ).astype(bf16)

            in_chunks(self.T, 32, step)

        @pl.when(jnp.logical_not(inner))
        def _():
            def step(c):
                slot[c] = (mine[c].astype(f32) + slot[c].astype(f32)).astype(bf16)

            in_chunks(self.T, 32, step)

        self.z_copy(d, up).start()

    def finish(self, out_ref):
        z = self.z
        self.y_copy(z).wait_recv()
        mine, slot = self.rows(z, self.y), self.ybuf.at[z]

        def first(c):
            out_ref[c] = mine[c].astype(f32) + slot[c].astype(f32)

        in_chunks(self.T, 32, first)

        def more(slot):
            def step(c):
                out_ref[c] += slot[c].astype(f32)

            in_chunks(self.T, 32, step)

        @pl.when(z > 0)
        def _():
            self.z_copy(z, 1).wait_recv()
            more(self.rbuf.at[z + 1])

        @pl.when(z < 3)
        def _():
            self.z_copy(z, 0).wait_recv()
            more(self.rbuf.at[z])

        for d in range(4):
            self.y_copy(d).wait_send()

            @pl.when(z != d)
            def _():
                self.z_copy(d, above(d, z)).wait_send()


def line_sems(n):
    return [pltpu.SemaphoreType.DMA((4,))] * 3 + [
        pltpu.SemaphoreType.DMA((8,)),
        pltpu.SemaphoreType.DMA,
    ]


def sum_scratch(T, width):
    return [
        pltpu.VMEM((4, T, width), bf16),
        pltpu.VMEM((5, T, width), bf16),
        pltpu.SemaphoreType.DMA((4,)),
        pltpu.SemaphoreType.DMA((4,)),
        pltpu.SemaphoreType.DMA((4,)),
        pltpu.SemaphoreType.DMA((5,)),
    ]


class DpSum:
    def __init__(self, src, size, abuf, bbuf, a_s, a_r, b_s, b_r):
        dp = lax.axis_index("dp")
        self.core, self.far = dp % 2, dp // 2
        self.partner, self.across = dp + 1 - 2 * (dp % 2), dp + 2 - 4 * (dp // 2)
        self.src, self.size = src, size
        self.abuf, self.bbuf = abuf, bbuf
        self.a_s, self.a_r, self.b_s, self.b_r = a_s, a_r, b_s, b_r

    def rows(self, d):
        return rows_of(self.src, d * self.size, self.size)

    def a_copy(self, j):
        return send(
            self.rows(2 * j + 1 - self.core),
            self.abuf.at[j],
            self.a_s.at[j],
            self.a_r.at[j],
            self.partner,
            "dp",
        )

    def b_copy(self):
        return send(self.abuf.at[1 - self.far], self.bbuf, self.b_s, self.b_r, self.across, "dp")

    def start(self):
        self.a_copy(0).start()
        self.a_copy(1).start()

    def middle(self):
        self.a_copy(0).wait_recv()
        self.a_copy(1).wait_recv()
        j = 1 - self.far
        mine, slot = self.rows(2 * j + self.core), self.abuf.at[j]

        def step(c):
            slot[c] = (mine[c].astype(f32) + slot[c].astype(f32)).astype(bf16)

        in_chunks(self.size, 16, step)
        self.b_copy().start()

    def finish(self, out_ref):
        self.b_copy().wait_recv()
        mine, slot = self.rows(2 * self.far + self.core), self.abuf.at[self.far]

        def step(c):
            out_ref[c] = (
                mine[c].astype(f32) + slot[c].astype(f32) + self.bbuf[c].astype(f32)
            ).astype(out_ref.dtype)

        in_chunks(self.size, 16, step)
        self.a_copy(0).wait_send()
        self.a_copy(1).wait_send()
        self.b_copy().wait_send()


def dp_scratch(size, width):
    return [
        pltpu.VMEM((2, size, width), bf16),
        pltpu.VMEM((size, width), bf16),
        pltpu.SemaphoreType.DMA((2,)),
        pltpu.SemaphoreType.DMA((2,)),
        pltpu.SemaphoreType.DMA,
        pltpu.SemaphoreType.DMA,
    ]


def feedforward_kernel(
    T, x_ref, dy_ref, wgu_ref, wd_ref, pout_ref, e2_ref, ggu_ref, gd_ref,
    full, hid, dgu, part, ggu, gdown, up_sem, dn_sem, ag_y, ag_r, own_sem,
    ybuf, rbuf, y_s, y_r, z_s, z_r,
    ga, gb, ga_s, ga_r, gb_s, gb_r,
    da, db, da_s, da_r, db_s, db_r,
):
    z, y = seq_place()
    dp = lax.axis_index("dp")
    F = hid.shape[1]
    greet(z, y, 4, dp)
    gather = Gather(z, y, T, x_ref, full, up_sem, dn_sem, ag_y, ag_r, own_sem)
    scatter = Scatter(z, y, T, part, ybuf, rbuf, y_s, y_r, z_s, z_r)
    sum_gu = DpSum(ggu, ggu.shape[0] // 4, ga, gb, ga_s, ga_r, gb_s, gb_r)
    sum_down = DpSum(gdown, gd_ref.shape[0], da, db, da_s, da_r, db_s, db_r)
    gather.start()
    gather.own_ready()

    def compute(i, carry):
        for h in range(1, 4):

            @pl.when(i == h - 1)
            def _():
                gather.hop(h)

        zz = line_rank(i, z)
        gather.pair_ready(zz)

        @pl.when(i == 3)
        def _():
            scatter.start(line_rank(2, z))

        r = pl.ds(pl.multiple_of(zz * 2 * T, 2 * T), 2 * T)
        gu = mm(full[r, :], wgu_ref[...])
        gate, up = gu[:, :F], gu[:, F:]
        sig = 1.0 / (1.0 + jnp.exp(-gate))
        act = gate * sig
        h = (act * up).astype(bf16)
        hid[r, :] = h
        pout_ref[r, :] = mm(h, wd_ref[...]).astype(bf16)
        dh = mm_nt(dy_ref[r, :], wd_ref[...])
        dgu[r, :F] = (dh * up * sig * (1.0 + gate * (1.0 - sig))).astype(bf16)
        dgu[r, F:] = (dh * act).astype(bf16)
        part[r, :] = mm_nt(dgu[r, :], wgu_ref[...]).astype(bf16)
        return carry

    lax.fori_loop(0, 4, compute, 0)
    for i in (3, 1, 0):
        scatter.start(line_rank(i, z))

    def gate_up_tile(i, carry):
        r = pl.ds(pl.multiple_of(i * 256, 256), 256)
        ggu[r, :] = mm_tn(full[:, r], dgu[...]).astype(bf16)
        return carry

    def down_tile(i, carry):
        r = pl.ds(pl.multiple_of(i * 256, 256), 256)
        gdown[r, :] = mm_tn(hid[:, r], dy_ref[...]).astype(bf16)
        return carry

    lax.fori_loop(0, 8, gate_up_tile, 0)
    sum_gu.start()
    scatter.pass_on(line_rank(3, z))
    lax.fori_loop(0, F // 256, down_tile, 0)
    sum_down.start()
    sum_gu.middle()
    scatter.pass_on(line_rank(2, z))
    sum_down.middle()
    scatter.pass_on(line_rank(1, z))
    sum_gu.finish(ggu_ref)
    sum_down.finish(gd_ref)
    scatter.finish(e2_ref)
    gather.finish()


def feedforward(x, dy_all, w_gu, w_d, down_rows, cid=3):
    T, width = x.shape
    L, F = dy_all.shape[0], w_d.shape[0]
    vmem = pl.BlockSpec(memory_space=pltpu.VMEM)
    return pl.pallas_call(
        functools.partial(feedforward_kernel, T),
        out_shape=(
            jax.ShapeDtypeStruct((L, width), bf16),
            jax.ShapeDtypeStruct((T, width), f32),
            jax.ShapeDtypeStruct((width // 4, 2 * F), bf16),
            jax.ShapeDtypeStruct((down_rows, width), f32),
        ),
        in_specs=[vmem] * 4,
        out_specs=(vmem,) * 4,
        scratch_shapes=[
            pltpu.VMEM((L, width), bf16),
            pltpu.VMEM((L, F), bf16),
            pltpu.VMEM((L, 2 * F), bf16),
            pltpu.VMEM((L, width), bf16),
            pltpu.VMEM((width, 2 * F), bf16),
            pltpu.VMEM((F, width), bf16),
        ]
        + line_sems(4)
        + sum_scratch(T, width)
        + dp_scratch(width // 4, 2 * F)
        + dp_scratch(down_rows, width),
        compiler_params=pltpu.CompilerParams(
            collective_id=cid, has_side_effects=True, vmem_limit_bytes=67000000
        ),
        name="feedforward",
    )(x, dy_all, w_gu, w_d)


def attention_back_kernel(
    T, heads, dm_ref, q_ref, k_ref, kz_ref, vz_ref, lse_ref, att_ref, s1_ref, wqkv_ref, wo_ref, table_ref,
    e1_ref, got_ref, go_ref,
    full, grads, probs, dprobs, dk, dv, dqkv, part, gqkv, go_part, gsum,
    up_sem, dn_sem, ag_y, ag_r, own_sem,
    ybuf, rbuf, y_s, y_r, z_s, z_r,
    qa, qb, qa_s, qa_r, qb_s, qb_r,
    oa, ob, oa_s, oa_r, ob_s, ob_r,
    ex_s, ex_r, ex_own,
):
    z, y = seq_place()
    me = z * 2 + y
    dp = lax.axis_index("dp")
    rows = got_ref.shape[1]
    barrier = pltpu.get_barrier_semaphore()
    for step in range(1, 8):
        hello(barrier, (me + step) % 8, "seq")
    hello(barrier, dp + 1 - 2 * (dp % 2), "dp")
    hello(barrier, dp + 2 - 4 * (dp // 2), "dp")
    pl.semaphore_wait(barrier, 9)
    gather = Gather(z, y, T, dm_ref, full, up_sem, dn_sem, ag_y, ag_r, own_sem)
    scatter = Scatter(z, y, T, part, ybuf, rbuf, y_s, y_r, z_s, z_r)
    sum_qkv = DpSum(gqkv, gqkv.shape[0] // 4, qa, qb, qa_s, qa_r, qb_s, qb_r)
    sum_o = DpSum(go_part, go_part.shape[0] // 4, oa, ob, oa_s, oa_r, ob_s, ob_r)
    gather.start()
    dk[...] = jnp.zeros_like(dk)
    dv[...] = jnp.zeros_like(dv)
    gather.own_ready()
    U = 2 * T
    low_lanes = lax.broadcasted_iota(jnp.int32, (U, 128), 1) < HEAD
    scale = HEAD ** (-0.5)

    def both(product, table):
        turned = product * table
        return turned + pltpu.roll(turned, HEAD, 1)

    def unit(i, carry):
        for h in range(1, 4):

            @pl.when(i == h - 1)
            def _():
                gather.hop(h)

        u = line_rank(i, z)
        gather.pair_ready(u)
        r = pl.ds(pl.multiple_of(u * U, U), U)
        d_att = mm_nt(full[r, :], wo_ref[...]).astype(bf16)
        for h in range(heads):
            grads[h] = d_att[:, h * 128 : (h + 1) * 128]
        g = grads[...].reshape(heads * U, 128)
        q = q_ref[:, r, :].reshape(heads * U, 128)
        lse = lse_ref[:, r, :].reshape(heads * U, 1)

        def scores(j, inner):
            c = pl.ds(pl.multiple_of(j * U, U), U)
            s = mm_nt(q, kz_ref[c, :]) * scale
            row = lax.broadcasted_iota(jnp.int32, (heads, U, U), 1).reshape(heads * U, U)
            col = lax.broadcasted_iota(jnp.int32, (heads * U, U), 1)
            s = jnp.where(col + (j - u) * U <= row, s, masked)
            p = jnp.exp(s - lse)
            dp_ = mm_nt(g, vz_ref[c, :])
            probs[j] = p
            dprobs[j] = dp_
            return inner + jnp.sum(p * dp_, axis=1, keepdims=True)

        inner = lax.fori_loop(0, u + 1, scores, jnp.zeros((heads * U, 1), f32))

        def products(j, dq):
            c = pl.ds(pl.multiple_of(j * U, U), U)
            p = probs[j]
            ds = (p * (dprobs[j] - inner)).astype(bf16)
            dk[c, :] += mm_tn(ds, q)
            dv[c, :] += mm_tn(p.astype(bf16), g)
            return dq + mm(ds, k_ref[c, :])

        dq = lax.fori_loop(0, u + 1, products, jnp.zeros((heads * U, 128), f32))
        table = table_ref[r, :]
        for h in range(0, heads, 2):
            first = both(dq[h * U : (h + 1) * U], table)
            second = both(dq[(h + 1) * U : (h + 2) * U], table)
            dqkv[r, h * HEAD : (h + 2) * HEAD] = jnp.where(low_lanes, first, second).astype(bf16)
        return carry

    lax.fori_loop(0, 4, unit, 0)

    def part_rows(i):
        u = line_rank(i, z)
        r = pl.ds(pl.multiple_of(u * U, U), U)
        d_key = both(dk[r, :], table_ref[r, :])
        dqkv[r, heads * HEAD :] = jnp.where(low_lanes, d_key, pltpu.roll(dv[r, :], HEAD, 1)).astype(bf16)
        part[r, :] = mm_nt(dqkv[r, :], wqkv_ref[...]).astype(bf16)
        scatter.start(u)

    def part_loop(i, carry):
        part_rows(3 - i)
        return carry

    lax.fori_loop(0, 4, part_loop, 0)

    def qkv_tile(i, carry):
        r = pl.ds(pl.multiple_of(i * 256, 256), 256)
        gqkv[r, :] = mm_tn(s1_ref[:, r], dqkv[...]).astype(bf16)
        return carry

    lax.fori_loop(0, gqkv.shape[0] // 256, qkv_tile, 0)
    sum_qkv.start()
    scatter.pass_on(line_rank(3, z))
    sum_qkv.middle()
    go_part[...] = mm_tn(att_ref[...], full[...]).astype(bf16)
    sum_o.start()
    scatter.pass_on(line_rank(2, z))
    sum_qkv.finish(gsum)

    def piece(peer):
        return rows_of(gsum, peer * rows, rows)

    def exchange(peer):
        return send(piece(peer), got_ref.at[me], ex_s.at[peer], ex_r.at[me], peer)

    own = pltpu.make_async_copy(piece(me), got_ref.at[me], ex_own)
    own.start()
    for step in range(1, 8):
        exchange((me + step) % 8).start()
    sum_o.middle()
    scatter.pass_on(line_rank(1, z))
    sum_o.finish(go_ref)
    scatter.finish(e1_ref)
    own.wait()
    for step in range(1, 8):
        peer = (me + step) % 8
        send(piece(me), got_ref.at[peer], ex_s.at[peer], ex_r.at[peer], peer).wait_recv()
        exchange(peer).wait_send()
    gather.finish()


def attention_back(dm, q2, k2, kz, vz, lse, attended, s1_all, w_qkv, w_o2, table, rows, cid=4):
    T, width = dm.shape
    heads, L, _ = q2.shape
    cols = w_qkv.shape[1]
    vmem = pl.BlockSpec(memory_space=pltpu.VMEM)
    U = 2 * T
    return pl.pallas_call(
        functools.partial(attention_back_kernel, T, heads),
        out_shape=(
            jax.ShapeDtypeStruct((T, width), f32),
            jax.ShapeDtypeStruct((8, rows, cols), bf16),
            jax.ShapeDtypeStruct((rows, width), f32),
        ),
        in_specs=[vmem] * 11,
        out_specs=(vmem,) * 3,
        scratch_shapes=[
            pltpu.VMEM((L, width), bf16),
            pltpu.VMEM((heads, U, 128), bf16),
            pltpu.VMEM((L // U, heads * U, U), f32),
            pltpu.VMEM((L // U, heads * U, U), f32),
            pltpu.VMEM((L, 128), f32),
            pltpu.VMEM((L, 128), f32),
            pltpu.VMEM((L, cols), bf16),
            pltpu.VMEM((L, width), bf16),
            pltpu.VMEM((width, cols), bf16),
            pltpu.VMEM((heads * HEAD, width), bf16),
            pltpu.VMEM((width // 4, cols), bf16),
        ]
        + line_sems(4)
        + sum_scratch(T, width)
        + dp_scratch(width // 4, cols)
        + dp_scratch(rows, width)
        + [pltpu.SemaphoreType.DMA((8,)), pltpu.SemaphoreType.DMA((8,)), pltpu.SemaphoreType.DMA],
        compiler_params=pltpu.CompilerParams(
            collective_id=cid, has_side_effects=True, vmem_limit_bytes=67000000
        ),
        name="attention_back",
    )(dm, q2, k2, kz, vz, lse, attended, s1_all, w_qkv, w_o2, table)


def spread_kernel(
    down_rows, repeats, gu_ref, qkv_ref, wg_ref, wu_ref, wq_ref, wk_ref, wv_ref, one_ref, two_ref,
    gate_ref, up_ref, query_ref, key_ref, value_ref, gain1_ref, gain2_ref,
):
    S, rows, wide = gu_ref.shape
    F = wide // 2
    Dp = gate_ref.shape[1] // (S * down_rows)
    q_cols = query_ref.shape[1] // S
    for s in range(S):
        for d in range(Dp):
            to = pl.ds((d * S + s) * down_rows, down_rows)
            gate_ref[:, to] = gu_ref[s, :, d * down_rows : (d + 1) * down_rows].astype(f32)
            up_ref[:, to] = gu_ref[s, :, F + d * down_rows : F + (d + 1) * down_rows].astype(f32)
        query_ref[:, s * q_cols : (s + 1) * q_cols] = qkv_ref[s, :, :q_cols].astype(f32)
    for j in range(S // repeats):
        total = qkv_ref[j * repeats, :, q_cols:].astype(f32)
        for s in range(j * repeats + 1, (j + 1) * repeats):
            total = total + qkv_ref[s, :, q_cols:].astype(f32)
        key_ref[:, j * HEAD : (j + 1) * HEAD] = total[:, :HEAD]
        value_ref[:, j * HEAD : (j + 1) * HEAD] = total[:, HEAD:]

    def close(pairs, gain_ref, out_ref):
        total = jnp.zeros((rows, 1), f32)
        for weight_ref, grad_ref in pairs:
            grad = grad_ref[...]
            total = total + jnp.sum(weight_ref[...].astype(f32) * grad, axis=1, keepdims=True)
            grad_ref[...] = grad * gain_ref[...]
        out_ref[...] = total

    close(((wg_ref, gate_ref), (wu_ref, up_ref)), two_ref, gain2_ref)
    close(((wq_ref, query_ref), (wk_ref, key_ref), (wv_ref, value_ref)), one_ref, gain1_ref)


def spread(gu, qkv, weights, gains, down_rows, repeats):
    rows = gu.shape[1]
    outs = [jax.ShapeDtypeStruct(w.shape, f32) for w in weights]
    outs += [jax.ShapeDtypeStruct((rows, 1), f32)] * 2
    vmem = pl.BlockSpec(memory_space=pltpu.VMEM)
    return pl.pallas_call(
        functools.partial(spread_kernel, down_rows, repeats),
        out_shape=tuple(outs),
        in_specs=[vmem] * 9,
        out_specs=(vmem,) * 7,
        compiler_params=pltpu.CompilerParams(vmem_limit_bytes=40 << 20),
        name="spread",
    )(gu, qkv, *weights, *gains)


def gather_seq(rows):
    if lax.axis_size("seq") == 8:
        return gather_line(rows)
    return lax.all_gather(rows, "seq", axis=0, tiled=True)


def scatter_seq(rows):
    if lax.axis_size("seq") == 8:
        return scatter_line(rows)
    return lax.psum_scatter(rows, "seq", scatter_dimension=0, tiled=True).astype(f32)


def feedforward_plain(x, dy_all, w_gu, w_d):
    hidden = w_d.shape[0]
    s2_all = gather_seq(x)
    gate_up = mm(s2_all, w_gu)
    gate, up = gate_up[:, :hidden], gate_up[:, hidden:]
    sig = jax.nn.sigmoid(gate)
    hid = (gate * sig * up).astype(bf16)
    d_hid = mm_nt(dy_all, w_d)
    d_gate = (d_hid * up * sig * (1.0 + gate * (1.0 - sig))).astype(bf16)
    d_up = (d_hid * (gate * sig)).astype(bf16)
    d_gu = jnp.concatenate([d_gate, d_up], axis=1)
    return (
        mm(hid, w_d).astype(bf16),
        scatter_seq(mm_nt(d_gu, w_gu).astype(bf16)),
        scatter_dp(mm_tn(s2_all, d_gu).astype(bf16)),
        scatter_dp(mm_tn(hid, dy_all).astype(bf16)).astype(f32),
    )


def gather_dp(rows):
    return lax.all_gather(rows, "dp", axis=0, tiled=True)


def scatter_dp(rows):
    return lax.psum_scatter(rows, "dp", scatter_dimension=0, tiled=True)


def exchange_seq(pieces):
    return lax.all_to_all(pieces, "seq", split_axis=0, concat_axis=0, tiled=True)


def causal_mask(offset, block_rows, block_end):
    return jnp.arange(block_end)[None, :] <= (offset + jnp.arange(block_rows))[:, None]


def attention_forward(queries, keys, values, block_rows):
    outputs, totals = [], []
    for offset in range(0, queries.shape[1], block_rows):
        end = offset + block_rows
        scores = jnp.einsum(
            "hqd,kd->hqk", queries[:, offset:end], keys[:end], preferred_element_type=f32
        ) * HEAD ** (-0.5)
        scores = jnp.where(causal_mask(offset, block_rows, end), scores, masked)
        row_max = jnp.max(scores, axis=-1, keepdims=True)
        total = row_max + jnp.log(jnp.sum(jnp.exp(scores - row_max), axis=-1, keepdims=True))
        probs_low = jnp.exp(scores - total).astype(bf16)
        outputs.append(
            jnp.einsum("hqk,kd->hqd", probs_low, values[:end], preferred_element_type=f32).astype(
                bf16
            )
        )
        totals.append(total)
    return jnp.concatenate(outputs, axis=1), jnp.concatenate(totals, axis=1)


def attention_backward(queries, keys, values, grads, totals, block_rows):
    length = keys.shape[0]
    scale = HEAD ** (-0.5)
    key_sum = jnp.zeros((length, HEAD), f32)
    value_sum = jnp.zeros((length, HEAD), f32)
    query_parts = []
    for offset in range(0, length, block_rows):
        end = offset + block_rows
        query_block, grad_block = queries[:, offset:end], grads[:, offset:end]
        key_block, value_block = keys[:end], values[:end]
        scores = (
            jnp.einsum("hqd,kd->hqk", query_block, key_block, preferred_element_type=f32) * scale
        )
        scores = jnp.where(causal_mask(offset, block_rows, end), scores, masked)
        probs = jnp.exp(scores - totals[:, offset:end])
        probs_low = probs.astype(bf16)
        grad_probs = jnp.einsum(
            "hqd,kd->hqk", grad_block, value_block, preferred_element_type=f32
        )
        inner = jnp.sum(probs * grad_probs, axis=-1, keepdims=True)
        grad_scores = (probs * (grad_probs - inner)).astype(bf16)
        query_parts.append(
            jnp.einsum("hqk,kd->hqd", grad_scores, key_block, preferred_element_type=f32) * scale
        )
        padding = ((0, length - end), (0, 0))
        key_sum = key_sum + jnp.pad(
            jnp.einsum("hqk,hqd->kd", grad_scores, query_block, preferred_element_type=f32)
            * scale,
            padding,
        )
        value_sum = value_sum + jnp.pad(
            jnp.einsum("hqk,hqd->kd", probs_low, grad_block, preferred_element_type=f32), padding
        )
    return jnp.concatenate(query_parts, axis=1), key_sum, value_sum


def heads_first(flat, heads):
    return jnp.transpose(flat.reshape(flat.shape[0], heads, HEAD), (1, 0, 2))


def heads_last(stacked):
    return jnp.transpose(stacked, (1, 0, 2)).reshape(stacked.shape[1], -1)


def shards(
    inputs,
    attention_gain,
    query_weight,
    key_weight,
    value_weight,
    output_weight,
    feedforward_gain,
    gate_weight,
    up_weight,
    down_weight,
    cotangent,
):
    S, Dp = lax.axis_size("seq"), lax.axis_size("dp")
    sequences, tokens, width = inputs.shape
    length = tokens * S
    rows = query_weight.shape[0]
    heads = H // S
    q_cols = heads * HEAD
    repeats = S // KV
    down_rows = down_weight.shape[0]
    hidden = down_rows * Dp
    block_rows = min(length, max(512, length // 8))

    gain_one = attention_gain.astype(f32)[:, None]
    gain_two = feedforward_gain.astype(f32)[:, None]

    def folded(weight, gain):
        return (weight.astype(f32) * gain).astype(bf16)

    def per_group_kv(weight):
        return jnp.repeat(weight.reshape(rows, KV, HEAD), repeats, axis=1)

    def per_group_hidden(weight):
        return jnp.transpose(weight.reshape(rows, Dp, S, down_rows), (2, 0, 1, 3)).reshape(
            S, rows, hidden
        )

    packed = jnp.concatenate(
        [
            folded(query_weight, gain_one).reshape(rows, S, q_cols),
            per_group_kv(folded(key_weight, gain_one)),
            per_group_kv(folded(value_weight, gain_one)),
        ],
        axis=2,
    )
    packed = jnp.transpose(packed, (1, 0, 2))
    w_qkv = gather_dp(exchange_seq(packed).reshape(S * rows, q_cols + 2 * HEAD))
    forward_perm = [(Dp * s + d, d * S + s) for s in range(S) for d in range(Dp)]
    backward_perm = [(b, a) for a, b in forward_perm]
    w_o = gather_dp(lax.ppermute(output_weight, ("dp", "seq"), forward_perm))
    packed = jnp.concatenate(
        [
            per_group_hidden(folded(gate_weight, gain_two)),
            per_group_hidden(folded(up_weight, gain_two)),
        ],
        axis=2,
    )
    line = S == 8 and Dp == 4
    width_f = -(-hidden // 256) * 256 if line else hidden

    def padded(part, axis):
        pads = [(0, 0)] * part.ndim
        pads[axis] = (0, width_f - hidden)
        return jnp.pad(part, pads)

    packed = exchange_seq(packed).reshape(S * rows, 2 * hidden)
    packed = jnp.concatenate(
        [padded(packed[:, :hidden], 1), padded(packed[:, hidden:], 1)], axis=1
    )
    w_gu = gather_dp(packed)
    w_d = padded(gather_dp(down_weight), 0)

    flat = inputs.reshape(tokens, width).astype(f32)
    r1 = rms_scale(flat)
    s1 = flat * r1
    s1_all = gather_seq(s1.astype(bf16))
    cosine, sine = rope_tables(length)
    qkv = mm(s1_all, w_qkv)
    queries = rotate(qkv[:, :q_cols].reshape(length, heads, HEAD), cosine, sine).astype(bf16)
    queries = jnp.transpose(queries, (1, 0, 2))
    keys = rotate(qkv[:, None, q_cols : q_cols + HEAD], cosine, sine).astype(bf16)[:, 0]
    values = qkv[:, q_cols + HEAD :].astype(bf16)
    attended, totals = attention_forward(queries, keys, values, block_rows)
    attended = heads_last(attended)
    middle = flat + scatter_seq(mm(attended, w_o).astype(bf16))
    r2 = rms_scale(middle)
    s2 = middle * r2
    dy = cotangent.reshape(tokens, width)
    dy_all = gather_seq(dy)
    if line:
        out_part, e2, g_gu, down_grad = feedforward(
            s2.astype(bf16), dy_all, w_gu, w_d, down_rows
        )
    else:
        out_part, e2, g_gu, down_grad = feedforward_plain(s2.astype(bf16), dy_all, w_gu, w_d)

    g_gu = exchange_seq(g_gu.reshape(S, rows, 2 * width_f))
    d_middle = dy.astype(f32) + r2 * (e2 - s2 * jnp.mean(e2 * s2, axis=-1, keepdims=True))
    if line:
        table = jnp.concatenate([cosine, cosine, sine, -sine], axis=-1)[:, 0] * HEAD ** (-0.5)
        half = HEAD // 2

        def with_swapped(u):
            return jnp.concatenate([u, u[..., half:], u[..., :half]], axis=-1)

        def with_zeros(u):
            return jnp.concatenate([u, jnp.zeros_like(u)], axis=-1)

        w_o2 = with_zeros(w_o.reshape(heads, 1, HEAD, width).swapaxes(2, 3)).swapaxes(2, 3)
        e1, g_qkv, g_o = attention_back(
            d_middle.astype(bf16),
            with_swapped(queries),
            with_swapped(keys),
            with_zeros(keys),
            with_zeros(values),
            totals,
            attended,
            s1_all,
            w_qkv,
            w_o2.reshape(2 * q_cols, width),
            table,
            rows,
        )
        g_o = g_o.astype(bf16)
    else:
        dm_all = gather_seq(d_middle.astype(bf16))
        d_att = heads_first(mm_nt(dm_all, w_o).astype(bf16), heads)
        d_q, d_k, d_v = attention_backward(queries, keys, values, d_att, totals, block_rows)
        d_q = jnp.transpose(d_q, (1, 0, 2))
        d_qkv = jnp.concatenate(
            [
                rotate(d_q, cosine, -sine).reshape(length, q_cols).astype(bf16),
                rotate(d_k[:, None], cosine, -sine)[:, 0].astype(bf16),
                d_v.astype(bf16),
            ],
            axis=1,
        )
        e1 = scatter_seq(mm_nt(d_qkv, w_qkv).astype(bf16))
        g_o = scatter_dp(mm_tn(attended, dm_all).astype(bf16))
        g_qkv = scatter_dp(mm_tn(s1_all, d_qkv).astype(bf16))
        g_qkv = exchange_seq(g_qkv.reshape(S, rows, q_cols + 2 * HEAD))
    output = (middle + scatter_seq(out_part)).astype(bf16)
    input_grad = d_middle + r1 * (e1 - s1 * jnp.mean(e1 * s1, axis=-1, keepdims=True))
    output_grad = lax.ppermute(g_o, ("dp", "seq"), backward_perm).astype(f32)

    if line:
        g_gate, g_up, g_query, g_key, g_value, gain_one_grad, gain_two_grad = spread(
            g_gu,
            g_qkv,
            (gate_weight, up_weight, query_weight, key_weight, value_weight),
            (gain_one, gain_two),
            down_rows,
            repeats,
        )
        return (
            output.reshape(sequences, tokens, width),
            input_grad.reshape(sequences, tokens, width),
            gain_one_grad[:, 0],
            g_query,
            g_key,
            g_value,
            output_grad,
            gain_two_grad[:, 0],
            g_gate,
            g_up,
            down_grad,
        )

    g_gu, g_qkv = g_gu.astype(f32), g_qkv.astype(f32)

    def back_hidden(part):
        return jnp.transpose(part.reshape(S, rows, Dp, down_rows), (1, 2, 0, 3)).reshape(rows, -1)

    def back_kv(part):
        part = jnp.sum(part.reshape(KV, repeats, rows, HEAD), axis=1)
        return jnp.transpose(part, (1, 0, 2)).reshape(rows, KV * HEAD)

    g_gate, g_up = back_hidden(g_gu[..., :hidden]), back_hidden(g_gu[..., hidden:])
    g_query = jnp.transpose(g_qkv[..., :q_cols], (1, 0, 2)).reshape(rows, width)
    g_key = back_kv(g_qkv[..., q_cols : q_cols + HEAD])
    g_value = back_kv(g_qkv[..., q_cols + HEAD :])

    def row_dot(weight, grad):
        return jnp.sum(weight.astype(f32) * grad, axis=1)

    gain_two_grad = row_dot(gate_weight, g_gate) + row_dot(up_weight, g_up)
    gain_one_grad = (
        row_dot(query_weight, g_query) + row_dot(key_weight, g_key) + row_dot(value_weight, g_value)
    )
    return (
        output.reshape(sequences, tokens, width),
        input_grad.reshape(sequences, tokens, width),
        gain_one_grad,
        g_query * gain_one,
        g_key * gain_one,
        g_value * gain_one,
        output_grad,
        gain_two_grad,
        g_gate * gain_two,
        g_up * gain_two,
        down_grad,
    )


def solution(mesh):
    both = ("dp", "seq")
    tok, vec, mat = P("dp", "seq", None), P(both), P(both, None)
    in_specs = (tok, vec, mat, mat, mat, mat, vec, mat, mat, mat, tok)
    out_specs = (tok, tok, vec, mat, mat, mat, mat, vec, mat, mat, mat)
    return jax.shard_map(shards, mesh=mesh, in_specs=in_specs, out_specs=out_specs, check_vma=False)
```

```python
import functools

import jax
import jax.numpy as jnp
from jax import lax
from jax.experimental import pallas as pl
from jax.experimental.pallas import tpu as pltpu
from jax.sharding import PartitionSpec as P

H = 32
KV = 4
HEAD = 64

epsilon = 1e-05
masked = -1e30
f32 = jnp.float32
bf16 = jnp.bfloat16


def rope_tables(length):
    half_width = HEAD // 2
    frequency = 10000.0 ** (-(jnp.arange(half_width, dtype=f32) * 2.0) / HEAD)
    angles = jnp.arange(length, dtype=f32)[:, None] * frequency[None, :]
    return (jnp.cos(angles)[:, None, :], jnp.sin(angles)[:, None, :])


def rotate(values, cosine, sine):
    front, back = values[..., : HEAD // 2], values[..., HEAD // 2 :]
    return jnp.concatenate([front * cosine - back * sine, back * cosine + front * sine], axis=-1)


def rms_scale(values):
    return lax.rsqrt(jnp.mean(values * values, axis=-1, keepdims=True) + epsilon)


def mm(a, b):
    return lax.dot_general(a, b, (((1,), (0,)), ((), ())), preferred_element_type=f32)


def mm_nt(a, b):
    return lax.dot_general(a, b, (((1,), (1,)), ((), ())), preferred_element_type=f32)


def mm_tn(a, b):
    return lax.dot_general(a, b, (((0,), (0,)), ((), ())), preferred_element_type=f32)


def seq_place():
    me = lax.axis_index("seq")
    return me // 2, me % 2

def hello(barrier, peer, axis):
    pl.semaphore_signal(
        barrier, inc=1, device_id={axis: peer}, device_id_type=pl.DeviceIdType.MESH
    )


def greet(z, y, Z, dp=None):
    barrier = pltpu.get_barrier_semaphore()
    hello(barrier, z * 2 + 1 - y, "seq")

    @pl.when(z > 0)
    def _():
        hello(barrier, z * 2 + y - 2, "seq")

    @pl.when(z < Z - 1)
    def _():
        hello(barrier, z * 2 + y + 2, "seq")

    count = 1 + (z + Z - 1) // Z + (2 * Z - 2 - z) // Z
    if dp is not None:
        hello(barrier, dp + 1 - 2 * (dp % 2), "dp")
        hello(barrier, dp + 2 - 4 * (dp // 2), "dp")
        count = count + 2
    pl.semaphore_wait(barrier, count)


def send(src, dst, ssem, rsem, peer, axis="seq"):
    return pltpu.make_async_remote_copy(
        src_ref=src,
        dst_ref=dst,
        send_sem=ssem,
        recv_sem=rsem,
        device_id={axis: peer},
        device_id_type=pl.DeviceIdType.MESH,
    )


def gather_kernel(Z, T, x_ref, out_ref, up_sem, dn_sem, y_sem, recv_sem, own_sem):
    z, y = seq_place()
    greet(z, y, Z)
    def block(zz, yy):
        return out_ref.at[pl.ds(pl.multiple_of((zz * 2 + yy) * T, T), T)]
    def copy(src, zz, sem, peer):
        return send(src, block(zz, y), sem.at[zz], recv_sem.at[zz * 2 + y], peer)
    own = pltpu.make_async_copy(x_ref, block(z, y), own_sem)
    own.start()
    peer_y, peer_up, peer_dn = z * 2 + 1 - y, z * 2 + y + 2, z * 2 + y - 2
    copy(x_ref, z, y_sem, peer_y).start()
    @pl.when(z < Z - 1)
    def _(): copy(x_ref, z, up_sem, peer_up).start()
    @pl.when(z > 0)
    def _(): copy(x_ref, z, dn_sem, peer_dn).start()
    for h in range(1, Z):
        @pl.when(z >= h)
        def _():
            zz = z - h
            copy(block(zz, y), zz, y_sem, peer_y).wait_recv()
            @pl.when(z < Z - 1)
            def _(): copy(block(zz, y), zz, up_sem, peer_up).start()
            copy(block(zz, y), zz, y_sem, peer_y).start()
        @pl.when(z + h < Z)
        def _():
            zz = z + h
            copy(block(zz, y), zz, y_sem, peer_y).wait_recv()
            @pl.when(z > 0)
            def _(): copy(block(zz, y), zz, dn_sem, peer_dn).start()
            copy(block(zz, y), zz, y_sem, peer_y).start()
    own.wait()
    for zz in range(Z):
        b = block(zz, 1 - y)
        send(b, b, y_sem.at[zz], recv_sem.at[zz * 2 + 1 - y], peer_y).wait_recv()
        c = copy(block(zz, y), zz, y_sem, peer_y)
        c.wait_send()
        @pl.when((zz <= z) & (z < Z - 1))
        def _(): copy(block(zz, y), zz, up_sem, peer_up).wait_send()
        @pl.when((zz >= z) & (z > 0))
        def _(): copy(block(zz, y), zz, dn_sem, peer_dn).wait_send()

def gather_line(x, cid=1):
    S = lax.axis_size("seq"); Z = S // 2
    T, D = x.shape
    return pl.pallas_call(
        functools.partial(gather_kernel, Z, T),
        out_shape=jax.ShapeDtypeStruct((S * T, D), x.dtype),
        in_specs=[pl.BlockSpec(memory_space=pltpu.VMEM)],
        out_specs=pl.BlockSpec(memory_space=pl.ANY),
        scratch_shapes=[pltpu.SemaphoreType.DMA((Z,))] * 3 + [pltpu.SemaphoreType.DMA((S,)), pltpu.SemaphoreType.DMA],
        compiler_params=pltpu.CompilerParams(collective_id=cid, has_side_effects=True),
        name="gather_seq",
    )(x)

def scatter_kernel(Z, T, p_ref, out_ref, ybuf, upbuf, dnbuf, upst, dnst, up_s, dn_s, y_s, up_r, dn_r, y_r):
    z, y = seq_place()
    greet(z, y, Z)
    peer_y, peer_up, peer_dn = z * 2 + 1 - y, z * 2 + y + 2, z * 2 + y - 2
    def mine(zz, yy):
        return p_ref.at[pl.ds(pl.multiple_of((zz * 2 + yy) * T, T), T)]
    def y_copy(zz):
        return send(mine(zz, 1 - y), ybuf.at[zz], y_s.at[zz], y_r.at[zz], peer_y)
    def up_copy(zz):
        return send(upst.at[zz], upbuf.at[zz], up_s.at[zz], up_r.at[zz], peer_up)
    def dn_copy(zz):
        return send(dnst.at[zz], dnbuf.at[zz], dn_s.at[zz], dn_r.at[zz], peer_dn)
    for h in range(Z - 1, 0, -1):
        @pl.when(z + h < Z)
        def _(): y_copy(z + h).start()
        @pl.when(z - h >= 0)
        def _(): y_copy(z - h).start()
    y_copy(z).start()
    for h in range(Z - 1, 0, -1):
        @pl.when(z + h < Z)
        def _():
            d = z + h
            y_copy(d).wait_recv()
            upst[d] = (mine(d, y)[...].astype(f32) + ybuf[d].astype(f32)).astype(bf16)
            @pl.when(z > 0)
            def _():
                up_copy(d).wait_recv()
                upst[d] = (mine(d, y)[...].astype(f32) + ybuf[d].astype(f32) + upbuf[d].astype(f32)).astype(bf16)
            up_copy(d).start()
        @pl.when(z - h >= 0)
        def _():
            d = z - h
            y_copy(d).wait_recv()
            dnst[d] = (mine(d, y)[...].astype(f32) + ybuf[d].astype(f32)).astype(bf16)
            @pl.when(z < Z - 1)
            def _():
                dn_copy(d).wait_recv()
                dnst[d] = (mine(d, y)[...].astype(f32) + ybuf[d].astype(f32) + dnbuf[d].astype(f32)).astype(bf16)
            dn_copy(d).start()
    y_copy(z).wait_recv()
    out_ref[...] = mine(z, y)[...].astype(f32) + ybuf[z].astype(f32)
    @pl.when(z > 0)
    def _():
        up_copy(z).wait_recv()
        out_ref[...] += upbuf[z].astype(f32)
    @pl.when(z < Z - 1)
    def _():
        dn_copy(z).wait_recv()
        out_ref[...] += dnbuf[z].astype(f32)
    for zz in range(Z):
        y_copy(zz).wait_send()
        @pl.when(zz > z)
        def _(): up_copy(zz).wait_send()
        @pl.when(zz < z)
        def _(): dn_copy(zz).wait_send()

def scatter_line(p, cid=2):
    S = lax.axis_size("seq"); Z = S // 2
    L, D = p.shape; T = L // S
    return pl.pallas_call(
        functools.partial(scatter_kernel, Z, T),
        out_shape=jax.ShapeDtypeStruct((T, D), f32),
        in_specs=[pl.BlockSpec(memory_space=pltpu.VMEM)],
        out_specs=pl.BlockSpec(memory_space=pltpu.VMEM),
        scratch_shapes=[pltpu.VMEM((Z, T, D), bf16)] * 5 + [pltpu.SemaphoreType.DMA((Z,))] * 6,
        compiler_params=pltpu.CompilerParams(collective_id=cid, has_side_effects=True, vmem_limit_bytes=60 << 20),
        name="scatter_seq",
    )(p)


def line_rank(i, z):
    upper = z // 2
    inner = (z + upper) % 2
    base = i + inner * (1 - i // 2) * (1 - 2 * i)
    return base + upper * (3 - 2 * base)


def above(d, z):
    return (d - z + 3) // 4


def rows_of(ref, start, size):
    return ref.at[pl.ds(pl.multiple_of(start, size), size)]


def in_chunks(rows, chunk, step):
    def body(i, carry):
        step(pl.ds(pl.multiple_of(i * chunk, chunk), chunk))
        return carry

    lax.fori_loop(0, rows // chunk, body, 0)


class Gather:
    def __init__(self, z, y, T, own, full, up_sem, dn_sem, y_sem, recv_sem, own_sem):
        self.z, self.y, self.T, self.own, self.full = z, y, T, own, full
        self.sems = {"up": up_sem, "dn": dn_sem, "y": y_sem}
        self.peers = {"up": z * 2 + y + 2, "dn": z * 2 + y - 2, "y": z * 2 + 1 - y}
        self.recv_sem, self.own_sem = recv_sem, own_sem

    def block(self, zz, yy):
        return rows_of(self.full, (zz * 2 + yy) * self.T, self.T)

    def copy(self, src, zz, way):
        return send(
            src,
            self.block(zz, self.y),
            self.sems[way].at[zz],
            self.recv_sem.at[zz * 2 + self.y],
            self.peers[way],
        )

    def start(self):
        z = self.z
        pltpu.make_async_copy(self.own, self.block(z, self.y), self.own_sem).start()
        self.copy(self.own, z, "y").start()

        @pl.when(z < 3)
        def _():
            self.copy(self.own, z, "up").start()

        @pl.when(z > 0)
        def _():
            self.copy(self.own, z, "dn").start()

    def own_ready(self):
        pltpu.make_async_copy(self.own, self.block(self.z, self.y), self.own_sem).wait()

    def hop(self, h):
        z = self.z

        @pl.when(z >= h)
        def _():
            src = self.block(z - h, self.y)
            self.copy(src, z - h, "y").wait_recv()

            @pl.when(z < 3)
            def _():
                self.copy(src, z - h, "up").start()

            self.copy(src, z - h, "y").start()

        @pl.when(z + h < 4)
        def _():
            src = self.block(z + h, self.y)
            self.copy(src, z + h, "y").wait_recv()

            @pl.when(z > 0)
            def _():
                self.copy(src, z + h, "dn").start()

            self.copy(src, z + h, "y").start()

    def pair_ready(self, zz):
        b = self.block(zz, 1 - self.y)
        send(
            b, b, self.sems["y"].at[zz], self.recv_sem.at[zz * 2 + 1 - self.y], self.peers["y"]
        ).wait_recv()

    def finish_one(self, zz):
        z = self.z
        src = self.block(zz, self.y)
        self.copy(src, zz, "y").wait_send()

        @pl.when((zz <= z) & (z < 3))
        def _():
            self.copy(src, zz, "up").wait_send()

        @pl.when((zz >= z) & (z > 0))
        def _():
            self.copy(src, zz, "dn").wait_send()

    def finish(self):
        for zz in range(4):
            self.finish_one(zz)


class Scatter:
    def __init__(self, z, y, T, part, ybuf, rbuf, y_s, y_r, z_s, z_r):
        self.z, self.y, self.T, self.part = z, y, T, part
        self.ybuf, self.rbuf = ybuf, rbuf
        self.y_s, self.y_r, self.z_s, self.z_r = y_s, y_r, z_s, z_r

    def rows(self, zz, yy):
        return rows_of(self.part, (zz * 2 + yy) * self.T, self.T)

    def y_copy(self, d):
        peer = self.z * 2 + 1 - self.y
        return send(
            self.rows(d, 1 - self.y), self.ybuf.at[d], self.y_s.at[d], self.y_r.at[d], peer
        )

    def z_copy(self, d, up):
        slot = d + up
        peer = self.z * 2 + self.y + 4 * up - 2
        return send(self.ybuf.at[d], self.rbuf.at[slot], self.z_s.at[d], self.z_r.at[slot], peer)

    def start(self, d):
        self.y_copy(d).start()

    def pass_on(self, d):
        z = self.z
        up = above(d, z)
        self.y_copy(d).wait_recv()
        mine, slot = self.rows(d, self.y), self.ybuf.at[d]
        inner = (z > 0) & (z < 3)

        @pl.when(inner)
        def _():
            self.z_copy(d, up).wait_recv()
            far = self.rbuf.at[d + up]

            def step(c):
                slot[c] = (
                    mine[c].astype(f32) + slot[c].astype(f32) + far[c].astype(f32)
                ).astype(bf16)

            in_chunks(self.T, 32, step)

        @pl.when(jnp.logical_not(inner))
        def _():
            def step(c):
                slot[c] = (mine[c].astype(f32) + slot[c].astype(f32)).astype(bf16)

            in_chunks(self.T, 32, step)

        self.z_copy(d, up).start()

    def finish(self, out_ref):
        z = self.z
        self.y_copy(z).wait_recv()
        mine, slot = self.rows(z, self.y), self.ybuf.at[z]

        def first(c):
            out_ref[c] = mine[c].astype(f32) + slot[c].astype(f32)

        in_chunks(self.T, 32, first)

        def more(slot):
            def step(c):
                out_ref[c] += slot[c].astype(f32)

            in_chunks(self.T, 32, step)

        @pl.when(z > 0)
        def _():
            self.z_copy(z, 1).wait_recv()
            more(self.rbuf.at[z + 1])

        @pl.when(z < 3)
        def _():
            self.z_copy(z, 0).wait_recv()
            more(self.rbuf.at[z])

        for d in range(4):
            self.y_copy(d).wait_send()

            @pl.when(z != d)
            def _():
                self.z_copy(d, above(d, z)).wait_send()


def line_sems(n):
    return [pltpu.SemaphoreType.DMA((4,))] * 3 + [
        pltpu.SemaphoreType.DMA((8,)),
        pltpu.SemaphoreType.DMA,
    ]


def sum_scratch(T, width):
    return [
        pltpu.VMEM((4, T, width), bf16),
        pltpu.VMEM((5, T, width), bf16),
        pltpu.SemaphoreType.DMA((4,)),
        pltpu.SemaphoreType.DMA((4,)),
        pltpu.SemaphoreType.DMA((4,)),
        pltpu.SemaphoreType.DMA((5,)),
    ]


class DpSum:
    def __init__(self, src, size, abuf, bbuf, a_s, a_r, b_s, b_r):
        dp = lax.axis_index("dp")
        self.core, self.far = dp % 2, dp // 2
        self.partner, self.across = dp + 1 - 2 * (dp % 2), dp + 2 - 4 * (dp // 2)
        self.src, self.size = src, size
        self.abuf, self.bbuf = abuf, bbuf
        self.a_s, self.a_r, self.b_s, self.b_r = a_s, a_r, b_s, b_r

    def rows(self, d):
        return rows_of(self.src, d * self.size, self.size)

    def a_copy(self, j):
        return send(
            self.rows(2 * j + 1 - self.core),
            self.abuf.at[j],
            self.a_s.at[j],
            self.a_r.at[j],
            self.partner,
            "dp",
        )

    def b_copy(self):
        return send(self.abuf.at[1 - self.far], self.bbuf, self.b_s, self.b_r, self.across, "dp")

    def start(self):
        self.a_copy(0).start()
        self.a_copy(1).start()

    def middle(self):
        self.a_copy(0).wait_recv()
        self.a_copy(1).wait_recv()
        j = 1 - self.far
        mine, slot = self.rows(2 * j + self.core), self.abuf.at[j]

        def step(c):
            slot[c] = (mine[c].astype(f32) + slot[c].astype(f32)).astype(bf16)

        in_chunks(self.size, 16, step)
        self.b_copy().start()

    def finish(self, out_ref):
        self.b_copy().wait_recv()
        mine, slot = self.rows(2 * self.far + self.core), self.abuf.at[self.far]

        def step(c):
            out_ref[c] = (
                mine[c].astype(f32) + slot[c].astype(f32) + self.bbuf[c].astype(f32)
            ).astype(out_ref.dtype)

        in_chunks(self.size, 16, step)
        self.a_copy(0).wait_send()
        self.a_copy(1).wait_send()
        self.b_copy().wait_send()


class DpGather:
    def __init__(self, own, full, size, s_sem, r_sem):
        dp = lax.axis_index("dp")
        self.dp, self.partner, self.across = dp, dp + 1 - 2 * (dp % 2), dp + 2 - 4 * (dp // 2)
        self.diagonal = 3 - dp
        self.own, self.full, self.size = own, full, size
        self.s_sem, self.r_sem = s_sem, r_sem

    def block(self, d):
        return rows_of(self.full, d * self.size, self.size)

    def copy(self, src, d, k, peer):
        return send(src, self.block(d), self.s_sem.at[k], self.r_sem.at[k], peer, "dp")

    def start(self):
        self.copy(self.own, self.dp, 0, self.across).start()
        self.copy(self.own, self.dp, 1, self.partner).start()

    def relay(self):
        far = self.block(self.across)
        self.copy(far, self.across, 0, self.across).wait_recv()
        self.copy(far, self.across, 2, self.partner).start()

    def ready(self):
        near, diagonal = self.block(self.partner), self.block(self.diagonal)
        self.copy(near, self.partner, 1, self.partner).wait_recv()
        self.copy(diagonal, self.diagonal, 2, self.partner).wait_recv()

    def finish(self):
        self.copy(self.own, self.dp, 0, self.across).wait_send()
        self.copy(self.own, self.dp, 1, self.partner).wait_send()
        self.copy(self.block(self.across), self.across, 2, self.partner).wait_send()


def dp_scratch(size, width):
    return [
        pltpu.VMEM((2, size, width), bf16),
        pltpu.VMEM((size, width), bf16),
        pltpu.SemaphoreType.DMA((2,)),
        pltpu.SemaphoreType.DMA((2,)),
        pltpu.SemaphoreType.DMA,
        pltpu.SemaphoreType.DMA,
    ]


def feedforward_kernel(
    T, x_ref, dy_ref, wgu_ref, wd_ref, pout_ref, e2_ref, ggu_ref, gd_ref,
    full, hid, dgu, part, ggu, gdown, up_sem, dn_sem, ag_y, ag_r, own_sem,
    ybuf, rbuf, y_s, y_r, z_s, z_r,
    ga, gb, ga_s, ga_r, gb_s, gb_r,
    da, db, da_s, da_r, db_s, db_r,
):
    z, y = seq_place()
    dp = lax.axis_index("dp")
    F = hid.shape[1]
    greet(z, y, 4, dp)
    gather = Gather(z, y, T, x_ref, full, up_sem, dn_sem, ag_y, ag_r, own_sem)
    scatter = Scatter(z, y, T, part, ybuf, rbuf, y_s, y_r, z_s, z_r)
    sum_gu = DpSum(ggu, ggu.shape[0] // 4, ga, gb, ga_s, ga_r, gb_s, gb_r)
    sum_down = DpSum(gdown, gd_ref.shape[0], da, db, da_s, da_r, db_s, db_r)
    gather.start()
    gather.own_ready()

    def compute(i, carry):
        for h in range(1, 4):

            @pl.when(i == h - 1)
            def _():
                gather.hop(h)

        zz = line_rank(i, z)
        gather.pair_ready(zz)

        @pl.when(i == 3)
        def _():
            scatter.start(line_rank(2, z))

        r = pl.ds(pl.multiple_of(zz * 2 * T, 2 * T), 2 * T)
        gu = mm(full[r, :], wgu_ref[...])
        gate, up = gu[:, :F], gu[:, F:]
        sig = 1.0 / (1.0 + jnp.exp(-gate))
        act = gate * sig
        h = (act * up).astype(bf16)
        hid[r, :] = h
        pout_ref[r, :] = mm(h, wd_ref[...]).astype(bf16)
        dh = mm_nt(dy_ref[r, :], wd_ref[...])
        dgu[r, :F] = (dh * up * sig * (1.0 + gate * (1.0 - sig))).astype(bf16)
        dgu[r, F:] = (dh * act).astype(bf16)
        part[r, :] = mm_nt(dgu[r, :], wgu_ref[...]).astype(bf16)
        return carry

    lax.fori_loop(0, 4, compute, 0)
    for i in (3, 1, 0):
        scatter.start(line_rank(i, z))

    def gate_up_tile(i, carry):
        r = pl.ds(pl.multiple_of(i * 256, 256), 256)
        ggu[r, :] = mm_tn(full[:, r], dgu[...]).astype(bf16)
        return carry

    def down_tile(i, carry):
        r = pl.ds(pl.multiple_of(i * 256, 256), 256)
        gdown[r, :] = mm_tn(hid[:, r], dy_ref[...]).astype(bf16)
        return carry

    lax.fori_loop(0, 8, gate_up_tile, 0)
    sum_gu.start()
    scatter.pass_on(line_rank(3, z))
    lax.fori_loop(0, F // 256, down_tile, 0)
    sum_down.start()
    sum_gu.middle()
    scatter.pass_on(line_rank(2, z))
    sum_down.middle()
    scatter.pass_on(line_rank(1, z))
    sum_gu.finish(ggu_ref)
    sum_down.finish(gd_ref)
    scatter.finish(e2_ref)
    gather.finish()


def feedforward(x, dy_all, w_gu, w_d, down_rows, cid=3):
    T, width = x.shape
    L, F = dy_all.shape[0], w_d.shape[0]
    vmem = pl.BlockSpec(memory_space=pltpu.VMEM)
    return pl.pallas_call(
        functools.partial(feedforward_kernel, T),
        out_shape=(
            jax.ShapeDtypeStruct((L, width), bf16),
            jax.ShapeDtypeStruct((T, width), f32),
            jax.ShapeDtypeStruct((width // 4, 2 * F), bf16),
            jax.ShapeDtypeStruct((down_rows, width), f32),
        ),
        in_specs=[vmem] * 4,
        out_specs=(vmem,) * 4,
        scratch_shapes=[
            pltpu.VMEM((L, width), bf16),
            pltpu.VMEM((L, F), bf16),
            pltpu.VMEM((L, 2 * F), bf16),
            pltpu.VMEM((L, width), bf16),
            pltpu.VMEM((width, 2 * F), bf16),
            pltpu.VMEM((F, width), bf16),
        ]
        + line_sems(4)
        + sum_scratch(T, width)
        + dp_scratch(width // 4, 2 * F)
        + dp_scratch(down_rows, width),
        compiler_params=pltpu.CompilerParams(
            collective_id=cid, has_side_effects=True, vmem_limit_bytes=67000000
        ),
        name="feedforward",
    )(x, dy_all, w_gu, w_d)


def attention_front_kernel(
    T, heads, s1_ref, piece_ref, wo_piece_ref, dy_ref, table_ref,
    mid_ref, s1_all, dy_all, wqkv, wo, q_out, k2_ref, kz_ref, vz_ref, lse_ref, att_ref,
    score, part,
    up_sem, dn_sem, ag_y, ag_r, own_sem,
    up_sem2, dn_sem2, ag_y2, ag_r2, own_sem2,
    ybuf, rbuf, y_s, y_r, z_s, z_r,
    w_s, w_r, o_s, o_r, ex_s, ex_r, ex_own, wo_own,
):
    z, y = seq_place()
    me = z * 2 + y
    dp = lax.axis_index("dp")
    rows, out_rows = piece_ref.shape[1], wo_piece_ref.shape[0]
    barrier = pltpu.get_barrier_semaphore()
    for step in range(1, 8):
        hello(barrier, (me + step) % 8, "seq")
    hello(barrier, dp + 1 - 2 * (dp % 2), "dp")
    hello(barrier, dp + 2 - 4 * (dp // 2), "dp")
    pl.semaphore_wait(barrier, 9)
    gather = Gather(z, y, T, s1_ref, s1_all, up_sem, dn_sem, ag_y, ag_r, own_sem)
    gather_dy = Gather(z, y, T, dy_ref, dy_all, up_sem2, dn_sem2, ag_y2, ag_r2, own_sem2)
    scatter = Scatter(z, y, T, part, ybuf, rbuf, y_s, y_r, z_s, z_r)
    w_own = rows_of(wqkv, dp * 8 * rows, 8 * rows)
    w_all = DpGather(w_own, wqkv, 8 * rows, w_s, w_r)
    o_all = DpGather(wo_piece_ref, wo, out_rows, o_s, o_r)

    def landing(peer):
        return rows_of(wqkv, (dp * 8 + peer) * rows, rows)

    def exchange(peer):
        return send(piece_ref.at[peer], landing(me), ex_s.at[peer], ex_r.at[me], peer)

    own = pltpu.make_async_copy(piece_ref.at[me], landing(me), ex_own)
    own.start()
    own_o = pltpu.make_async_copy(wo_piece_ref, o_all.block(dp), wo_own)
    own_o.start()
    for step in range(1, 8):
        exchange((me + step) % 8).start()
    gather.start()
    o_all.start()
    own.wait()
    own_o.wait()
    for step in range(1, 8):
        peer = (me + step) % 8
        send(
            piece_ref.at[me], landing(peer), ex_s.at[peer], ex_r.at[peer], peer
        ).wait_recv()
    w_all.start()
    gather.own_ready()
    gather.hop(1)
    o_all.relay()
    w_all.relay()
    w_all.ready()
    U = 2 * T
    lane = lax.broadcasted_iota(jnp.int32, (U, 128), 1)
    low_lanes = lane < HEAD
    front = lane % HEAD < HEAD // 2
    scale = HEAD ** (-0.5)

    def swapped(u):
        return jnp.where(front, pltpu.roll(u, 128 - HEAD // 2, 1), pltpu.roll(u, HEAD // 2, 1))

    def project(i, carry):
        for h in (2, 3):

            @pl.when(i == h - 1)
            def _():
                gather.hop(h)

        @pl.when(i == 2)
        def _():
            gather_dy.start()

        u = line_rank(i, z)
        gather.pair_ready(u)
        r = pl.ds(pl.multiple_of(u * U, U), U)
        qkv = mm(s1_all[r, :], wqkv[...])
        cos, sin = table_ref[r, :128], table_ref[r, 128:]

        def roped(tile):
            return tile * cos + swapped(tile) * sin

        for h in range(0, heads, 2):
            turned = roped(qkv[:, h * HEAD : (h + 2) * HEAD])
            other = swapped(turned)
            q_out[h, r, :] = jnp.where(low_lanes, turned, pltpu.roll(other, HEAD, 1)).astype(bf16)
            q_out[h + 1, r, :] = jnp.where(low_lanes, pltpu.roll(turned, HEAD, 1), other).astype(bf16)
        tile = qkv[:, heads * HEAD :]
        turned = roped(tile)
        k2_ref[r, :] = jnp.where(low_lanes, turned, pltpu.roll(swapped(turned), HEAD, 1)).astype(bf16)
        kz_ref[r, :] = jnp.where(low_lanes, turned, 0.0).astype(bf16)
        vz_ref[r, :] = jnp.where(low_lanes, pltpu.roll(tile, HEAD, 1), 0.0).astype(bf16)
        return carry

    lax.fori_loop(0, 4, project, 0)
    o_all.ready()
    gather_dy.own_ready()

    def unit(i, carry):
        for h in range(1, 4):

            @pl.when(i == h)
            def _():
                gather_dy.hop(h)

        u = line_rank(3 - i, z)
        r = pl.ds(pl.multiple_of(u * U, U), U)
        q = q_out[:, r, :].reshape(heads * U, 128)

        def scores(j, top):
            c = pl.ds(pl.multiple_of(j * U, U), U)
            s = mm_nt(q, kz_ref[c, :]) * scale
            row = lax.broadcasted_iota(jnp.int32, (heads, U, U), 1).reshape(heads * U, U)
            col = lax.broadcasted_iota(jnp.int32, (heads * U, U), 1)
            s = jnp.where(col + (j - u) * U <= row, s, masked)
            score[j] = s
            return jnp.maximum(top, jnp.max(s, axis=1, keepdims=True))

        top = lax.fori_loop(0, u + 1, scores, jnp.full((heads * U, 1), masked, f32))

        def weigh(j, carry):
            total, out = carry
            c = pl.ds(pl.multiple_of(j * U, U), U)
            p = jnp.exp(score[j] - top)
            return (
                total + jnp.sum(p, axis=1, keepdims=True),
                out + mm(p.astype(bf16), vz_ref[c, :]),
            )

        total, out = lax.fori_loop(
            0,
            u + 1,
            weigh,
            (jnp.zeros((heads * U, 1), f32), jnp.zeros((heads * U, 128), f32)),
        )
        lse_ref[:, r, :] = (top + jnp.log(total)).reshape(heads, U, 1)
        out = out / total
        for h in range(0, heads, 2):
            first, second = out[h * U : (h + 1) * U], out[(h + 1) * U : (h + 2) * U]
            att_ref[r, h * HEAD : (h + 2) * HEAD] = jnp.where(
                low_lanes, first, pltpu.roll(second, HEAD, 1)
            ).astype(bf16)
        part[r, :] = mm(att_ref[r, :], wo[...]).astype(bf16)
        scatter.start(u)
        for k in (1, 2):

            @pl.when(i == k)
            def _():
                scatter.pass_on(line_rank(4 - k, z))

        return carry

    lax.fori_loop(0, 4, unit, 0)
    scatter.pass_on(line_rank(1, z))
    scatter.finish(mid_ref)
    for zz in range(4):
        gather.finish_one(zz)
        gather_dy.pair_ready(zz)
        gather_dy.finish_one(zz)
    for step in range(1, 8):
        exchange((me + step) % 8).wait_send()
    w_all.finish()
    o_all.finish()


def attention_front(s1, piece, wo_piece, dy, table, heads, cid=5):
    T, width = s1.shape
    S, rows, cols = piece.shape
    L, q_cols, U = S * T, heads * HEAD, 2 * T
    vmem = pl.BlockSpec(memory_space=pltpu.VMEM)
    return pl.pallas_call(
        functools.partial(attention_front_kernel, T, heads),
        out_shape=(
            jax.ShapeDtypeStruct((T, width), f32),
            jax.ShapeDtypeStruct((L, width), bf16),
            jax.ShapeDtypeStruct((L, width), bf16),
            jax.ShapeDtypeStruct((width, cols), bf16),
            jax.ShapeDtypeStruct((q_cols, width), bf16),
            jax.ShapeDtypeStruct((heads, L, 128), bf16),
            jax.ShapeDtypeStruct((L, 128), bf16),
            jax.ShapeDtypeStruct((L, 128), bf16),
            jax.ShapeDtypeStruct((L, 128), bf16),
            jax.ShapeDtypeStruct((heads, L, 1), f32),
            jax.ShapeDtypeStruct((L, q_cols), bf16),
        ),
        in_specs=[vmem] * 5,
        out_specs=(vmem,) * 11,
        scratch_shapes=[
            pltpu.VMEM((L // U, heads * U, U), f32),
            pltpu.VMEM((L, width), bf16),
        ]
        + line_sems(4)
        + line_sems(4)
        + sum_scratch(T, width)
        + [pltpu.SemaphoreType.DMA((3,))] * 4
        + [pltpu.SemaphoreType.DMA((8,))] * 2
        + [pltpu.SemaphoreType.DMA] * 2,
        compiler_params=pltpu.CompilerParams(
            collective_id=cid, has_side_effects=True, vmem_limit_bytes=67000000
        ),
        name="attention_front",
    )(s1, piece, wo_piece, dy, table)


def attention_back_kernel(
    T, heads, dm_ref, q_ref, k_ref, kz_ref, vz_ref, lse_ref, att_ref, s1_ref, wqkv_ref, wo_ref, table_ref,
    e1_ref, got_ref, go_ref,
    full, grads, probs, dprobs, dk, dv, dqkv, part, gqkv, go_part, gsum,
    up_sem, dn_sem, ag_y, ag_r, own_sem,
    ybuf, rbuf, y_s, y_r, z_s, z_r,
    qa, qb, qa_s, qa_r, qb_s, qb_r,
    oa, ob, oa_s, oa_r, ob_s, ob_r,
    ex_s, ex_r, ex_own,
):
    z, y = seq_place()
    me = z * 2 + y
    dp = lax.axis_index("dp")
    rows = got_ref.shape[1]
    barrier = pltpu.get_barrier_semaphore()
    for step in range(1, 8):
        hello(barrier, (me + step) % 8, "seq")
    hello(barrier, dp + 1 - 2 * (dp % 2), "dp")
    hello(barrier, dp + 2 - 4 * (dp // 2), "dp")
    pl.semaphore_wait(barrier, 9)
    gather = Gather(z, y, T, dm_ref, full, up_sem, dn_sem, ag_y, ag_r, own_sem)
    scatter = Scatter(z, y, T, part, ybuf, rbuf, y_s, y_r, z_s, z_r)
    sum_qkv = DpSum(gqkv, gqkv.shape[0] // 4, qa, qb, qa_s, qa_r, qb_s, qb_r)
    sum_o = DpSum(go_part, go_part.shape[0] // 4, oa, ob, oa_s, oa_r, ob_s, ob_r)
    gather.start()
    dk[...] = jnp.zeros_like(dk)
    dv[...] = jnp.zeros_like(dv)
    gather.own_ready()
    U = 2 * T
    low_lanes = lax.broadcasted_iota(jnp.int32, (U, 128), 1) < HEAD
    scale = HEAD ** (-0.5)

    def both(product, table):
        turned = product * table
        return turned + pltpu.roll(turned, HEAD, 1)

    def unit(i, carry):
        for h in range(1, 4):

            @pl.when(i == h - 1)
            def _():
                gather.hop(h)

        u = line_rank(i, z)
        gather.pair_ready(u)
        r = pl.ds(pl.multiple_of(u * U, U), U)
        d_att = mm_nt(full[r, :], wo_ref[...]).astype(bf16)
        for h in range(heads):
            grads[h] = d_att[:, h * 128 : (h + 1) * 128]
        g = grads[...].reshape(heads * U, 128)
        q = q_ref[:, r, :].reshape(heads * U, 128)
        lse = lse_ref[:, r, :].reshape(heads * U, 1)

        def scores(j, inner):
            c = pl.ds(pl.multiple_of(j * U, U), U)
            s = mm_nt(q, kz_ref[c, :]) * scale
            row = lax.broadcasted_iota(jnp.int32, (heads, U, U), 1).reshape(heads * U, U)
            col = lax.broadcasted_iota(jnp.int32, (heads * U, U), 1)
            s = jnp.where(col + (j - u) * U <= row, s, masked)
            p = jnp.exp(s - lse)
            dp_ = mm_nt(g, vz_ref[c, :])
            probs[j] = p
            dprobs[j] = dp_
            return inner + jnp.sum(p * dp_, axis=1, keepdims=True)

        inner = lax.fori_loop(0, u + 1, scores, jnp.zeros((heads * U, 1), f32))

        def products(j, dq):
            c = pl.ds(pl.multiple_of(j * U, U), U)
            p = probs[j]
            ds = (p * (dprobs[j] - inner)).astype(bf16)
            dk[c, :] += mm_tn(ds, q)
            dv[c, :] += mm_tn(p.astype(bf16), g)
            return dq + mm(ds, k_ref[c, :])

        dq = lax.fori_loop(0, u + 1, products, jnp.zeros((heads * U, 128), f32))
        table = table_ref[r, :]
        for h in range(0, heads, 2):
            first = both(dq[h * U : (h + 1) * U], table)
            second = both(dq[(h + 1) * U : (h + 2) * U], table)
            dqkv[r, h * HEAD : (h + 2) * HEAD] = jnp.where(low_lanes, first, second).astype(bf16)
        return carry

    lax.fori_loop(0, 4, unit, 0)

    def part_rows(i):
        u = line_rank(i, z)
        r = pl.ds(pl.multiple_of(u * U, U), U)
        d_key = both(dk[r, :], table_ref[r, :])
        dqkv[r, heads * HEAD :] = jnp.where(low_lanes, d_key, pltpu.roll(dv[r, :], HEAD, 1)).astype(bf16)
        part[r, :] = mm_nt(dqkv[r, :], wqkv_ref[...]).astype(bf16)
        scatter.start(u)

    def part_loop(i, carry):
        part_rows(3 - i)
        return carry

    lax.fori_loop(0, 4, part_loop, 0)

    def qkv_tile(i, carry):
        r = pl.ds(pl.multiple_of(i * 256, 256), 256)
        gqkv[r, :] = mm_tn(s1_ref[:, r], dqkv[...]).astype(bf16)
        return carry

    lax.fori_loop(0, gqkv.shape[0] // 256, qkv_tile, 0)
    sum_qkv.start()
    scatter.pass_on(line_rank(3, z))
    sum_qkv.middle()
    go_part[...] = mm_tn(att_ref[...], full[...]).astype(bf16)
    sum_o.start()
    scatter.pass_on(line_rank(2, z))
    sum_qkv.finish(gsum)

    def piece(peer):
        return rows_of(gsum, peer * rows, rows)

    def exchange(peer):
        return send(piece(peer), got_ref.at[me], ex_s.at[peer], ex_r.at[me], peer)

    own = pltpu.make_async_copy(piece(me), got_ref.at[me], ex_own)
    own.start()
    for step in range(1, 8):
        exchange((me + step) % 8).start()
    sum_o.middle()
    scatter.pass_on(line_rank(1, z))
    sum_o.finish(go_ref)
    scatter.finish(e1_ref)
    own.wait()
    for step in range(1, 8):
        peer = (me + step) % 8
        send(piece(me), got_ref.at[peer], ex_s.at[peer], ex_r.at[peer], peer).wait_recv()
        exchange(peer).wait_send()
    gather.finish()


def attention_back(dm, q2, k2, kz, vz, lse, attended, s1_all, w_qkv, w_o2, table, rows, cid=4):
    T, width = dm.shape
    heads, L, _ = q2.shape
    cols = w_qkv.shape[1]
    vmem = pl.BlockSpec(memory_space=pltpu.VMEM)
    U = 2 * T
    return pl.pallas_call(
        functools.partial(attention_back_kernel, T, heads),
        out_shape=(
            jax.ShapeDtypeStruct((T, width), f32),
            jax.ShapeDtypeStruct((8, rows, cols), bf16),
            jax.ShapeDtypeStruct((rows, width), f32),
        ),
        in_specs=[vmem] * 11,
        out_specs=(vmem,) * 3,
        scratch_shapes=[
            pltpu.VMEM((L, width), bf16),
            pltpu.VMEM((heads, U, 128), bf16),
            pltpu.VMEM((L // U, heads * U, U), f32),
            pltpu.VMEM((L // U, heads * U, U), f32),
            pltpu.VMEM((L, 128), f32),
            pltpu.VMEM((L, 128), f32),
            pltpu.VMEM((L, cols), bf16),
            pltpu.VMEM((L, width), bf16),
            pltpu.VMEM((width, cols), bf16),
            pltpu.VMEM((heads * HEAD, width), bf16),
            pltpu.VMEM((width // 4, cols), bf16),
        ]
        + line_sems(4)
        + sum_scratch(T, width)
        + dp_scratch(width // 4, cols)
        + dp_scratch(rows, width)
        + [pltpu.SemaphoreType.DMA((8,)), pltpu.SemaphoreType.DMA((8,)), pltpu.SemaphoreType.DMA],
        compiler_params=pltpu.CompilerParams(
            collective_id=cid, has_side_effects=True, vmem_limit_bytes=67000000
        ),
        name="attention_back",
    )(dm, q2, k2, kz, vz, lse, attended, s1_all, w_qkv, w_o2, table)


def spread_kernel(
    down_rows, repeats, gu_ref, qkv_ref, wg_ref, wu_ref, wq_ref, wk_ref, wv_ref, one_ref, two_ref,
    gate_ref, up_ref, query_ref, key_ref, value_ref, gain1_ref, gain2_ref,
):
    S, rows, wide = gu_ref.shape
    F = wide // 2
    Dp = gate_ref.shape[1] // (S * down_rows)
    q_cols = query_ref.shape[1] // S
    for s in range(S):
        for d in range(Dp):
            to = pl.ds((d * S + s) * down_rows, down_rows)
            gate_ref[:, to] = gu_ref[s, :, d * down_rows : (d + 1) * down_rows].astype(f32)
            up_ref[:, to] = gu_ref[s, :, F + d * down_rows : F + (d + 1) * down_rows].astype(f32)
        query_ref[:, s * q_cols : (s + 1) * q_cols] = qkv_ref[s, :, :q_cols].astype(f32)
    for j in range(S // repeats):
        total = qkv_ref[j * repeats, :, q_cols:].astype(f32)
        for s in range(j * repeats + 1, (j + 1) * repeats):
            total = total + qkv_ref[s, :, q_cols:].astype(f32)
        key_ref[:, j * HEAD : (j + 1) * HEAD] = total[:, :HEAD]
        value_ref[:, j * HEAD : (j + 1) * HEAD] = total[:, HEAD:]

    def close(pairs, gain_ref, out_ref):
        total = jnp.zeros((rows, 1), f32)
        for weight_ref, grad_ref in pairs:
            grad = grad_ref[...]
            total = total + jnp.sum(weight_ref[...].astype(f32) * grad, axis=1, keepdims=True)
            grad_ref[...] = grad * gain_ref[...]
        out_ref[...] = total

    close(((wg_ref, gate_ref), (wu_ref, up_ref)), two_ref, gain2_ref)
    close(((wq_ref, query_ref), (wk_ref, key_ref), (wv_ref, value_ref)), one_ref, gain1_ref)


def spread(gu, qkv, weights, gains, down_rows, repeats):
    rows = gu.shape[1]
    outs = [jax.ShapeDtypeStruct(w.shape, f32) for w in weights]
    outs += [jax.ShapeDtypeStruct((rows, 1), f32)] * 2
    vmem = pl.BlockSpec(memory_space=pltpu.VMEM)
    return pl.pallas_call(
        functools.partial(spread_kernel, down_rows, repeats),
        out_shape=tuple(outs),
        in_specs=[vmem] * 9,
        out_specs=(vmem,) * 7,
        compiler_params=pltpu.CompilerParams(vmem_limit_bytes=40 << 20),
        name="spread",
    )(gu, qkv, *weights, *gains)


def gather_seq(rows):
    if lax.axis_size("seq") == 8:
        return gather_line(rows)
    return lax.all_gather(rows, "seq", axis=0, tiled=True)


def scatter_seq(rows):
    if lax.axis_size("seq") == 8:
        return scatter_line(rows)
    return lax.psum_scatter(rows, "seq", scatter_dimension=0, tiled=True).astype(f32)


def feedforward_plain(x, dy_all, w_gu, w_d):
    hidden = w_d.shape[0]
    s2_all = gather_seq(x)
    gate_up = mm(s2_all, w_gu)
    gate, up = gate_up[:, :hidden], gate_up[:, hidden:]
    sig = jax.nn.sigmoid(gate)
    hid = (gate * sig * up).astype(bf16)
    d_hid = mm_nt(dy_all, w_d)
    d_gate = (d_hid * up * sig * (1.0 + gate * (1.0 - sig))).astype(bf16)
    d_up = (d_hid * (gate * sig)).astype(bf16)
    d_gu = jnp.concatenate([d_gate, d_up], axis=1)
    return (
        mm(hid, w_d).astype(bf16),
        scatter_seq(mm_nt(d_gu, w_gu).astype(bf16)),
        scatter_dp(mm_tn(s2_all, d_gu).astype(bf16)),
        scatter_dp(mm_tn(hid, dy_all).astype(bf16)).astype(f32),
    )


def gather_dp(rows):
    return lax.all_gather(rows, "dp", axis=0, tiled=True)


def scatter_dp(rows):
    return lax.psum_scatter(rows, "dp", scatter_dimension=0, tiled=True)


def exchange_seq(pieces):
    return lax.all_to_all(pieces, "seq", split_axis=0, concat_axis=0, tiled=True)


def causal_mask(offset, block_rows, block_end):
    return jnp.arange(block_end)[None, :] <= (offset + jnp.arange(block_rows))[:, None]


def attention_forward(queries, keys, values, block_rows):
    outputs, totals = [], []
    for offset in range(0, queries.shape[1], block_rows):
        end = offset + block_rows
        scores = jnp.einsum(
            "hqd,kd->hqk", queries[:, offset:end], keys[:end], preferred_element_type=f32
        ) * HEAD ** (-0.5)
        scores = jnp.where(causal_mask(offset, block_rows, end), scores, masked)
        row_max = jnp.max(scores, axis=-1, keepdims=True)
        total = row_max + jnp.log(jnp.sum(jnp.exp(scores - row_max), axis=-1, keepdims=True))
        probs_low = jnp.exp(scores - total).astype(bf16)
        outputs.append(
            jnp.einsum("hqk,kd->hqd", probs_low, values[:end], preferred_element_type=f32).astype(
                bf16
            )
        )
        totals.append(total)
    return jnp.concatenate(outputs, axis=1), jnp.concatenate(totals, axis=1)


def attention_backward(queries, keys, values, grads, totals, block_rows):
    length = keys.shape[0]
    scale = HEAD ** (-0.5)
    key_sum = jnp.zeros((length, HEAD), f32)
    value_sum = jnp.zeros((length, HEAD), f32)
    query_parts = []
    for offset in range(0, length, block_rows):
        end = offset + block_rows
        query_block, grad_block = queries[:, offset:end], grads[:, offset:end]
        key_block, value_block = keys[:end], values[:end]
        scores = (
            jnp.einsum("hqd,kd->hqk", query_block, key_block, preferred_element_type=f32) * scale
        )
        scores = jnp.where(causal_mask(offset, block_rows, end), scores, masked)
        probs = jnp.exp(scores - totals[:, offset:end])
        probs_low = probs.astype(bf16)
        grad_probs = jnp.einsum(
            "hqd,kd->hqk", grad_block, value_block, preferred_element_type=f32
        )
        inner = jnp.sum(probs * grad_probs, axis=-1, keepdims=True)
        grad_scores = (probs * (grad_probs - inner)).astype(bf16)
        query_parts.append(
            jnp.einsum("hqk,kd->hqd", grad_scores, key_block, preferred_element_type=f32) * scale
        )
        padding = ((0, length - end), (0, 0))
        key_sum = key_sum + jnp.pad(
            jnp.einsum("hqk,hqd->kd", grad_scores, query_block, preferred_element_type=f32)
            * scale,
            padding,
        )
        value_sum = value_sum + jnp.pad(
            jnp.einsum("hqk,hqd->kd", probs_low, grad_block, preferred_element_type=f32), padding
        )
    return jnp.concatenate(query_parts, axis=1), key_sum, value_sum


def heads_first(flat, heads):
    return jnp.transpose(flat.reshape(flat.shape[0], heads, HEAD), (1, 0, 2))


def heads_last(stacked):
    return jnp.transpose(stacked, (1, 0, 2)).reshape(stacked.shape[1], -1)


def shards(
    inputs,
    attention_gain,
    query_weight,
    key_weight,
    value_weight,
    output_weight,
    feedforward_gain,
    gate_weight,
    up_weight,
    down_weight,
    cotangent,
):
    S, Dp = lax.axis_size("seq"), lax.axis_size("dp")
    sequences, tokens, width = inputs.shape
    length = tokens * S
    rows = query_weight.shape[0]
    heads = H // S
    q_cols = heads * HEAD
    repeats = S // KV
    down_rows = down_weight.shape[0]
    hidden = down_rows * Dp
    block_rows = min(length, max(512, length // 8))

    gain_one = attention_gain.astype(f32)[:, None]
    gain_two = feedforward_gain.astype(f32)[:, None]

    def folded(weight, gain):
        return (weight.astype(f32) * gain).astype(bf16)

    def per_group_kv(weight):
        return jnp.repeat(weight.reshape(rows, KV, HEAD), repeats, axis=1)

    def per_group_hidden(weight):
        return jnp.transpose(weight.reshape(rows, Dp, S, down_rows), (2, 0, 1, 3)).reshape(
            S, rows, hidden
        )

    packed = jnp.concatenate(
        [
            folded(query_weight, gain_one).reshape(rows, S, q_cols),
            per_group_kv(folded(key_weight, gain_one)),
            per_group_kv(folded(value_weight, gain_one)),
        ],
        axis=2,
    )
    packed_qkv = jnp.transpose(packed, (1, 0, 2))
    forward_perm = [(Dp * s + d, d * S + s) for s in range(S) for d in range(Dp)]
    backward_perm = [(b, a) for a, b in forward_perm]
    w_o_piece = lax.ppermute(output_weight, ("dp", "seq"), forward_perm)
    packed = jnp.concatenate(
        [
            per_group_hidden(folded(gate_weight, gain_two)),
            per_group_hidden(folded(up_weight, gain_two)),
        ],
        axis=2,
    )
    line = S == 8 and Dp == 4
    width_f = -(-hidden // 256) * 256 if line else hidden

    def padded(part, axis):
        pads = [(0, 0)] * part.ndim
        pads[axis] = (0, width_f - hidden)
        return jnp.pad(part, pads)

    packed = exchange_seq(packed).reshape(S * rows, 2 * hidden)
    packed = jnp.concatenate(
        [padded(packed[:, :hidden], 1), padded(packed[:, hidden:], 1)], axis=1
    )
    w_gu = gather_dp(packed)
    w_d = padded(gather_dp(down_weight), 0)

    flat = inputs.reshape(tokens, width).astype(f32)
    r1 = rms_scale(flat)
    s1 = flat * r1
    cosine, sine = rope_tables(length)
    dy = cotangent.reshape(tokens, width)
    if line:
        turn = jnp.concatenate(
            [cosine, cosine, cosine, cosine, -sine, sine, -sine, sine], axis=-1
        )[:, 0]
        summed, s1_all, dy_all, w_qkv, w_o, q2, k2, kz, vz, totals, attended = attention_front(
            s1.astype(bf16), packed_qkv, w_o_piece, dy, turn, heads
        )
    else:
        w_qkv = gather_dp(exchange_seq(packed_qkv).reshape(S * rows, q_cols + 2 * HEAD))
        w_o = gather_dp(w_o_piece)
        s1_all = gather_seq(s1.astype(bf16))
        qkv = mm(s1_all, w_qkv)
        queries = rotate(qkv[:, :q_cols].reshape(length, heads, HEAD), cosine, sine).astype(bf16)
        queries = jnp.transpose(queries, (1, 0, 2))
        keys = rotate(qkv[:, None, q_cols : q_cols + HEAD], cosine, sine).astype(bf16)[:, 0]
        values = qkv[:, q_cols + HEAD :].astype(bf16)
        attended, totals = attention_forward(queries, keys, values, block_rows)
        attended = heads_last(attended)
        summed = scatter_seq(mm(attended, w_o).astype(bf16))
        dy_all = gather_seq(dy)
    middle = flat + summed
    r2 = rms_scale(middle)
    s2 = middle * r2
    if line:
        out_part, e2, g_gu, down_grad = feedforward(
            s2.astype(bf16), dy_all, w_gu, w_d, down_rows
        )
    else:
        out_part, e2, g_gu, down_grad = feedforward_plain(s2.astype(bf16), dy_all, w_gu, w_d)

    g_gu = exchange_seq(g_gu.reshape(S, rows, 2 * width_f))
    d_middle = dy.astype(f32) + r2 * (e2 - s2 * jnp.mean(e2 * s2, axis=-1, keepdims=True))
    if line:
        table = jnp.concatenate([cosine, cosine, sine, -sine], axis=-1)[:, 0] * HEAD ** (-0.5)

        def with_zeros(u):
            return jnp.concatenate([u, jnp.zeros_like(u)], axis=-1)

        w_o2 = with_zeros(w_o.reshape(heads, 1, HEAD, width).swapaxes(2, 3)).swapaxes(2, 3)
        e1, g_qkv, g_o = attention_back(
            d_middle.astype(bf16),
            q2,
            k2,
            kz,
            vz,
            totals,
            attended,
            s1_all,
            w_qkv,
            w_o2.reshape(2 * q_cols, width),
            table,
            rows,
        )
        g_o = g_o.astype(bf16)
    else:
        dm_all = gather_seq(d_middle.astype(bf16))
        d_att = heads_first(mm_nt(dm_all, w_o).astype(bf16), heads)
        d_q, d_k, d_v = attention_backward(queries, keys, values, d_att, totals, block_rows)
        d_q = jnp.transpose(d_q, (1, 0, 2))
        d_qkv = jnp.concatenate(
            [
                rotate(d_q, cosine, -sine).reshape(length, q_cols).astype(bf16),
                rotate(d_k[:, None], cosine, -sine)[:, 0].astype(bf16),
                d_v.astype(bf16),
            ],
            axis=1,
        )
        e1 = scatter_seq(mm_nt(d_qkv, w_qkv).astype(bf16))
        g_o = scatter_dp(mm_tn(attended, dm_all).astype(bf16))
        g_qkv = scatter_dp(mm_tn(s1_all, d_qkv).astype(bf16))
        g_qkv = exchange_seq(g_qkv.reshape(S, rows, q_cols + 2 * HEAD))
    output = (middle + scatter_seq(out_part)).astype(bf16)
    input_grad = d_middle + r1 * (e1 - s1 * jnp.mean(e1 * s1, axis=-1, keepdims=True))
    output_grad = lax.ppermute(g_o, ("dp", "seq"), backward_perm).astype(f32)

    if line:
        g_gate, g_up, g_query, g_key, g_value, gain_one_grad, gain_two_grad = spread(
            g_gu,
            g_qkv,
            (gate_weight, up_weight, query_weight, key_weight, value_weight),
            (gain_one, gain_two),
            down_rows,
            repeats,
        )
        return (
            output.reshape(sequences, tokens, width),
            input_grad.reshape(sequences, tokens, width),
            gain_one_grad[:, 0],
            g_query,
            g_key,
            g_value,
            output_grad,
            gain_two_grad[:, 0],
            g_gate,
            g_up,
            down_grad,
        )

    g_gu, g_qkv = g_gu.astype(f32), g_qkv.astype(f32)

    def back_hidden(part):
        return jnp.transpose(part.reshape(S, rows, Dp, down_rows), (1, 2, 0, 3)).reshape(rows, -1)

    def back_kv(part):
        part = jnp.sum(part.reshape(KV, repeats, rows, HEAD), axis=1)
        return jnp.transpose(part, (1, 0, 2)).reshape(rows, KV * HEAD)

    g_gate, g_up = back_hidden(g_gu[..., :hidden]), back_hidden(g_gu[..., hidden:])
    g_query = jnp.transpose(g_qkv[..., :q_cols], (1, 0, 2)).reshape(rows, width)
    g_key = back_kv(g_qkv[..., q_cols : q_cols + HEAD])
    g_value = back_kv(g_qkv[..., q_cols + HEAD :])

    def row_dot(weight, grad):
        return jnp.sum(weight.astype(f32) * grad, axis=1)

    gain_two_grad = row_dot(gate_weight, g_gate) + row_dot(up_weight, g_up)
    gain_one_grad = (
        row_dot(query_weight, g_query) + row_dot(key_weight, g_key) + row_dot(value_weight, g_value)
    )
    return (
        output.reshape(sequences, tokens, width),
        input_grad.reshape(sequences, tokens, width),
        gain_one_grad,
        g_query * gain_one,
        g_key * gain_one,
        g_value * gain_one,
        output_grad,
        gain_two_grad,
        g_gate * gain_two,
        g_up * gain_two,
        down_grad,
    )


def solution(mesh):
    both = ("dp", "seq")
    tok, vec, mat = P("dp", "seq", None), P(both), P(both, None)
    in_specs = (tok, vec, mat, mat, mat, mat, vec, mat, mat, mat, tok)
    out_specs = (tok, tok, vec, mat, mat, mat, mat, vec, mat, mat, mat)
    return jax.shard_map(shards, mesh=mesh, in_specs=in_specs, out_specs=out_specs, check_vma=False)
```

```python
import functools

import jax
import jax.numpy as jnp
from jax import lax
from jax.experimental import pallas as pl
from jax.experimental.pallas import tpu as pltpu
from jax.sharding import PartitionSpec as P

H = 32
KV = 4
HEAD = 64

epsilon = 1e-05
masked = -1e30
f32 = jnp.float32
bf16 = jnp.bfloat16


def rope_tables(length):
    half_width = HEAD // 2
    frequency = 10000.0 ** (-(jnp.arange(half_width, dtype=f32) * 2.0) / HEAD)
    angles = jnp.arange(length, dtype=f32)[:, None] * frequency[None, :]
    return (jnp.cos(angles)[:, None, :], jnp.sin(angles)[:, None, :])


def rotate(values, cosine, sine):
    front, back = values[..., : HEAD // 2], values[..., HEAD // 2 :]
    return jnp.concatenate([front * cosine - back * sine, back * cosine + front * sine], axis=-1)


def rms_scale(values):
    return lax.rsqrt(jnp.mean(values * values, axis=-1, keepdims=True) + epsilon)


def mm(a, b):
    return lax.dot_general(a, b, (((1,), (0,)), ((), ())), preferred_element_type=f32)


def mm_nt(a, b):
    return lax.dot_general(a, b, (((1,), (1,)), ((), ())), preferred_element_type=f32)


def mm_tn(a, b):
    return lax.dot_general(a, b, (((0,), (0,)), ((), ())), preferred_element_type=f32)


def seq_place():
    me = lax.axis_index("seq")
    return me // 2, me % 2

def hello(barrier, peer, axis):
    pl.semaphore_signal(
        barrier, inc=1, device_id={axis: peer}, device_id_type=pl.DeviceIdType.MESH
    )


def greet(z, y, Z, dp=None):
    barrier = pltpu.get_barrier_semaphore()
    hello(barrier, z * 2 + 1 - y, "seq")

    @pl.when(z > 0)
    def _():
        hello(barrier, z * 2 + y - 2, "seq")

    @pl.when(z < Z - 1)
    def _():
        hello(barrier, z * 2 + y + 2, "seq")

    count = 1 + (z + Z - 1) // Z + (2 * Z - 2 - z) // Z
    if dp is not None:
        hello(barrier, dp + 1 - 2 * (dp % 2), "dp")
        hello(barrier, dp + 2 - 4 * (dp // 2), "dp")
        count = count + 2
    pl.semaphore_wait(barrier, count)


def send(src, dst, ssem, rsem, peer, axis="seq"):
    return pltpu.make_async_remote_copy(
        src_ref=src,
        dst_ref=dst,
        send_sem=ssem,
        recv_sem=rsem,
        device_id={axis: peer},
        device_id_type=pl.DeviceIdType.MESH,
    )


def gather_kernel(Z, T, x_ref, out_ref, up_sem, dn_sem, y_sem, recv_sem, own_sem):
    z, y = seq_place()
    greet(z, y, Z)
    def block(zz, yy):
        return out_ref.at[pl.ds(pl.multiple_of((zz * 2 + yy) * T, T), T)]
    def copy(src, zz, sem, peer):
        return send(src, block(zz, y), sem.at[zz], recv_sem.at[zz * 2 + y], peer)
    own = pltpu.make_async_copy(x_ref, block(z, y), own_sem)
    own.start()
    peer_y, peer_up, peer_dn = z * 2 + 1 - y, z * 2 + y + 2, z * 2 + y - 2
    copy(x_ref, z, y_sem, peer_y).start()
    @pl.when(z < Z - 1)
    def _(): copy(x_ref, z, up_sem, peer_up).start()
    @pl.when(z > 0)
    def _(): copy(x_ref, z, dn_sem, peer_dn).start()
    for h in range(1, Z):
        @pl.when(z >= h)
        def _():
            zz = z - h
            copy(block(zz, y), zz, y_sem, peer_y).wait_recv()
            @pl.when(z < Z - 1)
            def _(): copy(block(zz, y), zz, up_sem, peer_up).start()
            copy(block(zz, y), zz, y_sem, peer_y).start()
        @pl.when(z + h < Z)
        def _():
            zz = z + h
            copy(block(zz, y), zz, y_sem, peer_y).wait_recv()
            @pl.when(z > 0)
            def _(): copy(block(zz, y), zz, dn_sem, peer_dn).start()
            copy(block(zz, y), zz, y_sem, peer_y).start()
    own.wait()
    for zz in range(Z):
        b = block(zz, 1 - y)
        send(b, b, y_sem.at[zz], recv_sem.at[zz * 2 + 1 - y], peer_y).wait_recv()
        c = copy(block(zz, y), zz, y_sem, peer_y)
        c.wait_send()
        @pl.when((zz <= z) & (z < Z - 1))
        def _(): copy(block(zz, y), zz, up_sem, peer_up).wait_send()
        @pl.when((zz >= z) & (z > 0))
        def _(): copy(block(zz, y), zz, dn_sem, peer_dn).wait_send()

def gather_line(x, cid=1):
    S = lax.axis_size("seq"); Z = S // 2
    T, D = x.shape
    return pl.pallas_call(
        functools.partial(gather_kernel, Z, T),
        out_shape=jax.ShapeDtypeStruct((S * T, D), x.dtype),
        in_specs=[pl.BlockSpec(memory_space=pltpu.VMEM)],
        out_specs=pl.BlockSpec(memory_space=pl.ANY),
        scratch_shapes=[pltpu.SemaphoreType.DMA((Z,))] * 3 + [pltpu.SemaphoreType.DMA((S,)), pltpu.SemaphoreType.DMA],
        compiler_params=pltpu.CompilerParams(collective_id=cid, has_side_effects=True),
        name="gather_seq",
    )(x)

def scatter_kernel(Z, T, p_ref, out_ref, ybuf, upbuf, dnbuf, upst, dnst, up_s, dn_s, y_s, up_r, dn_r, y_r):
    z, y = seq_place()
    greet(z, y, Z)
    peer_y, peer_up, peer_dn = z * 2 + 1 - y, z * 2 + y + 2, z * 2 + y - 2
    def mine(zz, yy):
        return p_ref.at[pl.ds(pl.multiple_of((zz * 2 + yy) * T, T), T)]
    def y_copy(zz):
        return send(mine(zz, 1 - y), ybuf.at[zz], y_s.at[zz], y_r.at[zz], peer_y)
    def up_copy(zz):
        return send(upst.at[zz], upbuf.at[zz], up_s.at[zz], up_r.at[zz], peer_up)
    def dn_copy(zz):
        return send(dnst.at[zz], dnbuf.at[zz], dn_s.at[zz], dn_r.at[zz], peer_dn)
    for h in range(Z - 1, 0, -1):
        @pl.when(z + h < Z)
        def _(): y_copy(z + h).start()
        @pl.when(z - h >= 0)
        def _(): y_copy(z - h).start()
    y_copy(z).start()
    for h in range(Z - 1, 0, -1):
        @pl.when(z + h < Z)
        def _():
            d = z + h
            y_copy(d).wait_recv()
            upst[d] = (mine(d, y)[...].astype(f32) + ybuf[d].astype(f32)).astype(bf16)
            @pl.when(z > 0)
            def _():
                up_copy(d).wait_recv()
                upst[d] = (mine(d, y)[...].astype(f32) + ybuf[d].astype(f32) + upbuf[d].astype(f32)).astype(bf16)
            up_copy(d).start()
        @pl.when(z - h >= 0)
        def _():
            d = z - h
            y_copy(d).wait_recv()
            dnst[d] = (mine(d, y)[...].astype(f32) + ybuf[d].astype(f32)).astype(bf16)
            @pl.when(z < Z - 1)
            def _():
                dn_copy(d).wait_recv()
                dnst[d] = (mine(d, y)[...].astype(f32) + ybuf[d].astype(f32) + dnbuf[d].astype(f32)).astype(bf16)
            dn_copy(d).start()
    y_copy(z).wait_recv()
    out_ref[...] = mine(z, y)[...].astype(f32) + ybuf[z].astype(f32)
    @pl.when(z > 0)
    def _():
        up_copy(z).wait_recv()
        out_ref[...] += upbuf[z].astype(f32)
    @pl.when(z < Z - 1)
    def _():
        dn_copy(z).wait_recv()
        out_ref[...] += dnbuf[z].astype(f32)
    for zz in range(Z):
        y_copy(zz).wait_send()
        @pl.when(zz > z)
        def _(): up_copy(zz).wait_send()
        @pl.when(zz < z)
        def _(): dn_copy(zz).wait_send()

def scatter_line(p, cid=2):
    S = lax.axis_size("seq"); Z = S // 2
    L, D = p.shape; T = L // S
    return pl.pallas_call(
        functools.partial(scatter_kernel, Z, T),
        out_shape=jax.ShapeDtypeStruct((T, D), f32),
        in_specs=[pl.BlockSpec(memory_space=pltpu.VMEM)],
        out_specs=pl.BlockSpec(memory_space=pltpu.VMEM),
        scratch_shapes=[pltpu.VMEM((Z, T, D), bf16)] * 5 + [pltpu.SemaphoreType.DMA((Z,))] * 6,
        compiler_params=pltpu.CompilerParams(collective_id=cid, has_side_effects=True, vmem_limit_bytes=60 << 20),
        name="scatter_seq",
    )(p)


def line_rank(i, z):
    upper = z // 2
    inner = (z + upper) % 2
    base = i + inner * (1 - i // 2) * (1 - 2 * i)
    return base + upper * (3 - 2 * base)


def above(d, z):
    return (d - z + 3) // 4


def rows_of(ref, start, size):
    return ref.at[pl.ds(pl.multiple_of(start, size), size)]


def in_chunks(rows, chunk, step):
    def body(i, carry):
        step(pl.ds(pl.multiple_of(i * chunk, chunk), chunk))
        return carry

    lax.fori_loop(0, rows // chunk, body, 0)


class Gather:
    def __init__(self, z, y, T, own, full, up_sem, dn_sem, y_sem, recv_sem, own_sem):
        self.z, self.y, self.T, self.own, self.full = z, y, T, own, full
        self.sems = {"up": up_sem, "dn": dn_sem, "y": y_sem}
        self.peers = {"up": z * 2 + y + 2, "dn": z * 2 + y - 2, "y": z * 2 + 1 - y}
        self.recv_sem, self.own_sem = recv_sem, own_sem

    def block(self, zz, yy):
        return rows_of(self.full, (zz * 2 + yy) * self.T, self.T)

    def copy(self, src, zz, way):
        return send(
            src,
            self.block(zz, self.y),
            self.sems[way].at[zz],
            self.recv_sem.at[zz * 2 + self.y],
            self.peers[way],
        )

    def start(self):
        z = self.z
        pltpu.make_async_copy(self.own, self.block(z, self.y), self.own_sem).start()
        self.copy(self.own, z, "y").start()

        @pl.when(z < 3)
        def _():
            self.copy(self.own, z, "up").start()

        @pl.when(z > 0)
        def _():
            self.copy(self.own, z, "dn").start()

    def own_ready(self):
        pltpu.make_async_copy(self.own, self.block(self.z, self.y), self.own_sem).wait()

    def hop(self, h):
        z = self.z

        @pl.when(z >= h)
        def _():
            src = self.block(z - h, self.y)
            self.copy(src, z - h, "y").wait_recv()

            @pl.when(z < 3)
            def _():
                self.copy(src, z - h, "up").start()

            self.copy(src, z - h, "y").start()

        @pl.when(z + h < 4)
        def _():
            src = self.block(z + h, self.y)
            self.copy(src, z + h, "y").wait_recv()

            @pl.when(z > 0)
            def _():
                self.copy(src, z + h, "dn").start()

            self.copy(src, z + h, "y").start()

    def pair_ready(self, zz):
        b = self.block(zz, 1 - self.y)
        send(
            b, b, self.sems["y"].at[zz], self.recv_sem.at[zz * 2 + 1 - self.y], self.peers["y"]
        ).wait_recv()

    def finish_one(self, zz):
        z = self.z
        src = self.block(zz, self.y)
        self.copy(src, zz, "y").wait_send()

        @pl.when((zz <= z) & (z < 3))
        def _():
            self.copy(src, zz, "up").wait_send()

        @pl.when((zz >= z) & (z > 0))
        def _():
            self.copy(src, zz, "dn").wait_send()

    def finish(self):
        for zz in range(4):
            self.finish_one(zz)


class Scatter:
    def __init__(self, z, y, T, part, ybuf, rbuf, y_s, y_r, z_s, z_r):
        self.z, self.y, self.T, self.part = z, y, T, part
        self.ybuf, self.rbuf = ybuf, rbuf
        self.y_s, self.y_r, self.z_s, self.z_r = y_s, y_r, z_s, z_r

    def rows(self, zz, yy):
        return rows_of(self.part, (zz * 2 + yy) * self.T, self.T)

    def y_copy(self, d):
        peer = self.z * 2 + 1 - self.y
        return send(
            self.rows(d, 1 - self.y), self.ybuf.at[d], self.y_s.at[d], self.y_r.at[d], peer
        )

    def z_copy(self, d, up):
        slot = d + up
        peer = self.z * 2 + self.y + 4 * up - 2
        return send(self.ybuf.at[d], self.rbuf.at[slot], self.z_s.at[d], self.z_r.at[slot], peer)

    def start(self, d):
        self.y_copy(d).start()

    def pass_on(self, d):
        z = self.z
        up = above(d, z)
        self.y_copy(d).wait_recv()
        mine, slot = self.rows(d, self.y), self.ybuf.at[d]
        inner = (z > 0) & (z < 3)

        @pl.when(inner)
        def _():
            self.z_copy(d, up).wait_recv()
            far = self.rbuf.at[d + up]

            def step(c):
                slot[c] = (
                    mine[c].astype(f32) + slot[c].astype(f32) + far[c].astype(f32)
                ).astype(bf16)

            in_chunks(self.T, 32, step)

        @pl.when(jnp.logical_not(inner))
        def _():
            def step(c):
                slot[c] = (mine[c].astype(f32) + slot[c].astype(f32)).astype(bf16)

            in_chunks(self.T, 32, step)

        self.z_copy(d, up).start()

    def finish(self, out_ref):
        z = self.z
        self.y_copy(z).wait_recv()
        mine, slot = self.rows(z, self.y), self.ybuf.at[z]

        def first(c):
            out_ref[c] = mine[c].astype(f32) + slot[c].astype(f32)

        in_chunks(self.T, 32, first)

        def more(slot):
            def step(c):
                out_ref[c] += slot[c].astype(f32)

            in_chunks(self.T, 32, step)

        @pl.when(z > 0)
        def _():
            self.z_copy(z, 1).wait_recv()
            more(self.rbuf.at[z + 1])

        @pl.when(z < 3)
        def _():
            self.z_copy(z, 0).wait_recv()
            more(self.rbuf.at[z])

        for d in range(4):
            self.y_copy(d).wait_send()

            @pl.when(z != d)
            def _():
                self.z_copy(d, above(d, z)).wait_send()


def line_sems(n):
    return [pltpu.SemaphoreType.DMA((4,))] * 3 + [
        pltpu.SemaphoreType.DMA((8,)),
        pltpu.SemaphoreType.DMA,
    ]


def sum_scratch(T, width):
    return [
        pltpu.VMEM((4, T, width), bf16),
        pltpu.VMEM((5, T, width), bf16),
        pltpu.SemaphoreType.DMA((4,)),
        pltpu.SemaphoreType.DMA((4,)),
        pltpu.SemaphoreType.DMA((4,)),
        pltpu.SemaphoreType.DMA((5,)),
    ]


class DpSum:
    def __init__(self, src, size, abuf, bbuf, a_s, a_r, b_s, b_r):
        dp = lax.axis_index("dp")
        self.core, self.far = dp % 2, dp // 2
        self.partner, self.across = dp + 1 - 2 * (dp % 2), dp + 2 - 4 * (dp // 2)
        self.src, self.size = src, size
        self.abuf, self.bbuf = abuf, bbuf
        self.a_s, self.a_r, self.b_s, self.b_r = a_s, a_r, b_s, b_r

    def rows(self, d):
        return rows_of(self.src, d * self.size, self.size)

    def a_copy(self, j):
        return send(
            self.rows(2 * j + 1 - self.core),
            self.abuf.at[j],
            self.a_s.at[j],
            self.a_r.at[j],
            self.partner,
            "dp",
        )

    def b_copy(self):
        return send(self.abuf.at[1 - self.far], self.bbuf, self.b_s, self.b_r, self.across, "dp")

    def start(self):
        self.a_copy(0).start()
        self.a_copy(1).start()

    def middle(self):
        self.a_copy(0).wait_recv()
        self.a_copy(1).wait_recv()
        j = 1 - self.far
        mine, slot = self.rows(2 * j + self.core), self.abuf.at[j]

        def step(c):
            slot[c] = (mine[c].astype(f32) + slot[c].astype(f32)).astype(bf16)

        in_chunks(self.size, 16, step)
        self.b_copy().start()

    def finish(self, out_ref):
        self.b_copy().wait_recv()
        mine, slot = self.rows(2 * self.far + self.core), self.abuf.at[self.far]

        def step(c):
            out_ref[c] = (
                mine[c].astype(f32) + slot[c].astype(f32) + self.bbuf[c].astype(f32)
            ).astype(out_ref.dtype)

        in_chunks(self.size, 16, step)
        self.a_copy(0).wait_send()
        self.a_copy(1).wait_send()
        self.b_copy().wait_send()


class Exchange:
    def __init__(self, me, src, landing, s_sem, r_sem, own_sem):
        self.me, self.src, self.landing = me, src, landing
        self.s_sem, self.r_sem, self.own_sem = s_sem, r_sem, own_sem

    def own(self):
        return pltpu.make_async_copy(self.src(self.me), self.landing(self.me), self.own_sem)

    def copy(self, peer, sender):
        return send(
            self.src(peer), self.landing(sender), self.s_sem.at[peer], self.r_sem.at[sender], peer
        )

    def start(self, *steps):
        for step in steps:
            self.copy((self.me + step) % 8, self.me).start()

    def ready(self):
        self.own().wait()
        for step in range(1, 8):
            peer = (self.me + step) % 8
            self.copy(peer, peer).wait_recv()

    def finish(self):
        for step in range(1, 8):
            self.copy((self.me + step) % 8, self.me).wait_send()


class DpGather:
    def __init__(self, own, full, size, s_sem, r_sem):
        dp = lax.axis_index("dp")
        self.dp, self.partner, self.across = dp, dp + 1 - 2 * (dp % 2), dp + 2 - 4 * (dp // 2)
        self.diagonal = 3 - dp
        self.own, self.full, self.size = own, full, size
        self.s_sem, self.r_sem = s_sem, r_sem

    def block(self, d):
        return rows_of(self.full, d * self.size, self.size)

    def copy(self, src, d, k, peer):
        return send(src, self.block(d), self.s_sem.at[k], self.r_sem.at[k], peer, "dp")

    def start(self):
        self.copy(self.own, self.dp, 0, self.across).start()
        self.copy(self.own, self.dp, 1, self.partner).start()

    def relay(self):
        far = self.block(self.across)
        self.copy(far, self.across, 0, self.across).wait_recv()
        self.copy(far, self.across, 2, self.partner).start()

    def ready(self):
        near, diagonal = self.block(self.partner), self.block(self.diagonal)
        self.copy(near, self.partner, 1, self.partner).wait_recv()
        self.copy(diagonal, self.diagonal, 2, self.partner).wait_recv()

    def finish(self):
        self.copy(self.own, self.dp, 0, self.across).wait_send()
        self.copy(self.own, self.dp, 1, self.partner).wait_send()
        self.copy(self.block(self.across), self.across, 2, self.partner).wait_send()


def dp_scratch(size, width):
    return [
        pltpu.VMEM((2, size, width), bf16),
        pltpu.VMEM((size, width), bf16),
        pltpu.SemaphoreType.DMA((2,)),
        pltpu.SemaphoreType.DMA((2,)),
        pltpu.SemaphoreType.DMA,
        pltpu.SemaphoreType.DMA,
    ]


def feedforward_kernel(
    T, x_ref, dy_ref, wgu_ref, wd_ref, out_ref, e2_ref, ggu_ref, gd_ref,
    full, hid, dgu, pout, part, ggu, gdown, up_sem, dn_sem, ag_y, ag_r, own_sem,
    pybuf, prbuf, py_s, py_r, pz_s, pz_r,
    ybuf, rbuf, y_s, y_r, z_s, z_r,
    ga, gb, ga_s, ga_r, gb_s, gb_r,
    da, db, da_s, da_r, db_s, db_r,
):
    z, y = seq_place()
    dp = lax.axis_index("dp")
    F = hid.shape[1]
    greet(z, y, 4, dp)
    gather = Gather(z, y, T, x_ref, full, up_sem, dn_sem, ag_y, ag_r, own_sem)
    scatter_out = Scatter(z, y, T, pout, pybuf, prbuf, py_s, py_r, pz_s, pz_r)
    scatter = Scatter(z, y, T, part, ybuf, rbuf, y_s, y_r, z_s, z_r)
    sum_gu = DpSum(ggu, ggu.shape[0] // 4, ga, gb, ga_s, ga_r, gb_s, gb_r)
    sum_down = DpSum(gdown, gd_ref.shape[0], da, db, da_s, da_r, db_s, db_r)
    gather.start()
    gather.own_ready()
    inner = (z > 0) & (z < 3)
    at_end = jnp.logical_not(inner)

    def pass_on(rank):
        scatter_out.pass_on(line_rank(rank, z))
        scatter.pass_on(line_rank(rank, z))

    def compute(i, carry):
        for h in range(1, 4):

            @pl.when(i == h - 1)
            def _():
                gather.hop(h)

        zz = line_rank(i, z)
        gather.pair_ready(zz)

        @pl.when(i == 2)
        def _():
            scatter_out.start(line_rank(1, z))

        @pl.when(i == 3)
        def _():
            scatter_out.start(line_rank(2, z))
            scatter.start(line_rank(2, z))

        @pl.when((i == 3) & at_end)
        def _():
            scatter_out.pass_on(line_rank(1, z))

        r = pl.ds(pl.multiple_of(zz * 2 * T, 2 * T), 2 * T)
        gu = mm(full[r, :], wgu_ref[...])
        gate, up = gu[:, :F], gu[:, F:]
        sig = 1.0 / (1.0 + jnp.exp(-gate))
        act = gate * sig
        hid[r, :] = (act * up).astype(bf16)
        dh = mm_nt(dy_ref[r, :], wd_ref[...])
        dgu[r, :F] = (dh * up * sig * (1.0 + gate * (1.0 - sig))).astype(bf16)
        dgu[r, F:] = (dh * act).astype(bf16)
        pout[r, :] = mm(hid[r, :], wd_ref[...]).astype(bf16)

        @pl.when(i == 3)
        def _():
            scatter_out.start(zz)

        part[r, :] = mm_nt(dgu[r, :], wgu_ref[...]).astype(bf16)
        return carry

    lax.fori_loop(0, 4, compute, 0)
    scatter.start(line_rank(3, z))
    scatter.start(line_rank(1, z))
    scatter_out.start(z)
    scatter.start(z)

    def gate_up_tile(i, carry):
        @pl.when((i == 4) & at_end)
        def _():
            pass_on(2)

        r = pl.ds(pl.multiple_of(i * 256, 256), 256)
        ggu[r, :] = mm_tn(full[:, r], dgu[...]).astype(bf16)
        return carry

    def down_tile(i, carry):
        r = pl.ds(pl.multiple_of(i * 256, 256), 256)
        gdown[r, :] = mm_tn(hid[:, r], dy_ref[...]).astype(bf16)
        return carry

    lax.fori_loop(0, 8, gate_up_tile, 0)
    sum_gu.start()
    pass_on(3 - (z + 1) % 4 // 2)
    lax.fori_loop(0, F // 256, down_tile, 0)
    sum_down.start()

    @pl.when(inner)
    def _():
        pass_on(3)

    sum_gu.middle()

    @pl.when(inner)
    def _():
        scatter_out.pass_on(line_rank(1, z))

    scatter.pass_on(line_rank(1, z))
    sum_down.middle()
    sum_gu.finish(ggu_ref)
    sum_down.finish(gd_ref)
    scatter_out.finish(out_ref)
    scatter.finish(e2_ref)
    gather.finish()


def feedforward(x, dy_all, w_gu, w_d, down_rows, cid=3):
    T, width = x.shape
    L, F = dy_all.shape[0], w_d.shape[0]
    vmem = pl.BlockSpec(memory_space=pltpu.VMEM)
    return pl.pallas_call(
        functools.partial(feedforward_kernel, T),
        out_shape=(
            jax.ShapeDtypeStruct((T, width), f32),
            jax.ShapeDtypeStruct((T, width), f32),
            jax.ShapeDtypeStruct((width // 4, 2 * F), bf16),
            jax.ShapeDtypeStruct((down_rows, width), f32),
        ),
        in_specs=[vmem] * 4,
        out_specs=(vmem,) * 4,
        scratch_shapes=[
            pltpu.VMEM((L, width), bf16),
            pltpu.VMEM((L, F), bf16),
            pltpu.VMEM((L, 2 * F), bf16),
            pltpu.VMEM((L, width), bf16),
            pltpu.VMEM((L, width), bf16),
            pltpu.VMEM((width, 2 * F), bf16),
            pltpu.VMEM((F, width), bf16),
        ]
        + line_sems(4)
        + sum_scratch(T, width)
        + sum_scratch(T, width)
        + dp_scratch(width // 4, 2 * F)
        + dp_scratch(down_rows, width),
        compiler_params=pltpu.CompilerParams(
            collective_id=cid, has_side_effects=True, vmem_limit_bytes=67000000
        ),
        name="feedforward",
    )(x, dy_all, w_gu, w_d)


def attention_front_kernel(
    T, heads, s1_ref, piece_ref, gu_ref, wo_piece_ref, dy_ref, table_ref,
    mid_ref, s1_all, dy_all, wqkv, wgu, wo, q_out, k2_ref, kz_ref, vz_ref, lse_ref, att_ref,
    score, part,
    up_sem, dn_sem, ag_y, ag_r, own_sem,
    up_sem2, dn_sem2, ag_y2, ag_r2, own_sem2,
    ybuf, rbuf, y_s, y_r, z_s, z_r,
    w_s, w_r, o_s, o_r, g_s, g_r, ex_s, ex_r, gx_s, gx_r, ex_own, gx_own, wo_own,
):
    z, y = seq_place()
    me = z * 2 + y
    dp = lax.axis_index("dp")
    rows, out_rows = piece_ref.shape[1], wo_piece_ref.shape[0]
    barrier = pltpu.get_barrier_semaphore()
    for step in range(1, 8):
        hello(barrier, (me + step) % 8, "seq")
    hello(barrier, dp + 1 - 2 * (dp % 2), "dp")
    hello(barrier, dp + 2 - 4 * (dp // 2), "dp")
    pl.semaphore_wait(barrier, 9)
    gather = Gather(z, y, T, s1_ref, s1_all, up_sem, dn_sem, ag_y, ag_r, own_sem)
    gather_dy = Gather(z, y, T, dy_ref, dy_all, up_sem2, dn_sem2, ag_y2, ag_r2, own_sem2)
    scatter = Scatter(z, y, T, part, ybuf, rbuf, y_s, y_r, z_s, z_r)
    w_own = rows_of(wqkv, dp * 8 * rows, 8 * rows)
    w_all = DpGather(w_own, wqkv, 8 * rows, w_s, w_r)
    o_all = DpGather(wo_piece_ref, wo, out_rows, o_s, o_r)

    g_own = rows_of(wgu, dp * 8 * rows, 8 * rows)
    g_all = DpGather(g_own, wgu, 8 * rows, g_s, g_r)

    def pieces(src, full, *sems):
        return Exchange(
            me, lambda p: src.at[p], lambda p: rows_of(full, (dp * 8 + p) * rows, rows), *sems
        )

    exchange = pieces(piece_ref, wqkv, ex_s, ex_r, ex_own)
    exchange_gu = pieces(gu_ref, wgu, gx_s, gx_r, gx_own)
    exchange.own().start()
    exchange_gu.own().start()
    own_o = pltpu.make_async_copy(wo_piece_ref, o_all.block(dp), wo_own)
    own_o.start()
    exchange.start(*range(1, 8))
    gather.start()
    o_all.start()
    own_o.wait()
    exchange.ready()
    w_all.start()
    gather.own_ready()
    gather.hop(1)
    o_all.relay()
    w_all.relay()
    w_all.ready()
    U = 2 * T
    lane = lax.broadcasted_iota(jnp.int32, (U, 128), 1)
    low_lanes = lane < HEAD
    front = lane % HEAD < HEAD // 2
    scale = HEAD ** (-0.5)

    def swapped(u):
        return jnp.where(front, pltpu.roll(u, 128 - HEAD // 2, 1), pltpu.roll(u, HEAD // 2, 1))

    def project(i, carry):
        for h in (2, 3):

            @pl.when(i == h - 1)
            def _():
                gather.hop(h)

        @pl.when(i == 2)
        def _():
            gather_dy.start()
            exchange_gu.start(1, 2)

        u = line_rank(i, z)
        gather.pair_ready(u)
        r = pl.ds(pl.multiple_of(u * U, U), U)
        qkv = mm(s1_all[r, :], wqkv[...])
        cos, sin = table_ref[r, :128], table_ref[r, 128:]

        def roped(tile):
            return tile * cos + swapped(tile) * sin

        for h in range(0, heads, 2):
            turned = roped(qkv[:, h * HEAD : (h + 2) * HEAD])
            other = swapped(turned)
            q_out[h, r, :] = jnp.where(low_lanes, turned, pltpu.roll(other, HEAD, 1)).astype(bf16)
            q_out[h + 1, r, :] = jnp.where(low_lanes, pltpu.roll(turned, HEAD, 1), other).astype(bf16)
        tile = qkv[:, heads * HEAD :]
        turned = roped(tile)
        k2_ref[r, :] = jnp.where(low_lanes, turned, pltpu.roll(swapped(turned), HEAD, 1)).astype(bf16)
        kz_ref[r, :] = jnp.where(low_lanes, turned, 0.0).astype(bf16)
        vz_ref[r, :] = jnp.where(low_lanes, pltpu.roll(tile, HEAD, 1), 0.0).astype(bf16)
        return carry

    lax.fori_loop(0, 4, project, 0)
    o_all.ready()
    gather_dy.own_ready()

    def unit(i, carry):
        for h in range(1, 4):

            @pl.when(i == h)
            def _():
                gather_dy.hop(h)

        for k in range(3):

            @pl.when(i == k)
            def _():
                exchange_gu.start(*range(2 * k + 3, min(2 * k + 5, 8)))

        u = line_rank(3 - i, z)
        r = pl.ds(pl.multiple_of(u * U, U), U)
        q = q_out[:, r, :].reshape(heads * U, 128)

        def scores(j, top):
            c = pl.ds(pl.multiple_of(j * U, U), U)
            s = mm_nt(q, kz_ref[c, :]) * scale
            row = lax.broadcasted_iota(jnp.int32, (heads, U, U), 1).reshape(heads * U, U)
            col = lax.broadcasted_iota(jnp.int32, (heads * U, U), 1)
            s = jnp.where(col + (j - u) * U <= row, s, masked)
            score[j] = s
            return jnp.maximum(top, jnp.max(s, axis=1, keepdims=True))

        top = lax.fori_loop(0, u + 1, scores, jnp.full((heads * U, 1), masked, f32))

        def weigh(j, carry):
            total, out = carry
            c = pl.ds(pl.multiple_of(j * U, U), U)
            p = jnp.exp(score[j] - top)
            return (
                total + jnp.sum(p, axis=1, keepdims=True),
                out + mm(p.astype(bf16), vz_ref[c, :]),
            )

        total, out = lax.fori_loop(
            0,
            u + 1,
            weigh,
            (jnp.zeros((heads * U, 1), f32), jnp.zeros((heads * U, 128), f32)),
        )
        lse_ref[:, r, :] = (top + jnp.log(total)).reshape(heads, U, 1)
        out = out / total
        for h in range(0, heads, 2):
            first, second = out[h * U : (h + 1) * U], out[(h + 1) * U : (h + 2) * U]
            att_ref[r, h * HEAD : (h + 2) * HEAD] = jnp.where(
                low_lanes, first, pltpu.roll(second, HEAD, 1)
            ).astype(bf16)
        part[r, :] = mm(att_ref[r, :], wo[...]).astype(bf16)
        scatter.start(u)
        for k in (1, 2):

            @pl.when(i == k)
            def _():
                scatter.pass_on(line_rank(4 - k, z))

        return carry

    lax.fori_loop(0, 4, unit, 0)
    exchange_gu.ready()
    g_all.start()
    scatter.pass_on(line_rank(1, z))
    scatter.finish(mid_ref)
    g_all.relay()
    for zz in range(4):
        gather.finish_one(zz)
        gather_dy.pair_ready(zz)
        gather_dy.finish_one(zz)
    exchange.finish()
    exchange_gu.finish()
    w_all.finish()
    o_all.finish()
    g_all.ready()
    g_all.finish()


def attention_front(s1, piece, gu_piece, wo_piece, dy, table, heads, cid=5):
    T, width = s1.shape
    S, rows, cols = piece.shape
    L, q_cols, U = S * T, heads * HEAD, 2 * T
    vmem = pl.BlockSpec(memory_space=pltpu.VMEM)
    return pl.pallas_call(
        functools.partial(attention_front_kernel, T, heads),
        out_shape=(
            jax.ShapeDtypeStruct((T, width), f32),
            jax.ShapeDtypeStruct((L, width), bf16),
            jax.ShapeDtypeStruct((L, width), bf16),
            jax.ShapeDtypeStruct((width, cols), bf16),
            jax.ShapeDtypeStruct((width, gu_piece.shape[2]), bf16),
            jax.ShapeDtypeStruct((q_cols, width), bf16),
            jax.ShapeDtypeStruct((heads, L, 128), bf16),
            jax.ShapeDtypeStruct((L, 128), bf16),
            jax.ShapeDtypeStruct((L, 128), bf16),
            jax.ShapeDtypeStruct((L, 128), bf16),
            jax.ShapeDtypeStruct((heads, L, 1), f32),
            jax.ShapeDtypeStruct((L, q_cols), bf16),
        ),
        in_specs=[vmem] * 6,
        out_specs=(vmem,) * 12,
        scratch_shapes=[
            pltpu.VMEM((L // U, heads * U, U), f32),
            pltpu.VMEM((L, width), bf16),
        ]
        + line_sems(4)
        + line_sems(4)
        + sum_scratch(T, width)
        + [pltpu.SemaphoreType.DMA((3,))] * 6
        + [pltpu.SemaphoreType.DMA((8,))] * 4
        + [pltpu.SemaphoreType.DMA] * 3,
        compiler_params=pltpu.CompilerParams(
            collective_id=cid, has_side_effects=True, vmem_limit_bytes=67000000
        ),
        name="attention_front",
    )(s1, piece, gu_piece, wo_piece, dy, table)


def attention_back_kernel(
    T, heads, dm_ref, q_ref, k_ref, kz_ref, vz_ref, lse_ref, att_ref, s1_ref, wqkv_ref, wo_ref, table_ref, ggu_ref,
    e1_ref, got_ref, go_ref, got_gu_ref,
    full, grads, probs, dprobs, dk, dv, dqkv, part, gqkv, go_part, gsum,
    up_sem, dn_sem, ag_y, ag_r, own_sem,
    ybuf, rbuf, y_s, y_r, z_s, z_r,
    qa, qb, qa_s, qa_r, qb_s, qb_r,
    oa, ob, oa_s, oa_r, ob_s, ob_r,
    ex_s, ex_r, gx_s, gx_r, ex_own, gx_own,
):
    z, y = seq_place()
    me = z * 2 + y
    dp = lax.axis_index("dp")
    rows = got_ref.shape[1]
    barrier = pltpu.get_barrier_semaphore()
    for step in range(1, 8):
        hello(barrier, (me + step) % 8, "seq")
    hello(barrier, dp + 1 - 2 * (dp % 2), "dp")
    hello(barrier, dp + 2 - 4 * (dp // 2), "dp")
    pl.semaphore_wait(barrier, 9)
    gather = Gather(z, y, T, dm_ref, full, up_sem, dn_sem, ag_y, ag_r, own_sem)
    scatter = Scatter(z, y, T, part, ybuf, rbuf, y_s, y_r, z_s, z_r)
    sum_qkv = DpSum(gqkv, gqkv.shape[0] // 4, qa, qb, qa_s, qa_r, qb_s, qb_r)
    sum_o = DpSum(go_part, go_part.shape[0] // 4, oa, ob, oa_s, oa_r, ob_s, ob_r)
    exchange = Exchange(
        me, lambda p: rows_of(gsum, p * rows, rows), lambda p: got_ref.at[p], ex_s, ex_r, ex_own
    )
    exchange_gu = Exchange(
        me, lambda p: rows_of(ggu_ref, p * rows, rows), lambda p: got_gu_ref.at[p], gx_s, gx_r, gx_own
    )
    gather.start()
    exchange_gu.own().start()
    dk[...] = jnp.zeros_like(dk)
    dv[...] = jnp.zeros_like(dv)
    gather.own_ready()
    U = 2 * T
    low_lanes = lax.broadcasted_iota(jnp.int32, (U, 128), 1) < HEAD
    scale = HEAD ** (-0.5)

    def both(product, table):
        turned = product * table
        return turned + pltpu.roll(turned, HEAD, 1)

    def unit(i, carry):
        for h in range(1, 4):

            @pl.when(i == h - 1)
            def _():
                gather.hop(h)

        @pl.when(i == 2)
        def _():
            exchange_gu.start(1, 2, 3)

        @pl.when(i == 3)
        def _():
            exchange_gu.start(4, 5, 6, 7)

        u = line_rank(i, z)
        gather.pair_ready(u)
        r = pl.ds(pl.multiple_of(u * U, U), U)
        d_att = mm_nt(full[r, :], wo_ref[...]).astype(bf16)
        for h in range(heads):
            grads[h] = d_att[:, h * 128 : (h + 1) * 128]
        g = grads[...].reshape(heads * U, 128)
        q = q_ref[:, r, :].reshape(heads * U, 128)
        lse = lse_ref[:, r, :].reshape(heads * U, 1)

        def scores(j, inner):
            c = pl.ds(pl.multiple_of(j * U, U), U)
            s = mm_nt(q, kz_ref[c, :]) * scale
            row = lax.broadcasted_iota(jnp.int32, (heads, U, U), 1).reshape(heads * U, U)
            col = lax.broadcasted_iota(jnp.int32, (heads * U, U), 1)
            s = jnp.where(col + (j - u) * U <= row, s, masked)
            p = jnp.exp(s - lse)
            dp_ = mm_nt(g, vz_ref[c, :])
            probs[j] = p
            dprobs[j] = dp_
            return inner + jnp.sum(p * dp_, axis=1, keepdims=True)

        inner = lax.fori_loop(0, u + 1, scores, jnp.zeros((heads * U, 1), f32))

        def products(j, dq):
            c = pl.ds(pl.multiple_of(j * U, U), U)
            p = probs[j]
            ds = (p * (dprobs[j] - inner)).astype(bf16)
            dk[c, :] += mm_tn(ds, q)
            dv[c, :] += mm_tn(p.astype(bf16), g)
            return dq + mm(ds, k_ref[c, :])

        dq = lax.fori_loop(0, u + 1, products, jnp.zeros((heads * U, 128), f32))
        table = table_ref[r, :]
        for h in range(0, heads, 2):
            first = both(dq[h * U : (h + 1) * U], table)
            second = both(dq[(h + 1) * U : (h + 2) * U], table)
            dqkv[r, h * HEAD : (h + 2) * HEAD] = jnp.where(low_lanes, first, second).astype(bf16)
        return carry

    lax.fori_loop(0, 4, unit, 0)

    def part_rows(i):
        u = line_rank(i, z)
        r = pl.ds(pl.multiple_of(u * U, U), U)
        d_key = both(dk[r, :], table_ref[r, :])
        dqkv[r, heads * HEAD :] = jnp.where(low_lanes, d_key, pltpu.roll(dv[r, :], HEAD, 1)).astype(bf16)
        part[r, :] = mm_nt(dqkv[r, :], wqkv_ref[...]).astype(bf16)
        scatter.start(u)

    def part_loop(i, carry):
        part_rows(3 - i)
        return carry

    lax.fori_loop(0, 4, part_loop, 0)

    def qkv_tile(i, carry):
        r = pl.ds(pl.multiple_of(i * 256, 256), 256)
        gqkv[r, :] = mm_tn(s1_ref[:, r], dqkv[...]).astype(bf16)
        return carry

    lax.fori_loop(0, gqkv.shape[0] // 256, qkv_tile, 0)
    sum_qkv.start()
    scatter.pass_on(line_rank(3, z))
    sum_qkv.middle()
    go_part[...] = mm_tn(att_ref[...], full[...]).astype(bf16)
    sum_o.start()
    scatter.pass_on(line_rank(2, z))
    sum_qkv.finish(gsum)

    exchange.own().start()
    exchange.start(*range(1, 8))
    sum_o.middle()
    scatter.pass_on(line_rank(1, z))
    sum_o.finish(go_ref)
    scatter.finish(e1_ref)
    for moved in (exchange, exchange_gu):
        moved.ready()
        moved.finish()
    gather.finish()


def attention_back(dm, q2, k2, kz, vz, lse, attended, s1_all, w_qkv, w_o2, table, g_gu, rows, cid=4):
    T, width = dm.shape
    heads, L, _ = q2.shape
    cols = w_qkv.shape[1]
    vmem = pl.BlockSpec(memory_space=pltpu.VMEM)
    U = 2 * T
    return pl.pallas_call(
        functools.partial(attention_back_kernel, T, heads),
        out_shape=(
            jax.ShapeDtypeStruct((T, width), f32),
            jax.ShapeDtypeStruct((8, rows, cols), bf16),
            jax.ShapeDtypeStruct((rows, width), f32),
            jax.ShapeDtypeStruct((8, rows, g_gu.shape[1]), bf16),
        ),
        in_specs=[vmem] * 12,
        out_specs=(vmem,) * 4,
        scratch_shapes=[
            pltpu.VMEM((L, width), bf16),
            pltpu.VMEM((heads, U, 128), bf16),
            pltpu.VMEM((L // U, heads * U, U), f32),
            pltpu.VMEM((L // U, heads * U, U), f32),
            pltpu.VMEM((L, 128), f32),
            pltpu.VMEM((L, 128), f32),
            pltpu.VMEM((L, cols), bf16),
            pltpu.VMEM((L, width), bf16),
            pltpu.VMEM((width, cols), bf16),
            pltpu.VMEM((heads * HEAD, width), bf16),
            pltpu.VMEM((width // 4, cols), bf16),
        ]
        + line_sems(4)
        + sum_scratch(T, width)
        + dp_scratch(width // 4, cols)
        + dp_scratch(rows, width)
        + [pltpu.SemaphoreType.DMA((8,))] * 4
        + [pltpu.SemaphoreType.DMA] * 2,
        compiler_params=pltpu.CompilerParams(
            collective_id=cid, has_side_effects=True, vmem_limit_bytes=67000000
        ),
        name="attention_back",
    )(dm, q2, k2, kz, vz, lse, attended, s1_all, w_qkv, w_o2, table, g_gu)


def spread_kernel(
    down_rows, repeats, gu_ref, qkv_ref, wg_ref, wu_ref, wq_ref, wk_ref, wv_ref, one_ref, two_ref,
    gate_ref, up_ref, query_ref, key_ref, value_ref, gain1_ref, gain2_ref,
):
    S, rows, wide = gu_ref.shape
    F = wide // 2
    Dp = gate_ref.shape[1] // (S * down_rows)
    q_cols = query_ref.shape[1] // S
    for s in range(S):
        for d in range(Dp):
            to = pl.ds((d * S + s) * down_rows, down_rows)
            gate_ref[:, to] = gu_ref[s, :, d * down_rows : (d + 1) * down_rows].astype(f32)
            up_ref[:, to] = gu_ref[s, :, F + d * down_rows : F + (d + 1) * down_rows].astype(f32)
        query_ref[:, s * q_cols : (s + 1) * q_cols] = qkv_ref[s, :, :q_cols].astype(f32)
    for j in range(S // repeats):
        total = qkv_ref[j * repeats, :, q_cols:].astype(f32)
        for s in range(j * repeats + 1, (j + 1) * repeats):
            total = total + qkv_ref[s, :, q_cols:].astype(f32)
        key_ref[:, j * HEAD : (j + 1) * HEAD] = total[:, :HEAD]
        value_ref[:, j * HEAD : (j + 1) * HEAD] = total[:, HEAD:]

    def close(pairs, gain_ref, out_ref):
        total = jnp.zeros((rows, 1), f32)
        for weight_ref, grad_ref in pairs:
            grad = grad_ref[...]
            total = total + jnp.sum(weight_ref[...].astype(f32) * grad, axis=1, keepdims=True)
            grad_ref[...] = grad * gain_ref[...]
        out_ref[...] = total

    close(((wg_ref, gate_ref), (wu_ref, up_ref)), two_ref, gain2_ref)
    close(((wq_ref, query_ref), (wk_ref, key_ref), (wv_ref, value_ref)), one_ref, gain1_ref)


def spread(gu, qkv, weights, gains, down_rows, repeats):
    rows = gu.shape[1]
    outs = [jax.ShapeDtypeStruct(w.shape, f32) for w in weights]
    outs += [jax.ShapeDtypeStruct((rows, 1), f32)] * 2
    vmem = pl.BlockSpec(memory_space=pltpu.VMEM)
    return pl.pallas_call(
        functools.partial(spread_kernel, down_rows, repeats),
        out_shape=tuple(outs),
        in_specs=[vmem] * 9,
        out_specs=(vmem,) * 7,
        compiler_params=pltpu.CompilerParams(vmem_limit_bytes=40 << 20),
        name="spread",
    )(gu, qkv, *weights, *gains)


def gather_seq(rows):
    if lax.axis_size("seq") == 8:
        return gather_line(rows)
    return lax.all_gather(rows, "seq", axis=0, tiled=True)


def scatter_seq(rows):
    if lax.axis_size("seq") == 8:
        return scatter_line(rows)
    return lax.psum_scatter(rows, "seq", scatter_dimension=0, tiled=True).astype(f32)


def feedforward_plain(x, dy_all, w_gu, w_d):
    hidden = w_d.shape[0]
    s2_all = gather_seq(x)
    gate_up = mm(s2_all, w_gu)
    gate, up = gate_up[:, :hidden], gate_up[:, hidden:]
    sig = jax.nn.sigmoid(gate)
    hid = (gate * sig * up).astype(bf16)
    d_hid = mm_nt(dy_all, w_d)
    d_gate = (d_hid * up * sig * (1.0 + gate * (1.0 - sig))).astype(bf16)
    d_up = (d_hid * (gate * sig)).astype(bf16)
    d_gu = jnp.concatenate([d_gate, d_up], axis=1)
    return (
        scatter_seq(mm(hid, w_d).astype(bf16)),
        scatter_seq(mm_nt(d_gu, w_gu).astype(bf16)),
        scatter_dp(mm_tn(s2_all, d_gu).astype(bf16)),
        scatter_dp(mm_tn(hid, dy_all).astype(bf16)).astype(f32),
    )


def gather_dp(rows):
    return lax.all_gather(rows, "dp", axis=0, tiled=True)


def scatter_dp(rows):
    return lax.psum_scatter(rows, "dp", scatter_dimension=0, tiled=True)


def exchange_seq(pieces):
    return lax.all_to_all(pieces, "seq", split_axis=0, concat_axis=0, tiled=True)


def causal_mask(offset, block_rows, block_end):
    return jnp.arange(block_end)[None, :] <= (offset + jnp.arange(block_rows))[:, None]


def attention_forward(queries, keys, values, block_rows):
    outputs, totals = [], []
    for offset in range(0, queries.shape[1], block_rows):
        end = offset + block_rows
        scores = jnp.einsum(
            "hqd,kd->hqk", queries[:, offset:end], keys[:end], preferred_element_type=f32
        ) * HEAD ** (-0.5)
        scores = jnp.where(causal_mask(offset, block_rows, end), scores, masked)
        row_max = jnp.max(scores, axis=-1, keepdims=True)
        total = row_max + jnp.log(jnp.sum(jnp.exp(scores - row_max), axis=-1, keepdims=True))
        probs_low = jnp.exp(scores - total).astype(bf16)
        outputs.append(
            jnp.einsum("hqk,kd->hqd", probs_low, values[:end], preferred_element_type=f32).astype(
                bf16
            )
        )
        totals.append(total)
    return jnp.concatenate(outputs, axis=1), jnp.concatenate(totals, axis=1)


def attention_backward(queries, keys, values, grads, totals, block_rows):
    length = keys.shape[0]
    scale = HEAD ** (-0.5)
    key_sum = jnp.zeros((length, HEAD), f32)
    value_sum = jnp.zeros((length, HEAD), f32)
    query_parts = []
    for offset in range(0, length, block_rows):
        end = offset + block_rows
        query_block, grad_block = queries[:, offset:end], grads[:, offset:end]
        key_block, value_block = keys[:end], values[:end]
        scores = (
            jnp.einsum("hqd,kd->hqk", query_block, key_block, preferred_element_type=f32) * scale
        )
        scores = jnp.where(causal_mask(offset, block_rows, end), scores, masked)
        probs = jnp.exp(scores - totals[:, offset:end])
        probs_low = probs.astype(bf16)
        grad_probs = jnp.einsum(
            "hqd,kd->hqk", grad_block, value_block, preferred_element_type=f32
        )
        inner = jnp.sum(probs * grad_probs, axis=-1, keepdims=True)
        grad_scores = (probs * (grad_probs - inner)).astype(bf16)
        query_parts.append(
            jnp.einsum("hqk,kd->hqd", grad_scores, key_block, preferred_element_type=f32) * scale
        )
        padding = ((0, length - end), (0, 0))
        key_sum = key_sum + jnp.pad(
            jnp.einsum("hqk,hqd->kd", grad_scores, query_block, preferred_element_type=f32)
            * scale,
            padding,
        )
        value_sum = value_sum + jnp.pad(
            jnp.einsum("hqk,hqd->kd", probs_low, grad_block, preferred_element_type=f32), padding
        )
    return jnp.concatenate(query_parts, axis=1), key_sum, value_sum


def heads_first(flat, heads):
    return jnp.transpose(flat.reshape(flat.shape[0], heads, HEAD), (1, 0, 2))


def heads_last(stacked):
    return jnp.transpose(stacked, (1, 0, 2)).reshape(stacked.shape[1], -1)


def shards(
    inputs,
    attention_gain,
    query_weight,
    key_weight,
    value_weight,
    output_weight,
    feedforward_gain,
    gate_weight,
    up_weight,
    down_weight,
    cotangent,
):
    S, Dp = lax.axis_size("seq"), lax.axis_size("dp")
    sequences, tokens, width = inputs.shape
    length = tokens * S
    rows = query_weight.shape[0]
    heads = H // S
    q_cols = heads * HEAD
    repeats = S // KV
    down_rows = down_weight.shape[0]
    hidden = down_rows * Dp
    block_rows = min(length, max(512, length // 8))

    gain_one = attention_gain.astype(f32)[:, None]
    gain_two = feedforward_gain.astype(f32)[:, None]

    def folded(weight, gain):
        return (weight.astype(f32) * gain).astype(bf16)

    def per_group_kv(weight):
        return jnp.repeat(weight.reshape(rows, KV, HEAD), repeats, axis=1)

    def per_group_hidden(weight):
        return jnp.transpose(weight.reshape(rows, Dp, S, down_rows), (2, 0, 1, 3)).reshape(
            S, rows, hidden
        )

    packed = jnp.concatenate(
        [
            folded(query_weight, gain_one).reshape(rows, S, q_cols),
            per_group_kv(folded(key_weight, gain_one)),
            per_group_kv(folded(value_weight, gain_one)),
        ],
        axis=2,
    )
    packed_qkv = jnp.transpose(packed, (1, 0, 2))
    forward_perm = [(Dp * s + d, d * S + s) for s in range(S) for d in range(Dp)]
    backward_perm = [(b, a) for a, b in forward_perm]
    w_o_piece = lax.ppermute(output_weight, ("dp", "seq"), forward_perm)
    line = S == 8 and Dp == 4
    width_f = -(-hidden // 256) * 256 if line else hidden

    def padded(part, axis):
        pads = [(0, 0)] * part.ndim
        pads[axis] = (0, width_f - hidden)
        return jnp.pad(part, pads)

    packed_gu = jnp.concatenate(
        [
            padded(per_group_hidden(folded(gate_weight, gain_two)), 2),
            padded(per_group_hidden(folded(up_weight, gain_two)), 2),
        ],
        axis=2,
    )
    w_d = padded(gather_dp(down_weight), 0)

    flat = inputs.reshape(tokens, width).astype(f32)
    r1 = rms_scale(flat)
    s1 = flat * r1
    cosine, sine = rope_tables(length)
    dy = cotangent.reshape(tokens, width)
    if line:
        turn = jnp.concatenate(
            [cosine, cosine, cosine, cosine, -sine, sine, -sine, sine], axis=-1
        )[:, 0]
        summed, s1_all, dy_all, w_qkv, w_gu, w_o, q2, k2, kz, vz, totals, attended = attention_front(
            s1.astype(bf16), packed_qkv, packed_gu, w_o_piece, dy, turn, heads
        )
    else:
        w_qkv = gather_dp(exchange_seq(packed_qkv).reshape(S * rows, q_cols + 2 * HEAD))
        w_gu = gather_dp(exchange_seq(packed_gu).reshape(S * rows, 2 * hidden))
        w_o = gather_dp(w_o_piece)
        s1_all = gather_seq(s1.astype(bf16))
        qkv = mm(s1_all, w_qkv)
        queries = rotate(qkv[:, :q_cols].reshape(length, heads, HEAD), cosine, sine).astype(bf16)
        queries = jnp.transpose(queries, (1, 0, 2))
        keys = rotate(qkv[:, None, q_cols : q_cols + HEAD], cosine, sine).astype(bf16)[:, 0]
        values = qkv[:, q_cols + HEAD :].astype(bf16)
        attended, totals = attention_forward(queries, keys, values, block_rows)
        attended = heads_last(attended)
        summed = scatter_seq(mm(attended, w_o).astype(bf16))
        dy_all = gather_seq(dy)
    middle = flat + summed
    r2 = rms_scale(middle)
    s2 = middle * r2
    if line:
        out_sum, e2, g_gu, down_grad = feedforward(
            s2.astype(bf16), dy_all, w_gu, w_d, down_rows
        )
    else:
        out_sum, e2, g_gu, down_grad = feedforward_plain(s2.astype(bf16), dy_all, w_gu, w_d)

    d_middle = dy.astype(f32) + r2 * (e2 - s2 * jnp.mean(e2 * s2, axis=-1, keepdims=True))
    if line:
        table = jnp.concatenate([cosine, cosine, sine, -sine], axis=-1)[:, 0] * HEAD ** (-0.5)

        def with_zeros(u):
            return jnp.concatenate([u, jnp.zeros_like(u)], axis=-1)

        w_o2 = with_zeros(w_o.reshape(heads, 1, HEAD, width).swapaxes(2, 3)).swapaxes(2, 3)
        e1, g_qkv, g_o, g_gu = attention_back(
            d_middle.astype(bf16),
            q2,
            k2,
            kz,
            vz,
            totals,
            attended,
            s1_all,
            w_qkv,
            w_o2.reshape(2 * q_cols, width),
            table,
            g_gu,
            rows,
        )
        g_o = g_o.astype(bf16)
    else:
        g_gu = exchange_seq(g_gu.reshape(S, rows, 2 * width_f))
        dm_all = gather_seq(d_middle.astype(bf16))
        d_att = heads_first(mm_nt(dm_all, w_o).astype(bf16), heads)
        d_q, d_k, d_v = attention_backward(queries, keys, values, d_att, totals, block_rows)
        d_q = jnp.transpose(d_q, (1, 0, 2))
        d_qkv = jnp.concatenate(
            [
                rotate(d_q, cosine, -sine).reshape(length, q_cols).astype(bf16),
                rotate(d_k[:, None], cosine, -sine)[:, 0].astype(bf16),
                d_v.astype(bf16),
            ],
            axis=1,
        )
        e1 = scatter_seq(mm_nt(d_qkv, w_qkv).astype(bf16))
        g_o = scatter_dp(mm_tn(attended, dm_all).astype(bf16))
        g_qkv = scatter_dp(mm_tn(s1_all, d_qkv).astype(bf16))
        g_qkv = exchange_seq(g_qkv.reshape(S, rows, q_cols + 2 * HEAD))
    output = (middle + out_sum).astype(bf16)
    input_grad = d_middle + r1 * (e1 - s1 * jnp.mean(e1 * s1, axis=-1, keepdims=True))
    output_grad = lax.ppermute(g_o, ("dp", "seq"), backward_perm).astype(f32)

    if line:
        g_gate, g_up, g_query, g_key, g_value, gain_one_grad, gain_two_grad = spread(
            g_gu,
            g_qkv,
            (gate_weight, up_weight, query_weight, key_weight, value_weight),
            (gain_one, gain_two),
            down_rows,
            repeats,
        )
        return (
            output.reshape(sequences, tokens, width),
            input_grad.reshape(sequences, tokens, width),
            gain_one_grad[:, 0],
            g_query,
            g_key,
            g_value,
            output_grad,
            gain_two_grad[:, 0],
            g_gate,
            g_up,
            down_grad,
        )

    g_gu, g_qkv = g_gu.astype(f32), g_qkv.astype(f32)

    def back_hidden(part):
        return jnp.transpose(part.reshape(S, rows, Dp, down_rows), (1, 2, 0, 3)).reshape(rows, -1)

    def back_kv(part):
        part = jnp.sum(part.reshape(KV, repeats, rows, HEAD), axis=1)
        return jnp.transpose(part, (1, 0, 2)).reshape(rows, KV * HEAD)

    g_gate, g_up = back_hidden(g_gu[..., :hidden]), back_hidden(g_gu[..., hidden:])
    g_query = jnp.transpose(g_qkv[..., :q_cols], (1, 0, 2)).reshape(rows, width)
    g_key = back_kv(g_qkv[..., q_cols : q_cols + HEAD])
    g_value = back_kv(g_qkv[..., q_cols + HEAD :])

    def row_dot(weight, grad):
        return jnp.sum(weight.astype(f32) * grad, axis=1)

    gain_two_grad = row_dot(gate_weight, g_gate) + row_dot(up_weight, g_up)
    gain_one_grad = (
        row_dot(query_weight, g_query) + row_dot(key_weight, g_key) + row_dot(value_weight, g_value)
    )
    return (
        output.reshape(sequences, tokens, width),
        input_grad.reshape(sequences, tokens, width),
        gain_one_grad,
        g_query * gain_one,
        g_key * gain_one,
        g_value * gain_one,
        output_grad,
        gain_two_grad,
        g_gate * gain_two,
        g_up * gain_two,
        down_grad,
    )


def solution(mesh):
    both = ("dp", "seq")
    tok, vec, mat = P("dp", "seq", None), P(both), P(both, None)
    in_specs = (tok, vec, mat, mat, mat, mat, vec, mat, mat, mat, tok)
    out_specs = (tok, tok, vec, mat, mat, mat, mat, vec, mat, mat, mat)
    return jax.shard_map(shards, mesh=mesh, in_specs=in_specs, out_specs=out_specs, check_vma=False)
```

```python
import functools

import jax
import jax.numpy as jnp
from jax import lax
from jax.experimental import pallas as pl
from jax.experimental.pallas import tpu as pltpu
from jax.sharding import PartitionSpec as P

H = 32
KV = 4
HEAD = 64

epsilon = 1e-05
masked = -1e30
f32 = jnp.float32
bf16 = jnp.bfloat16


def rope_tables(length):
    half_width = HEAD // 2
    frequency = 10000.0 ** (-(jnp.arange(half_width, dtype=f32) * 2.0) / HEAD)
    angles = jnp.arange(length, dtype=f32)[:, None] * frequency[None, :]
    return (jnp.cos(angles)[:, None, :], jnp.sin(angles)[:, None, :])


def rotate(values, cosine, sine):
    front, back = values[..., : HEAD // 2], values[..., HEAD // 2 :]
    return jnp.concatenate([front * cosine - back * sine, back * cosine + front * sine], axis=-1)


def rms_scale(values):
    return lax.rsqrt(jnp.mean(values * values, axis=-1, keepdims=True) + epsilon)


def mm(a, b):
    return lax.dot_general(a, b, (((1,), (0,)), ((), ())), preferred_element_type=f32)


def mm_nt(a, b):
    return lax.dot_general(a, b, (((1,), (1,)), ((), ())), preferred_element_type=f32)


def mm_tn(a, b):
    return lax.dot_general(a, b, (((0,), (0,)), ((), ())), preferred_element_type=f32)


def seq_place():
    me = lax.axis_index("seq")
    return me // 2, me % 2

def hello(barrier, peer, axis):
    pl.semaphore_signal(
        barrier, inc=1, device_id={axis: peer}, device_id_type=pl.DeviceIdType.MESH
    )


def greet(z, y, Z, dp=None):
    barrier = pltpu.get_barrier_semaphore()
    hello(barrier, z * 2 + 1 - y, "seq")

    @pl.when(z > 0)
    def _():
        hello(barrier, z * 2 + y - 2, "seq")

    @pl.when(z < Z - 1)
    def _():
        hello(barrier, z * 2 + y + 2, "seq")

    count = 1 + (z + Z - 1) // Z + (2 * Z - 2 - z) // Z
    if dp is not None:
        hello(barrier, dp + 1 - 2 * (dp % 2), "dp")
        hello(barrier, dp + 2 - 4 * (dp // 2), "dp")
        count = count + 2
    pl.semaphore_wait(barrier, count)


def send(src, dst, ssem, rsem, peer, axis="seq"):
    return pltpu.make_async_remote_copy(
        src_ref=src,
        dst_ref=dst,
        send_sem=ssem,
        recv_sem=rsem,
        device_id={axis: peer},
        device_id_type=pl.DeviceIdType.MESH,
    )


def gather_kernel(Z, T, x_ref, out_ref, up_sem, dn_sem, y_sem, recv_sem, own_sem):
    z, y = seq_place()
    greet(z, y, Z)
    def block(zz, yy):
        return out_ref.at[pl.ds(pl.multiple_of((zz * 2 + yy) * T, T), T)]
    def copy(src, zz, sem, peer):
        return send(src, block(zz, y), sem.at[zz], recv_sem.at[zz * 2 + y], peer)
    own = pltpu.make_async_copy(x_ref, block(z, y), own_sem)
    own.start()
    peer_y, peer_up, peer_dn = z * 2 + 1 - y, z * 2 + y + 2, z * 2 + y - 2
    copy(x_ref, z, y_sem, peer_y).start()
    @pl.when(z < Z - 1)
    def _(): copy(x_ref, z, up_sem, peer_up).start()
    @pl.when(z > 0)
    def _(): copy(x_ref, z, dn_sem, peer_dn).start()
    for h in range(1, Z):
        @pl.when(z >= h)
        def _():
            zz = z - h
            copy(block(zz, y), zz, y_sem, peer_y).wait_recv()
            @pl.when(z < Z - 1)
            def _(): copy(block(zz, y), zz, up_sem, peer_up).start()
            copy(block(zz, y), zz, y_sem, peer_y).start()
        @pl.when(z + h < Z)
        def _():
            zz = z + h
            copy(block(zz, y), zz, y_sem, peer_y).wait_recv()
            @pl.when(z > 0)
            def _(): copy(block(zz, y), zz, dn_sem, peer_dn).start()
            copy(block(zz, y), zz, y_sem, peer_y).start()
    own.wait()
    for zz in range(Z):
        b = block(zz, 1 - y)
        send(b, b, y_sem.at[zz], recv_sem.at[zz * 2 + 1 - y], peer_y).wait_recv()
        c = copy(block(zz, y), zz, y_sem, peer_y)
        c.wait_send()
        @pl.when((zz <= z) & (z < Z - 1))
        def _(): copy(block(zz, y), zz, up_sem, peer_up).wait_send()
        @pl.when((zz >= z) & (z > 0))
        def _(): copy(block(zz, y), zz, dn_sem, peer_dn).wait_send()

def gather_line(x, cid=1):
    S = lax.axis_size("seq"); Z = S // 2
    T, D = x.shape
    return pl.pallas_call(
        functools.partial(gather_kernel, Z, T),
        out_shape=jax.ShapeDtypeStruct((S * T, D), x.dtype),
        in_specs=[pl.BlockSpec(memory_space=pltpu.VMEM)],
        out_specs=pl.BlockSpec(memory_space=pl.ANY),
        scratch_shapes=[pltpu.SemaphoreType.DMA((Z,))] * 3 + [pltpu.SemaphoreType.DMA((S,)), pltpu.SemaphoreType.DMA],
        compiler_params=pltpu.CompilerParams(collective_id=cid, has_side_effects=True),
        name="gather_seq",
    )(x)

def scatter_kernel(Z, T, p_ref, out_ref, ybuf, upbuf, dnbuf, upst, dnst, up_s, dn_s, y_s, up_r, dn_r, y_r):
    z, y = seq_place()
    greet(z, y, Z)
    peer_y, peer_up, peer_dn = z * 2 + 1 - y, z * 2 + y + 2, z * 2 + y - 2
    def mine(zz, yy):
        return p_ref.at[pl.ds(pl.multiple_of((zz * 2 + yy) * T, T), T)]
    def y_copy(zz):
        return send(mine(zz, 1 - y), ybuf.at[zz], y_s.at[zz], y_r.at[zz], peer_y)
    def up_copy(zz):
        return send(upst.at[zz], upbuf.at[zz], up_s.at[zz], up_r.at[zz], peer_up)
    def dn_copy(zz):
        return send(dnst.at[zz], dnbuf.at[zz], dn_s.at[zz], dn_r.at[zz], peer_dn)
    for h in range(Z - 1, 0, -1):
        @pl.when(z + h < Z)
        def _(): y_copy(z + h).start()
        @pl.when(z - h >= 0)
        def _(): y_copy(z - h).start()
    y_copy(z).start()
    for h in range(Z - 1, 0, -1):
        @pl.when(z + h < Z)
        def _():
            d = z + h
            y_copy(d).wait_recv()
            upst[d] = (mine(d, y)[...].astype(f32) + ybuf[d].astype(f32)).astype(bf16)
            @pl.when(z > 0)
            def _():
                up_copy(d).wait_recv()
                upst[d] = (mine(d, y)[...].astype(f32) + ybuf[d].astype(f32) + upbuf[d].astype(f32)).astype(bf16)
            up_copy(d).start()
        @pl.when(z - h >= 0)
        def _():
            d = z - h
            y_copy(d).wait_recv()
            dnst[d] = (mine(d, y)[...].astype(f32) + ybuf[d].astype(f32)).astype(bf16)
            @pl.when(z < Z - 1)
            def _():
                dn_copy(d).wait_recv()
                dnst[d] = (mine(d, y)[...].astype(f32) + ybuf[d].astype(f32) + dnbuf[d].astype(f32)).astype(bf16)
            dn_copy(d).start()
    y_copy(z).wait_recv()
    out_ref[...] = mine(z, y)[...].astype(f32) + ybuf[z].astype(f32)
    @pl.when(z > 0)
    def _():
        up_copy(z).wait_recv()
        out_ref[...] += upbuf[z].astype(f32)
    @pl.when(z < Z - 1)
    def _():
        dn_copy(z).wait_recv()
        out_ref[...] += dnbuf[z].astype(f32)
    for zz in range(Z):
        y_copy(zz).wait_send()
        @pl.when(zz > z)
        def _(): up_copy(zz).wait_send()
        @pl.when(zz < z)
        def _(): dn_copy(zz).wait_send()

def scatter_line(p, cid=2):
    S = lax.axis_size("seq"); Z = S // 2
    L, D = p.shape; T = L // S
    return pl.pallas_call(
        functools.partial(scatter_kernel, Z, T),
        out_shape=jax.ShapeDtypeStruct((T, D), f32),
        in_specs=[pl.BlockSpec(memory_space=pltpu.VMEM)],
        out_specs=pl.BlockSpec(memory_space=pltpu.VMEM),
        scratch_shapes=[pltpu.VMEM((Z, T, D), bf16)] * 5 + [pltpu.SemaphoreType.DMA((Z,))] * 6,
        compiler_params=pltpu.CompilerParams(collective_id=cid, has_side_effects=True, vmem_limit_bytes=60 << 20),
        name="scatter_seq",
    )(p)


def line_rank(i, z):
    upper = z // 2
    inner = (z + upper) % 2
    base = i + inner * (1 - i // 2) * (1 - 2 * i)
    return base + upper * (3 - 2 * base)


def above(d, z):
    return (d - z + 3) // 4


def rows_of(ref, start, size):
    return ref.at[pl.ds(pl.multiple_of(start, size), size)]


def in_chunks(rows, chunk, step):
    def body(i, carry):
        step(pl.ds(pl.multiple_of(i * chunk, chunk), chunk))
        return carry

    lax.fori_loop(0, rows // chunk, body, 0)


class Gather:
    def __init__(self, z, y, T, own, full, up_sem, dn_sem, y_sem, recv_sem, own_sem):
        self.z, self.y, self.T, self.own, self.full = z, y, T, own, full
        self.sems = {"up": up_sem, "dn": dn_sem, "y": y_sem}
        self.peers = {"up": z * 2 + y + 2, "dn": z * 2 + y - 2, "y": z * 2 + 1 - y}
        self.recv_sem, self.own_sem = recv_sem, own_sem

    def block(self, zz, yy):
        return rows_of(self.full, (zz * 2 + yy) * self.T, self.T)

    def copy(self, src, zz, way):
        return send(
            src,
            self.block(zz, self.y),
            self.sems[way].at[zz],
            self.recv_sem.at[zz * 2 + self.y],
            self.peers[way],
        )

    def start(self):
        z = self.z
        pltpu.make_async_copy(self.own, self.block(z, self.y), self.own_sem).start()
        self.copy(self.own, z, "y").start()

        @pl.when(z < 3)
        def _():
            self.copy(self.own, z, "up").start()

        @pl.when(z > 0)
        def _():
            self.copy(self.own, z, "dn").start()

    def own_ready(self):
        pltpu.make_async_copy(self.own, self.block(self.z, self.y), self.own_sem).wait()

    def hop(self, h):
        z = self.z

        @pl.when(z >= h)
        def _():
            src = self.block(z - h, self.y)
            self.copy(src, z - h, "y").wait_recv()

            @pl.when(z < 3)
            def _():
                self.copy(src, z - h, "up").start()

            self.copy(src, z - h, "y").start()

        @pl.when(z + h < 4)
        def _():
            src = self.block(z + h, self.y)
            self.copy(src, z + h, "y").wait_recv()

            @pl.when(z > 0)
            def _():
                self.copy(src, z + h, "dn").start()

            self.copy(src, z + h, "y").start()

    def pair_ready(self, zz):
        b = self.block(zz, 1 - self.y)
        send(
            b, b, self.sems["y"].at[zz], self.recv_sem.at[zz * 2 + 1 - self.y], self.peers["y"]
        ).wait_recv()

    def finish_one(self, zz):
        z = self.z
        src = self.block(zz, self.y)
        self.copy(src, zz, "y").wait_send()

        @pl.when((zz <= z) & (z < 3))
        def _():
            self.copy(src, zz, "up").wait_send()

        @pl.when((zz >= z) & (z > 0))
        def _():
            self.copy(src, zz, "dn").wait_send()

    def finish(self):
        for zz in range(4):
            self.finish_one(zz)


class Scatter:
    def __init__(self, z, y, T, part, ybuf, rbuf, y_s, y_r, z_s, z_r):
        self.z, self.y, self.T, self.part = z, y, T, part
        self.ybuf, self.rbuf = ybuf, rbuf
        self.y_s, self.y_r, self.z_s, self.z_r = y_s, y_r, z_s, z_r

    def rows(self, zz, yy):
        return rows_of(self.part, (zz * 2 + yy) * self.T, self.T)

    def y_copy(self, d):
        peer = self.z * 2 + 1 - self.y
        return send(
            self.rows(d, 1 - self.y), self.ybuf.at[d], self.y_s.at[d], self.y_r.at[d], peer
        )

    def z_copy(self, d, up):
        slot = d + up
        peer = self.z * 2 + self.y + 4 * up - 2
        return send(self.ybuf.at[d], self.rbuf.at[slot], self.z_s.at[d], self.z_r.at[slot], peer)

    def start(self, d):
        self.y_copy(d).start()

    def pass_on(self, d):
        z = self.z
        up = above(d, z)
        self.y_copy(d).wait_recv()
        mine, slot = self.rows(d, self.y), self.ybuf.at[d]
        inner = (z > 0) & (z < 3)

        @pl.when(inner)
        def _():
            self.z_copy(d, up).wait_recv()
            far = self.rbuf.at[d + up]

            def step(c):
                slot[c] = (
                    mine[c].astype(f32) + slot[c].astype(f32) + far[c].astype(f32)
                ).astype(bf16)

            in_chunks(self.T, 32, step)

        @pl.when(jnp.logical_not(inner))
        def _():
            def step(c):
                slot[c] = (mine[c].astype(f32) + slot[c].astype(f32)).astype(bf16)

            in_chunks(self.T, 32, step)

        self.z_copy(d, up).start()

    def finish(self, out_ref):
        z = self.z
        self.y_copy(z).wait_recv()
        mine, slot = self.rows(z, self.y), self.ybuf.at[z]

        def first(c):
            out_ref[c] = mine[c].astype(f32) + slot[c].astype(f32)

        in_chunks(self.T, 32, first)

        def more(slot):
            def step(c):
                out_ref[c] += slot[c].astype(f32)

            in_chunks(self.T, 32, step)

        @pl.when(z > 0)
        def _():
            self.z_copy(z, 1).wait_recv()
            more(self.rbuf.at[z + 1])

        @pl.when(z < 3)
        def _():
            self.z_copy(z, 0).wait_recv()
            more(self.rbuf.at[z])

        for d in range(4):
            self.y_copy(d).wait_send()

            @pl.when(z != d)
            def _():
                self.z_copy(d, above(d, z)).wait_send()


def line_sems(n):
    return [pltpu.SemaphoreType.DMA((4,))] * 3 + [
        pltpu.SemaphoreType.DMA((8,)),
        pltpu.SemaphoreType.DMA,
    ]


def sum_scratch(T, width):
    return [
        pltpu.VMEM((4, T, width), bf16),
        pltpu.VMEM((5, T, width), bf16),
        pltpu.SemaphoreType.DMA((4,)),
        pltpu.SemaphoreType.DMA((4,)),
        pltpu.SemaphoreType.DMA((4,)),
        pltpu.SemaphoreType.DMA((5,)),
    ]


class DpSum:
    def __init__(self, src, size, abuf, bbuf, a_s, a_r, b_s, b_r):
        dp = lax.axis_index("dp")
        self.core, self.far = dp % 2, dp // 2
        self.partner, self.across = dp + 1 - 2 * (dp % 2), dp + 2 - 4 * (dp // 2)
        self.src, self.size = src, size
        self.abuf, self.bbuf = abuf, bbuf
        self.a_s, self.a_r, self.b_s, self.b_r = a_s, a_r, b_s, b_r

    def rows(self, d):
        return rows_of(self.src, d * self.size, self.size)

    def a_copy(self, j):
        return send(
            self.rows(2 * j + 1 - self.core),
            self.abuf.at[j],
            self.a_s.at[j],
            self.a_r.at[j],
            self.partner,
            "dp",
        )

    def b_copy(self):
        return send(self.abuf.at[1 - self.far], self.bbuf, self.b_s, self.b_r, self.across, "dp")

    def start(self):
        self.a_copy(0).start()
        self.a_copy(1).start()

    def middle(self):
        self.a_copy(0).wait_recv()
        self.a_copy(1).wait_recv()
        j = 1 - self.far
        mine, slot = self.rows(2 * j + self.core), self.abuf.at[j]

        def step(c):
            slot[c] = (mine[c].astype(f32) + slot[c].astype(f32)).astype(bf16)

        in_chunks(self.size, 16, step)
        self.b_copy().start()

    def finish(self, out_ref):
        self.b_copy().wait_recv()
        mine, slot = self.rows(2 * self.far + self.core), self.abuf.at[self.far]

        def step(c):
            out_ref[c] = (
                mine[c].astype(f32) + slot[c].astype(f32) + self.bbuf[c].astype(f32)
            ).astype(out_ref.dtype)

        in_chunks(self.size, 16, step)
        self.a_copy(0).wait_send()
        self.a_copy(1).wait_send()
        self.b_copy().wait_send()


class Exchange:
    def __init__(self, me, src, landing, s_sem, r_sem, own_sem):
        self.me, self.src, self.landing = me, src, landing
        self.s_sem, self.r_sem, self.own_sem = s_sem, r_sem, own_sem

    def own(self):
        return pltpu.make_async_copy(self.src(self.me), self.landing(self.me), self.own_sem)

    def copy(self, peer, sender):
        return send(
            self.src(peer), self.landing(sender), self.s_sem.at[peer], self.r_sem.at[sender], peer
        )

    def start(self, *steps):
        for step in steps:
            self.copy((self.me + step) % 8, self.me).start()

    def ready(self):
        self.own().wait()
        for step in range(1, 8):
            peer = (self.me + step) % 8
            self.copy(peer, peer).wait_recv()

    def finish(self):
        for step in range(1, 8):
            self.copy((self.me + step) % 8, self.me).wait_send()


class DpGather:
    def __init__(self, own, full, size, s_sem, r_sem):
        dp = lax.axis_index("dp")
        self.dp, self.partner, self.across = dp, dp + 1 - 2 * (dp % 2), dp + 2 - 4 * (dp // 2)
        self.diagonal = 3 - dp
        self.own, self.full, self.size = own, full, size
        self.s_sem, self.r_sem = s_sem, r_sem

    def block(self, d):
        return rows_of(self.full, d * self.size, self.size)

    def copy(self, src, d, k, peer):
        return send(src, self.block(d), self.s_sem.at[k], self.r_sem.at[k], peer, "dp")

    def start(self):
        self.copy(self.own, self.dp, 0, self.across).start()
        self.copy(self.own, self.dp, 1, self.partner).start()

    def relay(self):
        far = self.block(self.across)
        self.copy(far, self.across, 0, self.across).wait_recv()
        self.copy(far, self.across, 2, self.partner).start()

    def ready(self):
        near, diagonal = self.block(self.partner), self.block(self.diagonal)
        self.copy(near, self.partner, 1, self.partner).wait_recv()
        self.copy(diagonal, self.diagonal, 2, self.partner).wait_recv()

    def finish(self):
        self.copy(self.own, self.dp, 0, self.across).wait_send()
        self.copy(self.own, self.dp, 1, self.partner).wait_send()
        self.copy(self.block(self.across), self.across, 2, self.partner).wait_send()


def dp_scratch(size, width):
    return [
        pltpu.VMEM((2, size, width), bf16),
        pltpu.VMEM((size, width), bf16),
        pltpu.SemaphoreType.DMA((2,)),
        pltpu.SemaphoreType.DMA((2,)),
        pltpu.SemaphoreType.DMA,
        pltpu.SemaphoreType.DMA,
    ]


def feedforward_kernel(
    T, x_ref, dy_ref, wgu_ref, wd_ref, out_ref, e2_ref, ggu_ref, gd_ref,
    full, hid, dgu, pout, part, ggu, gdown, up_sem, dn_sem, ag_y, ag_r, own_sem,
    pybuf, prbuf, py_s, py_r, pz_s, pz_r,
    ybuf, rbuf, y_s, y_r, z_s, z_r,
    ga, gb, ga_s, ga_r, gb_s, gb_r,
    da, db, da_s, da_r, db_s, db_r,
):
    z, y = seq_place()
    dp = lax.axis_index("dp")
    F = hid.shape[1]
    greet(z, y, 4, dp)
    gather = Gather(z, y, T, x_ref, full, up_sem, dn_sem, ag_y, ag_r, own_sem)
    scatter_out = Scatter(z, y, T, pout, pybuf, prbuf, py_s, py_r, pz_s, pz_r)
    scatter = Scatter(z, y, T, part, ybuf, rbuf, y_s, y_r, z_s, z_r)
    sum_gu = DpSum(ggu, ggu.shape[0] // 4, ga, gb, ga_s, ga_r, gb_s, gb_r)
    sum_down = DpSum(gdown, gd_ref.shape[0], da, db, da_s, da_r, db_s, db_r)
    gather.start()
    gather.own_ready()
    inner = (z > 0) & (z < 3)
    at_end = jnp.logical_not(inner)

    def pass_on(rank):
        scatter_out.pass_on(line_rank(rank, z))
        scatter.pass_on(line_rank(rank, z))

    def compute(i, carry):
        for h in range(1, 4):

            @pl.when(i == h - 1)
            def _():
                gather.hop(h)

        zz = line_rank(i, z)
        gather.pair_ready(zz)

        @pl.when(i == 2)
        def _():
            scatter_out.start(line_rank(1, z))

        @pl.when(i == 3)
        def _():
            scatter_out.start(line_rank(2, z))
            scatter.start(line_rank(2, z))

        @pl.when((i == 3) & at_end)
        def _():
            scatter_out.pass_on(line_rank(1, z))

        r = pl.ds(pl.multiple_of(zz * 2 * T, 2 * T), 2 * T)
        gu = mm(full[r, :], wgu_ref[...])
        gate, up = gu[:, :F], gu[:, F:]
        sig = 1.0 / (1.0 + jnp.exp(-gate))
        act = gate * sig
        hid[r, :] = (act * up).astype(bf16)
        dh = mm_nt(dy_ref[r, :], wd_ref[...])
        dgu[r, :F] = (dh * up * sig * (1.0 + gate * (1.0 - sig))).astype(bf16)
        dgu[r, F:] = (dh * act).astype(bf16)
        pout[r, :] = mm(hid[r, :], wd_ref[...]).astype(bf16)

        @pl.when(i == 3)
        def _():
            scatter_out.start(zz)

        part[r, :] = mm_nt(dgu[r, :], wgu_ref[...]).astype(bf16)
        return carry

    lax.fori_loop(0, 4, compute, 0)
    scatter.start(line_rank(3, z))
    scatter.start(line_rank(1, z))
    scatter_out.start(z)
    scatter.start(z)

    def gate_up_tile(i, carry):
        @pl.when((i == 4) & at_end)
        def _():
            pass_on(2)

        r = pl.ds(pl.multiple_of(i * 256, 256), 256)
        ggu[r, :] = mm_tn(full[:, r], dgu[...]).astype(bf16)
        return carry

    def down_tile(i, carry):
        r = pl.ds(pl.multiple_of(i * 256, 256), 256)
        gdown[r, :] = mm_tn(hid[:, r], dy_ref[...]).astype(bf16)
        return carry

    lax.fori_loop(0, 8, gate_up_tile, 0)
    sum_gu.start()
    pass_on(3 - (z + 1) % 4 // 2)
    lax.fori_loop(0, F // 256, down_tile, 0)
    sum_down.start()

    @pl.when(inner)
    def _():
        pass_on(3)

    sum_gu.middle()

    @pl.when(inner)
    def _():
        scatter_out.pass_on(line_rank(1, z))

    scatter.pass_on(line_rank(1, z))
    sum_down.middle()
    sum_gu.finish(ggu_ref)
    sum_down.finish(gd_ref)
    scatter_out.finish(out_ref)
    scatter.finish(e2_ref)
    gather.finish()


def feedforward(x, dy_all, w_gu, w_d, down_rows, cid=3):
    T, width = x.shape
    L, F = dy_all.shape[0], w_d.shape[0]
    vmem = pl.BlockSpec(memory_space=pltpu.VMEM)
    return pl.pallas_call(
        functools.partial(feedforward_kernel, T),
        out_shape=(
            jax.ShapeDtypeStruct((T, width), f32),
            jax.ShapeDtypeStruct((T, width), f32),
            jax.ShapeDtypeStruct((width // 4, 2 * F), bf16),
            jax.ShapeDtypeStruct((down_rows, width), f32),
        ),
        in_specs=[vmem] * 4,
        out_specs=(vmem,) * 4,
        scratch_shapes=[
            pltpu.VMEM((L, width), bf16),
            pltpu.VMEM((L, F), bf16),
            pltpu.VMEM((L, 2 * F), bf16),
            pltpu.VMEM((L, width), bf16),
            pltpu.VMEM((L, width), bf16),
            pltpu.VMEM((width, 2 * F), bf16),
            pltpu.VMEM((F, width), bf16),
        ]
        + line_sems(4)
        + sum_scratch(T, width)
        + sum_scratch(T, width)
        + dp_scratch(width // 4, 2 * F)
        + dp_scratch(down_rows, width),
        compiler_params=pltpu.CompilerParams(
            collective_id=cid, has_side_effects=True, vmem_limit_bytes=67000000
        ),
        name="feedforward",
    )(x, dy_all, w_gu, w_d)


def attention_front_kernel(
    T, heads, repeats, s1_ref, wq_ref, wk_ref, wv_ref, wg_ref, wu_ref, one_ref, two_ref,
    wo_piece_ref, wd_piece_ref, dy_ref, cos_ref, sin_ref,
    mid_ref, s1_all, dy_all, wqkv, wgu, wd, wo, q_out, k2_ref, kz_ref, vz_ref, lse_ref, att_ref,
    score, part, piece_ref, gu_ref,
    up_sem, dn_sem, ag_y, ag_r, own_sem,
    up_sem2, dn_sem2, ag_y2, ag_r2, own_sem2,
    ybuf, rbuf, y_s, y_r, z_s, z_r,
    w_s, w_r, o_s, o_r, g_s, g_r, d_s, d_r, ex_s, ex_r, gx_s, gx_r, ex_own, gx_own, wo_own, wd_own, turn_s, turn_r,
):
    z, y = seq_place()
    me = z * 2 + y
    dp = lax.axis_index("dp")
    rows, out_rows, down_rows = piece_ref.shape[1], wo_piece_ref.shape[0], wd_piece_ref.shape[0]
    q_cols, F = heads * HEAD, gu_ref.shape[2] // 2
    here, there = dp * 8 + me, me * 4 + dp
    stays = here == there
    barrier = pltpu.get_barrier_semaphore()

    def greet_at(place):
        pl.semaphore_signal(
            barrier,
            inc=1,
            device_id={"dp": place[0], "seq": place[1]},
            device_id_type=pl.DeviceIdType.MESH,
        )

    for step in range(1, 8):
        hello(barrier, (me + step) % 8, "seq")
    hello(barrier, dp + 1 - 2 * (dp % 2), "dp")
    hello(barrier, dp + 2 - 4 * (dp // 2), "dp")

    @pl.when(jnp.logical_not(stays))
    def _():
        greet_at((here % 4, here // 4))
        greet_at((there // 8, there % 8))

    gain = one_ref[...]
    for s in range(8):
        kv = pl.ds(s // repeats * HEAD, HEAD)
        q = wq_ref[:, s * q_cols : (s + 1) * q_cols].astype(f32) * gain
        k, v = wk_ref[:, kv].astype(f32) * gain, wv_ref[:, kv].astype(f32) * gain
        piece_ref[s, :, :q_cols] = q.astype(bf16)
        piece_ref[s, :, q_cols:] = jnp.concatenate([k, v], axis=1).astype(bf16)

    @pl.when(stays)
    def _():
        pl.semaphore_wait(barrier, 9)

    @pl.when(jnp.logical_not(stays))
    def _():
        pl.semaphore_wait(barrier, 11)

    gather = Gather(z, y, T, s1_ref, s1_all, up_sem, dn_sem, ag_y, ag_r, own_sem)
    gather_dy = Gather(z, y, T, dy_ref, dy_all, up_sem2, dn_sem2, ag_y2, ag_r2, own_sem2)
    scatter = Scatter(z, y, T, part, ybuf, rbuf, y_s, y_r, z_s, z_r)
    w_own = rows_of(wqkv, dp * 8 * rows, 8 * rows)
    w_all = DpGather(w_own, wqkv, 8 * rows, w_s, w_r)
    o_all = DpGather(rows_of(wo, dp * out_rows, out_rows), wo, out_rows, o_s, o_r)
    d_all = DpGather(wd_piece_ref, wd, down_rows, d_s, d_r)

    def turned_copy():
        return pltpu.make_async_remote_copy(
            src_ref=wo_piece_ref,
            dst_ref=rows_of(wo, here % 4 * out_rows, out_rows),
            send_sem=turn_s,
            recv_sem=turn_r,
            device_id={"dp": here % 4, "seq": here // 4},
            device_id_type=pl.DeviceIdType.MESH,
        )

    def landed():
        mine = o_all.block(dp)
        return pltpu.make_async_remote_copy(
            src_ref=mine,
            dst_ref=mine,
            send_sem=turn_s,
            recv_sem=turn_r,
            device_id={"dp": here % 4, "seq": here // 4},
            device_id_type=pl.DeviceIdType.MESH,
        )

    g_own = rows_of(wgu, dp * 8 * rows, 8 * rows)
    g_all = DpGather(g_own, wgu, 8 * rows, g_s, g_r)

    def pieces(src, full, *sems):
        return Exchange(
            me, lambda p: src.at[p], lambda p: rows_of(full, (dp * 8 + p) * rows, rows), *sems
        )

    exchange = pieces(piece_ref, wqkv, ex_s, ex_r, ex_own)
    exchange_gu = pieces(gu_ref, wgu, gx_s, gx_r, gx_own)
    gather.start()
    exchange.own().start()
    exchange.start(*range(1, 8))
    own_o = pltpu.make_async_copy(wo_piece_ref, o_all.block(dp), wo_own)
    own_d = pltpu.make_async_copy(wd_piece_ref, d_all.block(dp), wd_own)
    own_d.start()

    @pl.when(stays)
    def _():
        own_o.start()

    @pl.when(jnp.logical_not(stays))
    def _():
        turned_copy().start()

    gain_two = two_ref[...]
    for s in range(8):
        for half, weight_ref in ((0, wg_ref), (F, wu_ref)):
            units = [
                weight_ref[:, pl.ds((d * 8 + s) * down_rows, down_rows)].astype(f32) * gain_two
                for d in range(4)
            ]
            units.append(jnp.zeros((rows, F - 4 * down_rows), f32))
            gu_ref[s, :, half : half + F] = jnp.concatenate(units, axis=1).astype(bf16)
    wd[4 * down_rows :, :] = jnp.zeros((F - 4 * down_rows, wd.shape[1]), bf16)
    exchange_gu.own().start()
    exchange.ready()
    w_all.start()
    gather.own_ready()
    gather.hop(1)

    @pl.when(stays)
    def _():
        own_o.wait()

    @pl.when(jnp.logical_not(stays))
    def _():
        landed().wait_recv()

    w_all.relay()
    o_all.start()
    d_all.start()
    w_all.ready()
    U = 2 * T
    lane = lax.broadcasted_iota(jnp.int32, (U, 128), 1)
    low_lanes = lane < HEAD
    front = lane % HEAD < HEAD // 2
    scale = HEAD ** (-0.5)

    def swapped(u):
        return jnp.where(front, pltpu.roll(u, 128 - HEAD // 2, 1), pltpu.roll(u, HEAD // 2, 1))

    def project(i, carry):
        for h in (2, 3):

            @pl.when(i == h - 1)
            def _():
                gather.hop(h)

        @pl.when(i == 2)
        def _():
            gather_dy.start()
            exchange_gu.start(1, 2)

        u = line_rank(i, z)
        gather.pair_ready(u)
        r = pl.ds(pl.multiple_of(u * U, U), U)
        qkv = mm(s1_all[r, :], wqkv[...])
        cos, sin = cos_ref[r, :], sin_ref[r, :]

        def roped(tile):
            return tile * cos + swapped(tile) * sin

        for h in range(0, heads, 2):
            turned = roped(qkv[:, h * HEAD : (h + 2) * HEAD])
            other = swapped(turned)
            q_out[h, r, :] = jnp.where(low_lanes, turned, pltpu.roll(other, HEAD, 1)).astype(bf16)
            q_out[h + 1, r, :] = jnp.where(low_lanes, pltpu.roll(turned, HEAD, 1), other).astype(bf16)
        tile = qkv[:, heads * HEAD :]
        turned = roped(tile)
        k2_ref[r, :] = jnp.where(low_lanes, turned, pltpu.roll(swapped(turned), HEAD, 1)).astype(bf16)
        kz_ref[r, :] = jnp.where(low_lanes, turned, 0.0).astype(bf16)
        vz_ref[r, :] = jnp.where(low_lanes, pltpu.roll(tile, HEAD, 1), 0.0).astype(bf16)
        return carry

    lax.fori_loop(0, 4, project, 0)
    o_all.relay()
    o_all.ready()
    d_all.relay()
    gather_dy.own_ready()

    def unit(i, carry):
        for h in range(1, 4):

            @pl.when(i == h)
            def _():
                gather_dy.hop(h)

        for k in range(3):

            @pl.when(i == k)
            def _():
                exchange_gu.start(*range(2 * k + 3, min(2 * k + 5, 8)))

        u = line_rank(3 - i, z)
        r = pl.ds(pl.multiple_of(u * U, U), U)
        q = q_out[:, r, :].reshape(heads * U, 128)

        def scores(j, top):
            c = pl.ds(pl.multiple_of(j * U, U), U)
            s = mm_nt(q, kz_ref[c, :]) * scale
            row = lax.broadcasted_iota(jnp.int32, (heads, U, U), 1).reshape(heads * U, U)
            col = lax.broadcasted_iota(jnp.int32, (heads * U, U), 1)
            s = jnp.where(col + (j - u) * U <= row, s, masked)
            score[j] = s
            return jnp.maximum(top, jnp.max(s, axis=1, keepdims=True))

        top = lax.fori_loop(0, u + 1, scores, jnp.full((heads * U, 1), masked, f32))

        def weigh(j, carry):
            total, out = carry
            c = pl.ds(pl.multiple_of(j * U, U), U)
            p = jnp.exp(score[j] - top)
            return (
                total + jnp.sum(p, axis=1, keepdims=True),
                out + mm(p.astype(bf16), vz_ref[c, :]),
            )

        total, out = lax.fori_loop(
            0,
            u + 1,
            weigh,
            (jnp.zeros((heads * U, 1), f32), jnp.zeros((heads * U, 128), f32)),
        )
        lse_ref[:, r, :] = (top + jnp.log(total)).reshape(heads, U, 1)
        out = out / total
        for h in range(0, heads, 2):
            first, second = out[h * U : (h + 1) * U], out[(h + 1) * U : (h + 2) * U]
            att_ref[r, h * HEAD : (h + 2) * HEAD] = jnp.where(
                low_lanes, first, pltpu.roll(second, HEAD, 1)
            ).astype(bf16)
        part[r, :] = mm(att_ref[r, :], wo[...]).astype(bf16)
        scatter.start(u)
        for k in (1, 2):

            @pl.when(i == k)
            def _():
                scatter.pass_on(line_rank(4 - k, z))

        return carry

    lax.fori_loop(0, 4, unit, 0)
    exchange_gu.ready()
    g_all.start()
    scatter.pass_on(line_rank(1, z))
    scatter.finish(mid_ref)
    g_all.relay()
    for zz in range(4):
        gather.finish_one(zz)
        gather_dy.pair_ready(zz)
        gather_dy.finish_one(zz)
    exchange.finish()
    exchange_gu.finish()
    w_all.finish()
    o_all.finish()
    own_d.wait()
    d_all.ready()
    d_all.finish()

    @pl.when(jnp.logical_not(stays))
    def _():
        turned_copy().wait_send()

    g_all.ready()
    g_all.finish()


def attention_front(s1, weights, gains, wo_piece, wd_piece, dy, cos, sin, F, repeats, cid=5):
    T, width = s1.shape
    S = lax.axis_size("seq")
    heads, rows = H // S, wo_piece.shape[0]
    L, q_cols, U = S * T, heads * HEAD, 2 * T
    cols = q_cols + 2 * HEAD
    vmem = pl.BlockSpec(memory_space=pltpu.VMEM)
    return pl.pallas_call(
        functools.partial(attention_front_kernel, T, heads, repeats),
        out_shape=(
            jax.ShapeDtypeStruct((T, width), f32),
            jax.ShapeDtypeStruct((L, width), bf16),
            jax.ShapeDtypeStruct((L, width), bf16),
            jax.ShapeDtypeStruct((width, cols), bf16),
            jax.ShapeDtypeStruct((width, 2 * F), bf16),
            jax.ShapeDtypeStruct((F, width), bf16),
            jax.ShapeDtypeStruct((q_cols, width), bf16),
            jax.ShapeDtypeStruct((heads, L, 128), bf16),
            jax.ShapeDtypeStruct((L, 128), bf16),
            jax.ShapeDtypeStruct((L, 128), bf16),
            jax.ShapeDtypeStruct((L, 128), bf16),
            jax.ShapeDtypeStruct((heads, L, 1), f32),
            jax.ShapeDtypeStruct((L, q_cols), bf16),
        ),
        in_specs=[vmem] * 13,
        out_specs=(vmem,) * 13,
        scratch_shapes=[
            pltpu.VMEM((L // U, heads * U, U), f32),
            pltpu.VMEM((L, width), bf16),
            pltpu.VMEM((S, rows, cols), bf16),
            pltpu.VMEM((S, rows, 2 * F), bf16),
        ]
        + line_sems(4)
        + line_sems(4)
        + sum_scratch(T, width)
        + [pltpu.SemaphoreType.DMA((3,))] * 8
        + [pltpu.SemaphoreType.DMA((8,))] * 4
        + [pltpu.SemaphoreType.DMA] * 6,
        compiler_params=pltpu.CompilerParams(
            collective_id=cid, has_side_effects=True, vmem_limit_bytes=67000000
        ),
        name="attention_front",
    )(s1, *weights, *gains, wo_piece, wd_piece, dy, cos, sin)


def attention_back_kernel(
    T, heads, dm_ref, q_ref, k_ref, kz_ref, vz_ref, lse_ref, att_ref, s1_ref, wqkv_ref, wo_ref, table_ref, ggu_ref,
    e1_ref, got_ref, go_ref, got_gu_ref,
    full, grads, probs, dprobs, dk, dv, dqkv, part, gqkv, go_part, gsum,
    up_sem, dn_sem, ag_y, ag_r, own_sem,
    ybuf, rbuf, y_s, y_r, z_s, z_r,
    qa, qb, qa_s, qa_r, qb_s, qb_r,
    oa, ob, oa_s, oa_r, ob_s, ob_r,
    ex_s, ex_r, gx_s, gx_r, ex_own, gx_own,
):
    z, y = seq_place()
    me = z * 2 + y
    dp = lax.axis_index("dp")
    rows = got_ref.shape[1]
    barrier = pltpu.get_barrier_semaphore()
    for step in range(1, 8):
        hello(barrier, (me + step) % 8, "seq")
    hello(barrier, dp + 1 - 2 * (dp % 2), "dp")
    hello(barrier, dp + 2 - 4 * (dp // 2), "dp")
    pl.semaphore_wait(barrier, 9)
    gather = Gather(z, y, T, dm_ref, full, up_sem, dn_sem, ag_y, ag_r, own_sem)
    scatter = Scatter(z, y, T, part, ybuf, rbuf, y_s, y_r, z_s, z_r)
    sum_qkv = DpSum(gqkv, gqkv.shape[0] // 4, qa, qb, qa_s, qa_r, qb_s, qb_r)
    sum_o = DpSum(go_part, go_part.shape[0] // 4, oa, ob, oa_s, oa_r, ob_s, ob_r)
    exchange = Exchange(
        me, lambda p: rows_of(gsum, p * rows, rows), lambda p: got_ref.at[p], ex_s, ex_r, ex_own
    )
    exchange_gu = Exchange(
        me, lambda p: rows_of(ggu_ref, p * rows, rows), lambda p: got_gu_ref.at[p], gx_s, gx_r, gx_own
    )
    gather.start()
    exchange_gu.own().start()
    dk[...] = jnp.zeros_like(dk)
    dv[...] = jnp.zeros_like(dv)
    gather.own_ready()
    U = 2 * T
    low_lanes = lax.broadcasted_iota(jnp.int32, (U, 128), 1) < HEAD
    scale = HEAD ** (-0.5)

    def both(product, table):
        turned = product * table
        return turned + pltpu.roll(turned, HEAD, 1)

    def unit(i, carry):
        for h in range(1, 4):

            @pl.when(i == h - 1)
            def _():
                gather.hop(h)

        @pl.when(i == 2)
        def _():
            exchange_gu.start(1, 2, 3)

        @pl.when(i == 3)
        def _():
            exchange_gu.start(4, 5, 6, 7)

        u = line_rank(i, z)
        gather.pair_ready(u)
        r = pl.ds(pl.multiple_of(u * U, U), U)
        d_att = mm_nt(full[r, :], wo_ref[...]).astype(bf16)
        for h in range(heads):
            grads[h] = d_att[:, h * 128 : (h + 1) * 128]
        g = grads[...].reshape(heads * U, 128)
        q = q_ref[:, r, :].reshape(heads * U, 128)
        lse = lse_ref[:, r, :].reshape(heads * U, 1)

        def scores(j, inner):
            c = pl.ds(pl.multiple_of(j * U, U), U)
            s = mm_nt(q, kz_ref[c, :]) * scale
            row = lax.broadcasted_iota(jnp.int32, (heads, U, U), 1).reshape(heads * U, U)
            col = lax.broadcasted_iota(jnp.int32, (heads * U, U), 1)
            s = jnp.where(col + (j - u) * U <= row, s, masked)
            p = jnp.exp(s - lse)
            dp_ = mm_nt(g, vz_ref[c, :])
            probs[j] = p
            dprobs[j] = dp_
            return inner + jnp.sum(p * dp_, axis=1, keepdims=True)

        inner = lax.fori_loop(0, u + 1, scores, jnp.zeros((heads * U, 1), f32))

        def products(j, dq):
            c = pl.ds(pl.multiple_of(j * U, U), U)
            p = probs[j]
            ds = (p * (dprobs[j] - inner)).astype(bf16)
            dk[c, :] += mm_tn(ds, q)
            dv[c, :] += mm_tn(p.astype(bf16), g)
            return dq + mm(ds, k_ref[c, :])

        dq = lax.fori_loop(0, u + 1, products, jnp.zeros((heads * U, 128), f32))
        table = table_ref[r, :]
        for h in range(0, heads, 2):
            first = both(dq[h * U : (h + 1) * U], table)
            second = both(dq[(h + 1) * U : (h + 2) * U], table)
            dqkv[r, h * HEAD : (h + 2) * HEAD] = jnp.where(low_lanes, first, second).astype(bf16)
        return carry

    lax.fori_loop(0, 4, unit, 0)

    def part_rows(i):
        u = line_rank(i, z)
        r = pl.ds(pl.multiple_of(u * U, U), U)
        d_key = both(dk[r, :], table_ref[r, :])
        dqkv[r, heads * HEAD :] = jnp.where(low_lanes, d_key, pltpu.roll(dv[r, :], HEAD, 1)).astype(bf16)
        part[r, :] = mm_nt(dqkv[r, :], wqkv_ref[...]).astype(bf16)
        scatter.start(u)

    def part_loop(i, carry):
        part_rows(3 - i)
        return carry

    lax.fori_loop(0, 4, part_loop, 0)

    def qkv_tile(i, carry):
        r = pl.ds(pl.multiple_of(i * 256, 256), 256)
        gqkv[r, :] = mm_tn(s1_ref[:, r], dqkv[...]).astype(bf16)
        return carry

    lax.fori_loop(0, gqkv.shape[0] // 256, qkv_tile, 0)
    sum_qkv.start()
    scatter.pass_on(line_rank(3, z))
    sum_qkv.middle()
    go_part[...] = mm_tn(att_ref[...], full[...]).astype(bf16)
    sum_o.start()
    scatter.pass_on(line_rank(2, z))
    sum_qkv.finish(gsum)

    exchange.own().start()
    exchange.start(*range(1, 8))
    sum_o.middle()
    scatter.pass_on(line_rank(1, z))
    sum_o.finish(go_ref)
    scatter.finish(e1_ref)
    for moved in (exchange, exchange_gu):
        moved.ready()
        moved.finish()
    gather.finish()


def attention_back(dm, q2, k2, kz, vz, lse, attended, s1_all, w_qkv, w_o2, table, g_gu, rows, cid=4):
    T, width = dm.shape
    heads, L, _ = q2.shape
    cols = w_qkv.shape[1]
    vmem = pl.BlockSpec(memory_space=pltpu.VMEM)
    U = 2 * T
    return pl.pallas_call(
        functools.partial(attention_back_kernel, T, heads),
        out_shape=(
            jax.ShapeDtypeStruct((T, width), f32),
            jax.ShapeDtypeStruct((8, rows, cols), bf16),
            jax.ShapeDtypeStruct((rows, width), f32),
            jax.ShapeDtypeStruct((8, rows, g_gu.shape[1]), bf16),
        ),
        in_specs=[vmem] * 12,
        out_specs=(vmem,) * 4,
        scratch_shapes=[
            pltpu.VMEM((L, width), bf16),
            pltpu.VMEM((heads, U, 128), bf16),
            pltpu.VMEM((L // U, heads * U, U), f32),
            pltpu.VMEM((L // U, heads * U, U), f32),
            pltpu.VMEM((L, 128), f32),
            pltpu.VMEM((L, 128), f32),
            pltpu.VMEM((L, cols), bf16),
            pltpu.VMEM((L, width), bf16),
            pltpu.VMEM((width, cols), bf16),
            pltpu.VMEM((heads * HEAD, width), bf16),
            pltpu.VMEM((width // 4, cols), bf16),
        ]
        + line_sems(4)
        + sum_scratch(T, width)
        + dp_scratch(width // 4, cols)
        + dp_scratch(rows, width)
        + [pltpu.SemaphoreType.DMA((8,))] * 4
        + [pltpu.SemaphoreType.DMA] * 2,
        compiler_params=pltpu.CompilerParams(
            collective_id=cid, has_side_effects=True, vmem_limit_bytes=67000000
        ),
        name="attention_back",
    )(dm, q2, k2, kz, vz, lse, attended, s1_all, w_qkv, w_o2, table, g_gu)


def spread_kernel(
    down_rows, repeats, gu_ref, qkv_ref, wg_ref, wu_ref, wq_ref, wk_ref, wv_ref, one_ref, two_ref,
    gate_ref, up_ref, query_ref, key_ref, value_ref, gain1_ref, gain2_ref,
):
    S, rows, wide = gu_ref.shape
    F = wide // 2
    Dp = gate_ref.shape[1] // (S * down_rows)
    q_cols = query_ref.shape[1] // S
    for s in range(S):
        for d in range(Dp):
            to = pl.ds((d * S + s) * down_rows, down_rows)
            gate_ref[:, to] = gu_ref[s, :, d * down_rows : (d + 1) * down_rows].astype(f32)
            up_ref[:, to] = gu_ref[s, :, F + d * down_rows : F + (d + 1) * down_rows].astype(f32)
        query_ref[:, s * q_cols : (s + 1) * q_cols] = qkv_ref[s, :, :q_cols].astype(f32)
    for j in range(S // repeats):
        total = qkv_ref[j * repeats, :, q_cols:].astype(f32)
        for s in range(j * repeats + 1, (j + 1) * repeats):
            total = total + qkv_ref[s, :, q_cols:].astype(f32)
        key_ref[:, j * HEAD : (j + 1) * HEAD] = total[:, :HEAD]
        value_ref[:, j * HEAD : (j + 1) * HEAD] = total[:, HEAD:]

    def close(pairs, gain_ref, out_ref):
        total = jnp.zeros((rows, 1), f32)
        for weight_ref, grad_ref in pairs:
            grad = grad_ref[...]
            total = total + jnp.sum(weight_ref[...].astype(f32) * grad, axis=1, keepdims=True)
            grad_ref[...] = grad * gain_ref[...]
        out_ref[...] = total

    close(((wg_ref, gate_ref), (wu_ref, up_ref)), two_ref, gain2_ref)
    close(((wq_ref, query_ref), (wk_ref, key_ref), (wv_ref, value_ref)), one_ref, gain1_ref)


def spread(gu, qkv, weights, gains, down_rows, repeats):
    rows = gu.shape[1]
    outs = [jax.ShapeDtypeStruct(w.shape, f32) for w in weights]
    outs += [jax.ShapeDtypeStruct((rows, 1), f32)] * 2
    vmem = pl.BlockSpec(memory_space=pltpu.VMEM)
    return pl.pallas_call(
        functools.partial(spread_kernel, down_rows, repeats),
        out_shape=tuple(outs),
        in_specs=[vmem] * 9,
        out_specs=(vmem,) * 7,
        compiler_params=pltpu.CompilerParams(vmem_limit_bytes=40 << 20),
        name="spread",
    )(gu, qkv, *weights, *gains)


def gather_seq(rows):
    if lax.axis_size("seq") == 8:
        return gather_line(rows)
    return lax.all_gather(rows, "seq", axis=0, tiled=True)


def scatter_seq(rows):
    if lax.axis_size("seq") == 8:
        return scatter_line(rows)
    return lax.psum_scatter(rows, "seq", scatter_dimension=0, tiled=True).astype(f32)


def feedforward_plain(x, dy_all, w_gu, w_d):
    hidden = w_d.shape[0]
    s2_all = gather_seq(x)
    gate_up = mm(s2_all, w_gu)
    gate, up = gate_up[:, :hidden], gate_up[:, hidden:]
    sig = jax.nn.sigmoid(gate)
    hid = (gate * sig * up).astype(bf16)
    d_hid = mm_nt(dy_all, w_d)
    d_gate = (d_hid * up * sig * (1.0 + gate * (1.0 - sig))).astype(bf16)
    d_up = (d_hid * (gate * sig)).astype(bf16)
    d_gu = jnp.concatenate([d_gate, d_up], axis=1)
    return (
        scatter_seq(mm(hid, w_d).astype(bf16)),
        scatter_seq(mm_nt(d_gu, w_gu).astype(bf16)),
        scatter_dp(mm_tn(s2_all, d_gu).astype(bf16)),
        scatter_dp(mm_tn(hid, dy_all).astype(bf16)).astype(f32),
    )


def gather_dp(rows):
    return lax.all_gather(rows, "dp", axis=0, tiled=True)


def scatter_dp(rows):
    return lax.psum_scatter(rows, "dp", scatter_dimension=0, tiled=True)


def exchange_seq(pieces):
    return lax.all_to_all(pieces, "seq", split_axis=0, concat_axis=0, tiled=True)


def causal_mask(offset, block_rows, block_end):
    return jnp.arange(block_end)[None, :] <= (offset + jnp.arange(block_rows))[:, None]


def attention_forward(queries, keys, values, block_rows):
    outputs, totals = [], []
    for offset in range(0, queries.shape[1], block_rows):
        end = offset + block_rows
        scores = jnp.einsum(
            "hqd,kd->hqk", queries[:, offset:end], keys[:end], preferred_element_type=f32
        ) * HEAD ** (-0.5)
        scores = jnp.where(causal_mask(offset, block_rows, end), scores, masked)
        row_max = jnp.max(scores, axis=-1, keepdims=True)
        total = row_max + jnp.log(jnp.sum(jnp.exp(scores - row_max), axis=-1, keepdims=True))
        probs_low = jnp.exp(scores - total).astype(bf16)
        outputs.append(
            jnp.einsum("hqk,kd->hqd", probs_low, values[:end], preferred_element_type=f32).astype(
                bf16
            )
        )
        totals.append(total)
    return jnp.concatenate(outputs, axis=1), jnp.concatenate(totals, axis=1)


def attention_backward(queries, keys, values, grads, totals, block_rows):
    length = keys.shape[0]
    scale = HEAD ** (-0.5)
    key_sum = jnp.zeros((length, HEAD), f32)
    value_sum = jnp.zeros((length, HEAD), f32)
    query_parts = []
    for offset in range(0, length, block_rows):
        end = offset + block_rows
        query_block, grad_block = queries[:, offset:end], grads[:, offset:end]
        key_block, value_block = keys[:end], values[:end]
        scores = (
            jnp.einsum("hqd,kd->hqk", query_block, key_block, preferred_element_type=f32) * scale
        )
        scores = jnp.where(causal_mask(offset, block_rows, end), scores, masked)
        probs = jnp.exp(scores - totals[:, offset:end])
        probs_low = probs.astype(bf16)
        grad_probs = jnp.einsum(
            "hqd,kd->hqk", grad_block, value_block, preferred_element_type=f32
        )
        inner = jnp.sum(probs * grad_probs, axis=-1, keepdims=True)
        grad_scores = (probs * (grad_probs - inner)).astype(bf16)
        query_parts.append(
            jnp.einsum("hqk,kd->hqd", grad_scores, key_block, preferred_element_type=f32) * scale
        )
        padding = ((0, length - end), (0, 0))
        key_sum = key_sum + jnp.pad(
            jnp.einsum("hqk,hqd->kd", grad_scores, query_block, preferred_element_type=f32)
            * scale,
            padding,
        )
        value_sum = value_sum + jnp.pad(
            jnp.einsum("hqk,hqd->kd", probs_low, grad_block, preferred_element_type=f32), padding
        )
    return jnp.concatenate(query_parts, axis=1), key_sum, value_sum


def heads_first(flat, heads):
    return jnp.transpose(flat.reshape(flat.shape[0], heads, HEAD), (1, 0, 2))


def heads_last(stacked):
    return jnp.transpose(stacked, (1, 0, 2)).reshape(stacked.shape[1], -1)


def shards(
    inputs,
    attention_gain,
    query_weight,
    key_weight,
    value_weight,
    output_weight,
    feedforward_gain,
    gate_weight,
    up_weight,
    down_weight,
    cotangent,
):
    S, Dp = lax.axis_size("seq"), lax.axis_size("dp")
    sequences, tokens, width = inputs.shape
    length = tokens * S
    rows = query_weight.shape[0]
    heads = H // S
    q_cols = heads * HEAD
    repeats = S // KV
    down_rows = down_weight.shape[0]
    hidden = down_rows * Dp
    block_rows = min(length, max(512, length // 8))

    gain_one = attention_gain.astype(f32)[:, None]
    gain_two = feedforward_gain.astype(f32)[:, None]

    def folded(weight, gain):
        return (weight.astype(f32) * gain).astype(bf16)

    def per_group_kv(weight):
        return jnp.repeat(weight.reshape(rows, KV, HEAD), repeats, axis=1)

    def per_group_hidden(weight):
        return jnp.transpose(weight.reshape(rows, Dp, S, down_rows), (2, 0, 1, 3)).reshape(
            S, rows, hidden
        )

    packed = jnp.concatenate(
        [
            folded(query_weight, gain_one).reshape(rows, S, q_cols),
            per_group_kv(folded(key_weight, gain_one)),
            per_group_kv(folded(value_weight, gain_one)),
        ],
        axis=2,
    )
    packed_qkv = jnp.transpose(packed, (1, 0, 2))
    forward_perm = [(Dp * s + d, d * S + s) for s in range(S) for d in range(Dp)]
    backward_perm = [(b, a) for a, b in forward_perm]
    line = S == 8 and Dp == 4
    width_f = -(-hidden // 256) * 256 if line else hidden

    def padded(part, axis):
        pads = [(0, 0)] * part.ndim
        pads[axis] = (0, width_f - hidden)
        return jnp.pad(part, pads)

    packed_gu = jnp.concatenate(
        [
            padded(per_group_hidden(folded(gate_weight, gain_two)), 2),
            padded(per_group_hidden(folded(up_weight, gain_two)), 2),
        ],
        axis=2,
    )

    flat = inputs.reshape(tokens, width).astype(f32)
    r1 = rms_scale(flat)
    s1 = flat * r1
    cosine, sine = rope_tables(length)
    dy = cotangent.reshape(tokens, width)
    if line:
        lane = jnp.arange(128)[None, :]
        frequency = 10000.0 ** (-((lane % (HEAD // 2)).astype(f32) * 2.0) / HEAD)
        angles = jnp.arange(length, dtype=f32)[:, None] * frequency
        turn_cos = jnp.cos(angles)
        turn_sin = jnp.where(lane % HEAD < HEAD // 2, -1.0, 1.0) * jnp.sin(angles)
        outs = attention_front(
            s1.astype(bf16),
            (query_weight, key_weight, value_weight, gate_weight, up_weight),
            (gain_one, gain_two),
            output_weight,
            down_weight,
            dy,
            turn_cos,
            turn_sin,
            width_f,
            repeats,
        )
        summed, s1_all, dy_all, w_qkv, w_gu, w_d, w_o, q2, k2, kz, vz, totals, attended = outs
    else:
        w_qkv = gather_dp(exchange_seq(packed_qkv).reshape(S * rows, q_cols + 2 * HEAD))
        w_gu = gather_dp(exchange_seq(packed_gu).reshape(S * rows, 2 * hidden))
        w_o = gather_dp(lax.ppermute(output_weight, ("dp", "seq"), forward_perm))
        w_d = gather_dp(down_weight)
        s1_all = gather_seq(s1.astype(bf16))
        qkv = mm(s1_all, w_qkv)
        queries = rotate(qkv[:, :q_cols].reshape(length, heads, HEAD), cosine, sine).astype(bf16)
        queries = jnp.transpose(queries, (1, 0, 2))
        keys = rotate(qkv[:, None, q_cols : q_cols + HEAD], cosine, sine).astype(bf16)[:, 0]
        values = qkv[:, q_cols + HEAD :].astype(bf16)
        attended, totals = attention_forward(queries, keys, values, block_rows)
        attended = heads_last(attended)
        summed = scatter_seq(mm(attended, w_o).astype(bf16))
        dy_all = gather_seq(dy)
    middle = flat + summed
    r2 = rms_scale(middle)
    s2 = middle * r2
    if line:
        out_sum, e2, g_gu, down_grad = feedforward(
            s2.astype(bf16), dy_all, w_gu, w_d, down_rows
        )
    else:
        out_sum, e2, g_gu, down_grad = feedforward_plain(s2.astype(bf16), dy_all, w_gu, w_d)

    d_middle = dy.astype(f32) + r2 * (e2 - s2 * jnp.mean(e2 * s2, axis=-1, keepdims=True))
    if line:
        table = jnp.where(lane < HEAD, turn_cos, -turn_sin) * HEAD ** (-0.5)

        def with_zeros(u):
            return jnp.concatenate([u, jnp.zeros_like(u)], axis=-1)

        w_o2 = with_zeros(w_o.reshape(heads, 1, HEAD, width).swapaxes(2, 3)).swapaxes(2, 3)
        e1, g_qkv, g_o, g_gu = attention_back(
            d_middle.astype(bf16),
            q2,
            k2,
            kz,
            vz,
            totals,
            attended,
            s1_all,
            w_qkv,
            w_o2.reshape(2 * q_cols, width),
            table,
            g_gu,
            rows,
        )
        g_o = g_o.astype(bf16)
    else:
        g_gu = exchange_seq(g_gu.reshape(S, rows, 2 * width_f))
        dm_all = gather_seq(d_middle.astype(bf16))
        d_att = heads_first(mm_nt(dm_all, w_o).astype(bf16), heads)
        d_q, d_k, d_v = attention_backward(queries, keys, values, d_att, totals, block_rows)
        d_q = jnp.transpose(d_q, (1, 0, 2))
        d_qkv = jnp.concatenate(
            [
                rotate(d_q, cosine, -sine).reshape(length, q_cols).astype(bf16),
                rotate(d_k[:, None], cosine, -sine)[:, 0].astype(bf16),
                d_v.astype(bf16),
            ],
            axis=1,
        )
        e1 = scatter_seq(mm_nt(d_qkv, w_qkv).astype(bf16))
        g_o = scatter_dp(mm_tn(attended, dm_all).astype(bf16))
        g_qkv = scatter_dp(mm_tn(s1_all, d_qkv).astype(bf16))
        g_qkv = exchange_seq(g_qkv.reshape(S, rows, q_cols + 2 * HEAD))
    output = (middle + out_sum).astype(bf16)
    input_grad = d_middle + r1 * (e1 - s1 * jnp.mean(e1 * s1, axis=-1, keepdims=True))
    output_grad = lax.ppermute(g_o, ("dp", "seq"), backward_perm).astype(f32)

    if line:
        g_gate, g_up, g_query, g_key, g_value, gain_one_grad, gain_two_grad = spread(
            g_gu,
            g_qkv,
            (gate_weight, up_weight, query_weight, key_weight, value_weight),
            (gain_one, gain_two),
            down_rows,
            repeats,
        )
        return (
            output.reshape(sequences, tokens, width),
            input_grad.reshape(sequences, tokens, width),
            gain_one_grad[:, 0],
            g_query,
            g_key,
            g_value,
            output_grad,
            gain_two_grad[:, 0],
            g_gate,
            g_up,
            down_grad,
        )

    g_gu, g_qkv = g_gu.astype(f32), g_qkv.astype(f32)

    def back_hidden(part):
        return jnp.transpose(part.reshape(S, rows, Dp, down_rows), (1, 2, 0, 3)).reshape(rows, -1)

    def back_kv(part):
        part = jnp.sum(part.reshape(KV, repeats, rows, HEAD), axis=1)
        return jnp.transpose(part, (1, 0, 2)).reshape(rows, KV * HEAD)

    g_gate, g_up = back_hidden(g_gu[..., :hidden]), back_hidden(g_gu[..., hidden:])
    g_query = jnp.transpose(g_qkv[..., :q_cols], (1, 0, 2)).reshape(rows, width)
    g_key = back_kv(g_qkv[..., q_cols : q_cols + HEAD])
    g_value = back_kv(g_qkv[..., q_cols + HEAD :])

    def row_dot(weight, grad):
        return jnp.sum(weight.astype(f32) * grad, axis=1)

    gain_two_grad = row_dot(gate_weight, g_gate) + row_dot(up_weight, g_up)
    gain_one_grad = (
        row_dot(query_weight, g_query) + row_dot(key_weight, g_key) + row_dot(value_weight, g_value)
    )
    return (
        output.reshape(sequences, tokens, width),
        input_grad.reshape(sequences, tokens, width),
        gain_one_grad,
        g_query * gain_one,
        g_key * gain_one,
        g_value * gain_one,
        output_grad,
        gain_two_grad,
        g_gate * gain_two,
        g_up * gain_two,
        down_grad,
    )


def solution(mesh):
    both = ("dp", "seq")
    tok, vec, mat = P("dp", "seq", None), P(both), P(both, None)
    in_specs = (tok, vec, mat, mat, mat, mat, vec, mat, mat, mat, tok)
    out_specs = (tok, tok, vec, mat, mat, mat, mat, vec, mat, mat, mat)
    return jax.shard_map(shards, mesh=mesh, in_specs=in_specs, out_specs=out_specs, check_vma=False)
```

```python
import functools

import jax
import jax.numpy as jnp
from jax import lax
from jax.experimental import pallas as pl
from jax.experimental.pallas import tpu as pltpu
from jax.sharding import PartitionSpec as P

H = 32
KV = 4
HEAD = 64

epsilon = 1e-05
masked = -1e30
f32 = jnp.float32
bf16 = jnp.bfloat16


def rope_tables(length):
    half_width = HEAD // 2
    frequency = 10000.0 ** (-(jnp.arange(half_width, dtype=f32) * 2.0) / HEAD)
    angles = jnp.arange(length, dtype=f32)[:, None] * frequency[None, :]
    return (jnp.cos(angles)[:, None, :], jnp.sin(angles)[:, None, :])


def rotate(values, cosine, sine):
    front, back = values[..., : HEAD // 2], values[..., HEAD // 2 :]
    return jnp.concatenate([front * cosine - back * sine, back * cosine + front * sine], axis=-1)


def rms_scale(values):
    return lax.rsqrt(jnp.mean(values * values, axis=-1, keepdims=True) + epsilon)


def mm(a, b):
    return lax.dot_general(a, b, (((1,), (0,)), ((), ())), preferred_element_type=f32)


def mm_nt(a, b):
    return lax.dot_general(a, b, (((1,), (1,)), ((), ())), preferred_element_type=f32)


def mm_tn(a, b):
    return lax.dot_general(a, b, (((0,), (0,)), ((), ())), preferred_element_type=f32)


def seq_place():
    me = lax.axis_index("seq")
    return me // 2, me % 2

def hello(barrier, peer, axis):
    pl.semaphore_signal(
        barrier, inc=1, device_id={axis: peer}, device_id_type=pl.DeviceIdType.MESH
    )


def greet(z, y, Z, dp=None):
    barrier = pltpu.get_barrier_semaphore()
    hello(barrier, z * 2 + 1 - y, "seq")

    @pl.when(z > 0)
    def _():
        hello(barrier, z * 2 + y - 2, "seq")

    @pl.when(z < Z - 1)
    def _():
        hello(barrier, z * 2 + y + 2, "seq")

    count = 1 + (z + Z - 1) // Z + (2 * Z - 2 - z) // Z
    if dp is not None:
        hello(barrier, dp + 1 - 2 * (dp % 2), "dp")
        hello(barrier, dp + 2 - 4 * (dp // 2), "dp")
        count = count + 2
    pl.semaphore_wait(barrier, count)


def send(src, dst, ssem, rsem, peer, axis="seq"):
    return pltpu.make_async_remote_copy(
        src_ref=src,
        dst_ref=dst,
        send_sem=ssem,
        recv_sem=rsem,
        device_id={axis: peer},
        device_id_type=pl.DeviceIdType.MESH,
    )


def gather_kernel(Z, T, x_ref, out_ref, up_sem, dn_sem, y_sem, recv_sem, own_sem):
    z, y = seq_place()
    greet(z, y, Z)
    def block(zz, yy):
        return out_ref.at[pl.ds(pl.multiple_of((zz * 2 + yy) * T, T), T)]
    def copy(src, zz, sem, peer):
        return send(src, block(zz, y), sem.at[zz], recv_sem.at[zz * 2 + y], peer)
    own = pltpu.make_async_copy(x_ref, block(z, y), own_sem)
    own.start()
    peer_y, peer_up, peer_dn = z * 2 + 1 - y, z * 2 + y + 2, z * 2 + y - 2
    copy(x_ref, z, y_sem, peer_y).start()
    @pl.when(z < Z - 1)
    def _(): copy(x_ref, z, up_sem, peer_up).start()
    @pl.when(z > 0)
    def _(): copy(x_ref, z, dn_sem, peer_dn).start()
    for h in range(1, Z):
        @pl.when(z >= h)
        def _():
            zz = z - h
            copy(block(zz, y), zz, y_sem, peer_y).wait_recv()
            @pl.when(z < Z - 1)
            def _(): copy(block(zz, y), zz, up_sem, peer_up).start()
            copy(block(zz, y), zz, y_sem, peer_y).start()
        @pl.when(z + h < Z)
        def _():
            zz = z + h
            copy(block(zz, y), zz, y_sem, peer_y).wait_recv()
            @pl.when(z > 0)
            def _(): copy(block(zz, y), zz, dn_sem, peer_dn).start()
            copy(block(zz, y), zz, y_sem, peer_y).start()
    own.wait()
    for zz in range(Z):
        b = block(zz, 1 - y)
        send(b, b, y_sem.at[zz], recv_sem.at[zz * 2 + 1 - y], peer_y).wait_recv()
        c = copy(block(zz, y), zz, y_sem, peer_y)
        c.wait_send()
        @pl.when((zz <= z) & (z < Z - 1))
        def _(): copy(block(zz, y), zz, up_sem, peer_up).wait_send()
        @pl.when((zz >= z) & (z > 0))
        def _(): copy(block(zz, y), zz, dn_sem, peer_dn).wait_send()

def gather_line(x, cid=1):
    S = lax.axis_size("seq"); Z = S // 2
    T, D = x.shape
    return pl.pallas_call(
        functools.partial(gather_kernel, Z, T),
        out_shape=jax.ShapeDtypeStruct((S * T, D), x.dtype),
        in_specs=[pl.BlockSpec(memory_space=pltpu.VMEM)],
        out_specs=pl.BlockSpec(memory_space=pl.ANY),
        scratch_shapes=[pltpu.SemaphoreType.DMA((Z,))] * 3 + [pltpu.SemaphoreType.DMA((S,)), pltpu.SemaphoreType.DMA],
        compiler_params=pltpu.CompilerParams(collective_id=cid, has_side_effects=True),
        name="gather_seq",
    )(x)

def scatter_kernel(Z, T, p_ref, out_ref, ybuf, upbuf, dnbuf, upst, dnst, up_s, dn_s, y_s, up_r, dn_r, y_r):
    z, y = seq_place()
    greet(z, y, Z)
    peer_y, peer_up, peer_dn = z * 2 + 1 - y, z * 2 + y + 2, z * 2 + y - 2
    def mine(zz, yy):
        return p_ref.at[pl.ds(pl.multiple_of((zz * 2 + yy) * T, T), T)]
    def y_copy(zz):
        return send(mine(zz, 1 - y), ybuf.at[zz], y_s.at[zz], y_r.at[zz], peer_y)
    def up_copy(zz):
        return send(upst.at[zz], upbuf.at[zz], up_s.at[zz], up_r.at[zz], peer_up)
    def dn_copy(zz):
        return send(dnst.at[zz], dnbuf.at[zz], dn_s.at[zz], dn_r.at[zz], peer_dn)
    for h in range(Z - 1, 0, -1):
        @pl.when(z + h < Z)
        def _(): y_copy(z + h).start()
        @pl.when(z - h >= 0)
        def _(): y_copy(z - h).start()
    y_copy(z).start()
    for h in range(Z - 1, 0, -1):
        @pl.when(z + h < Z)
        def _():
            d = z + h
            y_copy(d).wait_recv()
            upst[d] = (mine(d, y)[...].astype(f32) + ybuf[d].astype(f32)).astype(bf16)
            @pl.when(z > 0)
            def _():
                up_copy(d).wait_recv()
                upst[d] = (mine(d, y)[...].astype(f32) + ybuf[d].astype(f32) + upbuf[d].astype(f32)).astype(bf16)
            up_copy(d).start()
        @pl.when(z - h >= 0)
        def _():
            d = z - h
            y_copy(d).wait_recv()
            dnst[d] = (mine(d, y)[...].astype(f32) + ybuf[d].astype(f32)).astype(bf16)
            @pl.when(z < Z - 1)
            def _():
                dn_copy(d).wait_recv()
                dnst[d] = (mine(d, y)[...].astype(f32) + ybuf[d].astype(f32) + dnbuf[d].astype(f32)).astype(bf16)
            dn_copy(d).start()
    y_copy(z).wait_recv()
    out_ref[...] = mine(z, y)[...].astype(f32) + ybuf[z].astype(f32)
    @pl.when(z > 0)
    def _():
        up_copy(z).wait_recv()
        out_ref[...] += upbuf[z].astype(f32)
    @pl.when(z < Z - 1)
    def _():
        dn_copy(z).wait_recv()
        out_ref[...] += dnbuf[z].astype(f32)
    for zz in range(Z):
        y_copy(zz).wait_send()
        @pl.when(zz > z)
        def _(): up_copy(zz).wait_send()
        @pl.when(zz < z)
        def _(): dn_copy(zz).wait_send()

def scatter_line(p, cid=2):
    S = lax.axis_size("seq"); Z = S // 2
    L, D = p.shape; T = L // S
    return pl.pallas_call(
        functools.partial(scatter_kernel, Z, T),
        out_shape=jax.ShapeDtypeStruct((T, D), f32),
        in_specs=[pl.BlockSpec(memory_space=pltpu.VMEM)],
        out_specs=pl.BlockSpec(memory_space=pltpu.VMEM),
        scratch_shapes=[pltpu.VMEM((Z, T, D), bf16)] * 5 + [pltpu.SemaphoreType.DMA((Z,))] * 6,
        compiler_params=pltpu.CompilerParams(collective_id=cid, has_side_effects=True, vmem_limit_bytes=60 << 20),
        name="scatter_seq",
    )(p)


def line_rank(i, z):
    upper = z // 2
    inner = (z + upper) % 2
    base = i + inner * (1 - i // 2) * (1 - 2 * i)
    return base + upper * (3 - 2 * base)


def above(d, z):
    return (d - z + 3) // 4


def rows_of(ref, start, size):
    return ref.at[pl.ds(pl.multiple_of(start, size), size)]


def in_chunks(rows, chunk, step):
    def body(i, carry):
        step(pl.ds(pl.multiple_of(i * chunk, chunk), chunk))
        return carry

    lax.fori_loop(0, rows // chunk, body, 0)


class Gather:
    def __init__(self, z, y, T, own, full, up_sem, dn_sem, y_sem, recv_sem, own_sem):
        self.z, self.y, self.T, self.own, self.full = z, y, T, own, full
        self.sems = {"up": up_sem, "dn": dn_sem, "y": y_sem}
        self.peers = {"up": z * 2 + y + 2, "dn": z * 2 + y - 2, "y": z * 2 + 1 - y}
        self.recv_sem, self.own_sem = recv_sem, own_sem

    def block(self, zz, yy):
        return rows_of(self.full, (zz * 2 + yy) * self.T, self.T)

    def copy(self, src, zz, way):
        return send(
            src,
            self.block(zz, self.y),
            self.sems[way].at[zz],
            self.recv_sem.at[zz * 2 + self.y],
            self.peers[way],
        )

    def start(self):
        z = self.z
        pltpu.make_async_copy(self.own, self.block(z, self.y), self.own_sem).start()
        self.copy(self.own, z, "y").start()

        @pl.when(z < 3)
        def _():
            self.copy(self.own, z, "up").start()

        @pl.when(z > 0)
        def _():
            self.copy(self.own, z, "dn").start()

    def own_ready(self):
        pltpu.make_async_copy(self.own, self.block(self.z, self.y), self.own_sem).wait()

    def hop(self, h):
        z = self.z

        @pl.when(z >= h)
        def _():
            src = self.block(z - h, self.y)
            self.copy(src, z - h, "y").wait_recv()

            @pl.when(z < 3)
            def _():
                self.copy(src, z - h, "up").start()

            self.copy(src, z - h, "y").start()

        @pl.when(z + h < 4)
        def _():
            src = self.block(z + h, self.y)
            self.copy(src, z + h, "y").wait_recv()

            @pl.when(z > 0)
            def _():
                self.copy(src, z + h, "dn").start()

            self.copy(src, z + h, "y").start()

    def pair_ready(self, zz):
        b = self.block(zz, 1 - self.y)
        send(
            b, b, self.sems["y"].at[zz], self.recv_sem.at[zz * 2 + 1 - self.y], self.peers["y"]
        ).wait_recv()

    def finish_one(self, zz):
        z = self.z
        src = self.block(zz, self.y)
        self.copy(src, zz, "y").wait_send()

        @pl.when((zz <= z) & (z < 3))
        def _():
            self.copy(src, zz, "up").wait_send()

        @pl.when((zz >= z) & (z > 0))
        def _():
            self.copy(src, zz, "dn").wait_send()

    def finish(self):
        for zz in range(4):
            self.finish_one(zz)


class Scatter:
    def __init__(self, z, y, T, part, ybuf, rbuf, y_s, y_r, z_s, z_r):
        self.z, self.y, self.T, self.part = z, y, T, part
        self.ybuf, self.rbuf = ybuf, rbuf
        self.y_s, self.y_r, self.z_s, self.z_r = y_s, y_r, z_s, z_r

    def rows(self, zz, yy):
        return rows_of(self.part, (zz * 2 + yy) * self.T, self.T)

    def y_copy(self, d):
        peer = self.z * 2 + 1 - self.y
        return send(
            self.rows(d, 1 - self.y), self.ybuf.at[d], self.y_s.at[d], self.y_r.at[d], peer
        )

    def z_copy(self, d, up):
        slot = d + up
        peer = self.z * 2 + self.y + 4 * up - 2
        return send(self.ybuf.at[d], self.rbuf.at[slot], self.z_s.at[d], self.z_r.at[slot], peer)

    def start(self, d):
        self.y_copy(d).start()

    def pass_on(self, d):
        z = self.z
        up = above(d, z)
        self.y_copy(d).wait_recv()
        mine, slot = self.rows(d, self.y), self.ybuf.at[d]
        inner = (z > 0) & (z < 3)

        @pl.when(inner)
        def _():
            self.z_copy(d, up).wait_recv()
            far = self.rbuf.at[d + up]

            def step(c):
                slot[c] = (
                    mine[c].astype(f32) + slot[c].astype(f32) + far[c].astype(f32)
                ).astype(bf16)

            in_chunks(self.T, 32, step)

        @pl.when(jnp.logical_not(inner))
        def _():
            def step(c):
                slot[c] = (mine[c].astype(f32) + slot[c].astype(f32)).astype(bf16)

            in_chunks(self.T, 32, step)

        self.z_copy(d, up).start()

    def finish(self, out_ref):
        z = self.z
        self.y_copy(z).wait_recv()
        mine, slot = self.rows(z, self.y), self.ybuf.at[z]

        def first(c):
            out_ref[c] = mine[c].astype(f32) + slot[c].astype(f32)

        in_chunks(self.T, 32, first)

        def more(slot):
            def step(c):
                out_ref[c] += slot[c].astype(f32)

            in_chunks(self.T, 32, step)

        @pl.when(z > 0)
        def _():
            self.z_copy(z, 1).wait_recv()
            more(self.rbuf.at[z + 1])

        @pl.when(z < 3)
        def _():
            self.z_copy(z, 0).wait_recv()
            more(self.rbuf.at[z])

        for d in range(4):
            self.y_copy(d).wait_send()

            @pl.when(z != d)
            def _():
                self.z_copy(d, above(d, z)).wait_send()


def line_sems(n):
    return [pltpu.SemaphoreType.DMA((4,))] * 3 + [
        pltpu.SemaphoreType.DMA((8,)),
        pltpu.SemaphoreType.DMA,
    ]


def sum_scratch(T, width):
    return [
        pltpu.VMEM((4, T, width), bf16),
        pltpu.VMEM((5, T, width), bf16),
        pltpu.SemaphoreType.DMA((4,)),
        pltpu.SemaphoreType.DMA((4,)),
        pltpu.SemaphoreType.DMA((4,)),
        pltpu.SemaphoreType.DMA((5,)),
    ]


class DpSum:
    def __init__(self, src, size, abuf, bbuf, a_s, a_r, b_s, b_r):
        dp = lax.axis_index("dp")
        self.core, self.far = dp % 2, dp // 2
        self.partner, self.across = dp + 1 - 2 * (dp % 2), dp + 2 - 4 * (dp // 2)
        self.src, self.size = src, size
        self.abuf, self.bbuf = abuf, bbuf
        self.a_s, self.a_r, self.b_s, self.b_r = a_s, a_r, b_s, b_r

    def rows(self, d):
        return rows_of(self.src, d * self.size, self.size)

    def a_copy(self, j):
        return send(
            self.rows(2 * j + 1 - self.core),
            self.abuf.at[j],
            self.a_s.at[j],
            self.a_r.at[j],
            self.partner,
            "dp",
        )

    def b_copy(self):
        return send(self.abuf.at[1 - self.far], self.bbuf, self.b_s, self.b_r, self.across, "dp")

    def start(self):
        self.a_copy(0).start()
        self.a_copy(1).start()

    def middle(self):
        self.a_copy(0).wait_recv()
        self.a_copy(1).wait_recv()
        j = 1 - self.far
        mine, slot = self.rows(2 * j + self.core), self.abuf.at[j]

        def step(c):
            slot[c] = (mine[c].astype(f32) + slot[c].astype(f32)).astype(bf16)

        in_chunks(self.size, 16, step)
        self.b_copy().start()

    def finish(self, out_ref):
        self.b_copy().wait_recv()
        mine, slot = self.rows(2 * self.far + self.core), self.abuf.at[self.far]

        def step(c):
            out_ref[c] = (
                mine[c].astype(f32) + slot[c].astype(f32) + self.bbuf[c].astype(f32)
            ).astype(out_ref.dtype)

        in_chunks(self.size, 16, step)
        self.a_copy(0).wait_send()
        self.a_copy(1).wait_send()
        self.b_copy().wait_send()


class Exchange:
    def __init__(self, me, src, landing, s_sem, r_sem, own_sem):
        self.me, self.src, self.landing = me, src, landing
        self.s_sem, self.r_sem, self.own_sem = s_sem, r_sem, own_sem

    def own(self):
        return pltpu.make_async_copy(self.src(self.me), self.landing(self.me), self.own_sem)

    def copy(self, peer, sender):
        return send(
            self.src(peer), self.landing(sender), self.s_sem.at[peer], self.r_sem.at[sender], peer
        )

    def start(self, *steps):
        for step in steps:
            self.copy((self.me + step) % 8, self.me).start()

    def ready(self):
        self.own().wait()
        for step in range(1, 8):
            peer = (self.me + step) % 8
            self.copy(peer, peer).wait_recv()

    def finish(self):
        for step in range(1, 8):
            self.copy((self.me + step) % 8, self.me).wait_send()


class DpGather:
    def __init__(self, own, full, size, s_sem, r_sem):
        dp = lax.axis_index("dp")
        self.dp, self.partner, self.across = dp, dp + 1 - 2 * (dp % 2), dp + 2 - 4 * (dp // 2)
        self.diagonal = 3 - dp
        self.own, self.full, self.size = own, full, size
        self.s_sem, self.r_sem = s_sem, r_sem

    def block(self, d):
        return rows_of(self.full, d * self.size, self.size)

    def copy(self, src, d, k, peer):
        return send(src, self.block(d), self.s_sem.at[k], self.r_sem.at[k], peer, "dp")

    def start(self):
        self.copy(self.own, self.dp, 0, self.across).start()
        self.copy(self.own, self.dp, 1, self.partner).start()

    def relay(self):
        far = self.block(self.across)
        self.copy(far, self.across, 0, self.across).wait_recv()
        self.copy(far, self.across, 2, self.partner).start()

    def ready(self):
        near, diagonal = self.block(self.partner), self.block(self.diagonal)
        self.copy(near, self.partner, 1, self.partner).wait_recv()
        self.copy(diagonal, self.diagonal, 2, self.partner).wait_recv()

    def finish(self):
        self.copy(self.own, self.dp, 0, self.across).wait_send()
        self.copy(self.own, self.dp, 1, self.partner).wait_send()
        self.copy(self.block(self.across), self.across, 2, self.partner).wait_send()


def dp_scratch(size, width):
    return [
        pltpu.VMEM((2, size, width), bf16),
        pltpu.VMEM((size, width), bf16),
        pltpu.SemaphoreType.DMA((2,)),
        pltpu.SemaphoreType.DMA((2,)),
        pltpu.SemaphoreType.DMA,
        pltpu.SemaphoreType.DMA,
    ]


def feedforward_kernel(
    T, x_ref, dy_ref, wgu_ref, wd_ref, out_ref, e2_ref, ggu_ref, gd_ref,
    full, hid, dgu, pout, part, ggu, gdown, up_sem, dn_sem, ag_y, ag_r, own_sem,
    pybuf, prbuf, py_s, py_r, pz_s, pz_r,
    ybuf, rbuf, y_s, y_r, z_s, z_r,
    ga, gb, ga_s, ga_r, gb_s, gb_r,
    da, db, da_s, da_r, db_s, db_r,
):
    z, y = seq_place()
    dp = lax.axis_index("dp")
    F = hid.shape[1]
    greet(z, y, 4, dp)
    gather = Gather(z, y, T, x_ref, full, up_sem, dn_sem, ag_y, ag_r, own_sem)
    scatter_out = Scatter(z, y, T, pout, pybuf, prbuf, py_s, py_r, pz_s, pz_r)
    scatter = Scatter(z, y, T, part, ybuf, rbuf, y_s, y_r, z_s, z_r)
    sum_gu = DpSum(ggu, ggu.shape[0] // 4, ga, gb, ga_s, ga_r, gb_s, gb_r)
    sum_down = DpSum(gdown, gd_ref.shape[0], da, db, da_s, da_r, db_s, db_r)
    gather.start()
    gather.own_ready()
    inner = (z > 0) & (z < 3)
    at_end = jnp.logical_not(inner)

    def pass_on(rank):
        scatter_out.pass_on(line_rank(rank, z))
        scatter.pass_on(line_rank(rank, z))

    def compute(i, carry):
        for h in range(1, 4):

            @pl.when(i == h - 1)
            def _():
                gather.hop(h)

        zz = line_rank(i, z)
        gather.pair_ready(zz)

        @pl.when(i == 2)
        def _():
            scatter_out.start(line_rank(1, z))

        @pl.when((i == 3) & at_end)
        def _():
            scatter_out.pass_on(line_rank(1, z))

        r = pl.ds(pl.multiple_of(zz * 2 * T, 2 * T), 2 * T)
        gu = mm(full[r, :], wgu_ref[...])
        gate, up = gu[:, :F], gu[:, F:]
        sig = 1.0 / (1.0 + jnp.exp(-gate))
        act = gate * sig
        hid[r, :] = (act * up).astype(bf16)
        dh = mm_nt(dy_ref[r, :], wd_ref[...])
        dgu[r, :F] = (dh * up * sig * (1.0 + gate * (1.0 - sig))).astype(bf16)
        dgu[r, F:] = (dh * act).astype(bf16)
        pout[r, :] = mm(hid[r, :], wd_ref[...]).astype(bf16)

        @pl.when(i >= 2)
        def _():
            scatter_out.start(zz)

        part[r, :] = mm_nt(dgu[r, :], wgu_ref[...]).astype(bf16)

        @pl.when(i == 2)
        def _():
            scatter.start(zz)

        return carry

    lax.fori_loop(0, 4, compute, 0)
    scatter.start(line_rank(3, z))
    scatter.start(line_rank(1, z))
    scatter_out.start(z)
    scatter.start(z)

    def gate_up_tile(i, carry):
        @pl.when((i == 4) & at_end)
        def _():
            pass_on(2)

        r = pl.ds(pl.multiple_of(i * 256, 256), 256)
        ggu[r, :] = mm_tn(full[:, r], dgu[...]).astype(bf16)
        return carry

    def down_tile(i, carry):
        r = pl.ds(pl.multiple_of(i * 256, 256), 256)
        gdown[r, :] = mm_tn(hid[:, r], dy_ref[...]).astype(bf16)
        return carry

    lax.fori_loop(0, 8, gate_up_tile, 0)
    sum_gu.start()
    pass_on(3 - (z + 1) % 4 // 2)
    lax.fori_loop(0, F // 256, down_tile, 0)
    sum_down.start()

    @pl.when(inner)
    def _():
        pass_on(3)

    sum_gu.middle()

    @pl.when(inner)
    def _():
        scatter_out.pass_on(line_rank(1, z))

    scatter.pass_on(line_rank(1, z))
    sum_down.middle()
    sum_gu.finish(ggu_ref)
    sum_down.finish(gd_ref)
    scatter_out.finish(out_ref)
    scatter.finish(e2_ref)
    gather.finish()


def feedforward(x, dy_all, w_gu, w_d, down_rows, cid=3):
    T, width = x.shape
    L, F = dy_all.shape[0], w_d.shape[0]
    vmem = pl.BlockSpec(memory_space=pltpu.VMEM)
    return pl.pallas_call(
        functools.partial(feedforward_kernel, T),
        out_shape=(
            jax.ShapeDtypeStruct((T, width), f32),
            jax.ShapeDtypeStruct((T, width), f32),
            jax.ShapeDtypeStruct((width // 4, 2 * F), bf16),
            jax.ShapeDtypeStruct((down_rows, width), f32),
        ),
        in_specs=[vmem] * 4,
        out_specs=(vmem,) * 4,
        scratch_shapes=[
            pltpu.VMEM((L, width), bf16),
            pltpu.VMEM((L, F), bf16),
            pltpu.VMEM((L, 2 * F), bf16),
            pltpu.VMEM((L, width), bf16),
            pltpu.VMEM((L, width), bf16),
            pltpu.VMEM((width, 2 * F), bf16),
            pltpu.VMEM((F, width), bf16),
        ]
        + line_sems(4)
        + sum_scratch(T, width)
        + sum_scratch(T, width)
        + dp_scratch(width // 4, 2 * F)
        + dp_scratch(down_rows, width),
        compiler_params=pltpu.CompilerParams(
            collective_id=cid, has_side_effects=True, vmem_limit_bytes=67000000
        ),
        name="feedforward",
    )(x, dy_all, w_gu, w_d)


def attention_front_kernel(
    T, heads, repeats, s1_ref, wq_ref, wk_ref, wv_ref, wg_ref, wu_ref, one_ref, two_ref,
    wo_piece_ref, wd_piece_ref, dy_ref, cos_ref, sin_ref,
    mid_ref, s1_all, dy_all, wqkv, wgu, wd, wo, q_out, k2_ref, kz_ref, vz_ref, lse_ref, att_ref,
    score, part, piece_ref, gu_ref,
    up_sem, dn_sem, ag_y, ag_r, own_sem,
    up_sem2, dn_sem2, ag_y2, ag_r2, own_sem2,
    ybuf, rbuf, y_s, y_r, z_s, z_r,
    w_s, w_r, o_s, o_r, g_s, g_r, d_s, d_r, ex_s, ex_r, gx_s, gx_r, ex_own, gx_own, wo_own, wd_own, turn_s, turn_r,
):
    z, y = seq_place()
    me = z * 2 + y
    dp = lax.axis_index("dp")
    rows, out_rows, down_rows = piece_ref.shape[1], wo_piece_ref.shape[0], wd_piece_ref.shape[0]
    q_cols, F = heads * HEAD, gu_ref.shape[2] // 2
    here, there = dp * 8 + me, me * 4 + dp
    stays = here == there
    barrier = pltpu.get_barrier_semaphore()

    def greet_at(place):
        pl.semaphore_signal(
            barrier,
            inc=1,
            device_id={"dp": place[0], "seq": place[1]},
            device_id_type=pl.DeviceIdType.MESH,
        )

    for step in range(1, 8):
        hello(barrier, (me + step) % 8, "seq")
    hello(barrier, dp + 1 - 2 * (dp % 2), "dp")
    hello(barrier, dp + 2 - 4 * (dp // 2), "dp")

    @pl.when(jnp.logical_not(stays))
    def _():
        greet_at((here % 4, here // 4))
        greet_at((there // 8, there % 8))

    gain = one_ref[...]
    for s in range(8):
        kv = pl.ds(s // repeats * HEAD, HEAD)
        q = wq_ref[:, s * q_cols : (s + 1) * q_cols].astype(f32) * gain
        k, v = wk_ref[:, kv].astype(f32) * gain, wv_ref[:, kv].astype(f32) * gain
        piece_ref[s, :, :q_cols] = q.astype(bf16)
        piece_ref[s, :, q_cols:] = jnp.concatenate([k, v], axis=1).astype(bf16)

    @pl.when(stays)
    def _():
        pl.semaphore_wait(barrier, 9)

    @pl.when(jnp.logical_not(stays))
    def _():
        pl.semaphore_wait(barrier, 11)

    gather = Gather(z, y, T, s1_ref, s1_all, up_sem, dn_sem, ag_y, ag_r, own_sem)
    gather_dy = Gather(z, y, T, dy_ref, dy_all, up_sem2, dn_sem2, ag_y2, ag_r2, own_sem2)
    scatter = Scatter(z, y, T, part, ybuf, rbuf, y_s, y_r, z_s, z_r)
    w_own = rows_of(wqkv, dp * 8 * rows, 8 * rows)
    w_all = DpGather(w_own, wqkv, 8 * rows, w_s, w_r)
    o_all = DpGather(rows_of(wo, dp * out_rows, out_rows), wo, out_rows, o_s, o_r)
    d_all = DpGather(wd_piece_ref, wd, down_rows, d_s, d_r)

    def turned_copy():
        return pltpu.make_async_remote_copy(
            src_ref=wo_piece_ref,
            dst_ref=rows_of(wo, here % 4 * out_rows, out_rows),
            send_sem=turn_s,
            recv_sem=turn_r,
            device_id={"dp": here % 4, "seq": here // 4},
            device_id_type=pl.DeviceIdType.MESH,
        )

    def landed():
        mine = o_all.block(dp)
        return pltpu.make_async_remote_copy(
            src_ref=mine,
            dst_ref=mine,
            send_sem=turn_s,
            recv_sem=turn_r,
            device_id={"dp": here % 4, "seq": here // 4},
            device_id_type=pl.DeviceIdType.MESH,
        )

    g_own = rows_of(wgu, dp * 8 * rows, 8 * rows)
    g_all = DpGather(g_own, wgu, 8 * rows, g_s, g_r)

    def pieces(src, full, *sems):
        return Exchange(
            me, lambda p: src.at[p], lambda p: rows_of(full, (dp * 8 + p) * rows, rows), *sems
        )

    exchange = pieces(piece_ref, wqkv, ex_s, ex_r, ex_own)
    exchange_gu = pieces(gu_ref, wgu, gx_s, gx_r, gx_own)
    gather.start()
    exchange.own().start()
    exchange.start(*range(1, 8))
    own_o = pltpu.make_async_copy(wo_piece_ref, o_all.block(dp), wo_own)
    own_d = pltpu.make_async_copy(wd_piece_ref, d_all.block(dp), wd_own)
    own_d.start()

    @pl.when(stays)
    def _():
        own_o.start()

    @pl.when(jnp.logical_not(stays))
    def _():
        turned_copy().start()

    gain_two = two_ref[...]
    for s in range(8):
        for half, weight_ref in ((0, wg_ref), (F, wu_ref)):
            units = [
                weight_ref[:, pl.ds((d * 8 + s) * down_rows, down_rows)].astype(f32) * gain_two
                for d in range(4)
            ]
            units.append(jnp.zeros((rows, F - 4 * down_rows), f32))
            gu_ref[s, :, half : half + F] = jnp.concatenate(units, axis=1).astype(bf16)
    wd[4 * down_rows :, :] = jnp.zeros((F - 4 * down_rows, wd.shape[1]), bf16)
    exchange_gu.own().start()
    exchange.ready()
    w_all.start()
    gather.own_ready()
    gather.hop(1)

    @pl.when(stays)
    def _():
        own_o.wait()

    @pl.when(jnp.logical_not(stays))
    def _():
        landed().wait_recv()

    w_all.relay()
    o_all.start()
    d_all.start()
    w_all.ready()
    U = 2 * T
    lane = lax.broadcasted_iota(jnp.int32, (U, 128), 1)
    low_lanes = lane < HEAD
    front = lane % HEAD < HEAD // 2
    scale = HEAD ** (-0.5)

    def swapped(u):
        return jnp.where(front, pltpu.roll(u, 128 - HEAD // 2, 1), pltpu.roll(u, HEAD // 2, 1))

    def project(i, carry):
        for h in (2, 3):

            @pl.when(i == h - 1)
            def _():
                gather.hop(h)

        @pl.when(i == 2)
        def _():
            gather_dy.start()
            exchange_gu.start(1, 2)

        u = line_rank(i, z)
        gather.pair_ready(u)
        r = pl.ds(pl.multiple_of(u * U, U), U)
        qkv = mm(s1_all[r, :], wqkv[...])
        cos, sin = cos_ref[r, :], sin_ref[r, :]

        def roped(tile):
            return tile * cos + swapped(tile) * sin

        for h in range(0, heads, 2):
            turned = roped(qkv[:, h * HEAD : (h + 2) * HEAD])
            other = swapped(turned)
            q_out[h, r, :] = jnp.where(low_lanes, turned, pltpu.roll(other, HEAD, 1)).astype(bf16)
            q_out[h + 1, r, :] = jnp.where(low_lanes, pltpu.roll(turned, HEAD, 1), other).astype(bf16)
        tile = qkv[:, heads * HEAD :]
        turned = roped(tile)
        k2_ref[r, :] = jnp.where(low_lanes, turned, pltpu.roll(swapped(turned), HEAD, 1)).astype(bf16)
        kz_ref[r, :] = jnp.where(low_lanes, turned, 0.0).astype(bf16)
        vz_ref[r, :] = jnp.where(low_lanes, pltpu.roll(tile, HEAD, 1), 0.0).astype(bf16)

        @pl.when(i == 3)
        def _():
            exchange_gu.start(3, 4, 5)

        return carry

    lax.fori_loop(0, 4, project, 0)
    o_all.relay()
    o_all.ready()
    d_all.relay()
    gather_dy.own_ready()

    def unit(i, carry):
        for h in range(1, 4):

            @pl.when(i == h)
            def _():
                gather_dy.hop(h)

        @pl.when(i == 0)
        def _():
            exchange_gu.start(6, 7)

        @pl.when(i == 3)
        def _():
            exchange_gu.ready()
            g_all.start()

        u = line_rank(3 - i, z)
        r = pl.ds(pl.multiple_of(u * U, U), U)
        q = q_out[:, r, :].reshape(heads * U, 128)

        def scores(j, top):
            c = pl.ds(pl.multiple_of(j * U, U), U)
            s = mm_nt(q, kz_ref[c, :]) * scale
            row = lax.broadcasted_iota(jnp.int32, (heads, U, U), 1).reshape(heads * U, U)
            col = lax.broadcasted_iota(jnp.int32, (heads * U, U), 1)
            s = jnp.where(col + (j - u) * U <= row, s, masked)
            score[j] = s
            return jnp.maximum(top, jnp.max(s, axis=1, keepdims=True))

        top = lax.fori_loop(0, u + 1, scores, jnp.full((heads * U, 1), masked, f32))

        def weigh(j, carry):
            total, out = carry
            c = pl.ds(pl.multiple_of(j * U, U), U)
            p = jnp.exp(score[j] - top)
            return (
                total + jnp.sum(p, axis=1, keepdims=True),
                out + mm(p.astype(bf16), vz_ref[c, :]),
            )

        total, out = lax.fori_loop(
            0,
            u + 1,
            weigh,
            (jnp.zeros((heads * U, 1), f32), jnp.zeros((heads * U, 128), f32)),
        )
        lse_ref[:, r, :] = (top + jnp.log(total)).reshape(heads, U, 1)
        out = out / total
        for h in range(0, heads, 2):
            first, second = out[h * U : (h + 1) * U], out[(h + 1) * U : (h + 2) * U]
            att_ref[r, h * HEAD : (h + 2) * HEAD] = jnp.where(
                low_lanes, first, pltpu.roll(second, HEAD, 1)
            ).astype(bf16)
        part[r, :] = mm(att_ref[r, :], wo[...]).astype(bf16)
        scatter.start(u)
        for k in (1, 2):

            @pl.when(i == k)
            def _():
                scatter.pass_on(line_rank(4 - k, z))

        return carry

    lax.fori_loop(0, 4, unit, 0)
    scatter.pass_on(line_rank(1, z))
    scatter.finish(mid_ref)
    g_all.relay()
    for zz in range(4):
        gather.finish_one(zz)
        gather_dy.pair_ready(zz)
        gather_dy.finish_one(zz)
    exchange.finish()
    exchange_gu.finish()
    w_all.finish()
    o_all.finish()
    own_d.wait()
    d_all.ready()
    d_all.finish()

    @pl.when(jnp.logical_not(stays))
    def _():
        turned_copy().wait_send()

    g_all.ready()
    g_all.finish()


def attention_front(s1, weights, gains, wo_piece, wd_piece, dy, cos, sin, F, repeats, cid=5):
    T, width = s1.shape
    S = lax.axis_size("seq")
    heads, rows = H // S, wo_piece.shape[0]
    L, q_cols, U = S * T, heads * HEAD, 2 * T
    cols = q_cols + 2 * HEAD
    vmem = pl.BlockSpec(memory_space=pltpu.VMEM)
    return pl.pallas_call(
        functools.partial(attention_front_kernel, T, heads, repeats),
        out_shape=(
            jax.ShapeDtypeStruct((T, width), f32),
            jax.ShapeDtypeStruct((L, width), bf16),
            jax.ShapeDtypeStruct((L, width), bf16),
            jax.ShapeDtypeStruct((width, cols), bf16),
            jax.ShapeDtypeStruct((width, 2 * F), bf16),
            jax.ShapeDtypeStruct((F, width), bf16),
            jax.ShapeDtypeStruct((q_cols, width), bf16),
            jax.ShapeDtypeStruct((heads, L, 128), bf16),
            jax.ShapeDtypeStruct((L, 128), bf16),
            jax.ShapeDtypeStruct((L, 128), bf16),
            jax.ShapeDtypeStruct((L, 128), bf16),
            jax.ShapeDtypeStruct((heads, L, 1), f32),
            jax.ShapeDtypeStruct((L, q_cols), bf16),
        ),
        in_specs=[vmem] * 13,
        out_specs=(vmem,) * 13,
        scratch_shapes=[
            pltpu.VMEM((L // U, heads * U, U), f32),
            pltpu.VMEM((L, width), bf16),
            pltpu.VMEM((S, rows, cols), bf16),
            pltpu.VMEM((S, rows, 2 * F), bf16),
        ]
        + line_sems(4)
        + line_sems(4)
        + sum_scratch(T, width)
        + [pltpu.SemaphoreType.DMA((3,))] * 8
        + [pltpu.SemaphoreType.DMA((8,))] * 4
        + [pltpu.SemaphoreType.DMA] * 6,
        compiler_params=pltpu.CompilerParams(
            collective_id=cid, has_side_effects=True, vmem_limit_bytes=67000000
        ),
        name="attention_front",
    )(s1, *weights, *gains, wo_piece, wd_piece, dy, cos, sin)


def attention_back_kernel(
    T, heads, dm_ref, q_ref, k_ref, kz_ref, vz_ref, lse_ref, att_ref, s1_ref, wqkv_ref, wo_ref, table_ref, ggu_ref,
    e1_ref, got_ref, go_ref, got_gu_ref,
    full, grads, probs, dprobs, dk, dv, dqkv, part, gqkv, go_part, gsum,
    up_sem, dn_sem, ag_y, ag_r, own_sem,
    ybuf, rbuf, y_s, y_r, z_s, z_r,
    qa, qb, qa_s, qa_r, qb_s, qb_r,
    oa, ob, oa_s, oa_r, ob_s, ob_r,
    ex_s, ex_r, gx_s, gx_r, ex_own, gx_own,
):
    z, y = seq_place()
    me = z * 2 + y
    dp = lax.axis_index("dp")
    rows = got_ref.shape[1]
    barrier = pltpu.get_barrier_semaphore()
    for step in range(1, 8):
        hello(barrier, (me + step) % 8, "seq")
    hello(barrier, dp + 1 - 2 * (dp % 2), "dp")
    hello(barrier, dp + 2 - 4 * (dp // 2), "dp")
    pl.semaphore_wait(barrier, 9)
    gather = Gather(z, y, T, dm_ref, full, up_sem, dn_sem, ag_y, ag_r, own_sem)
    scatter = Scatter(z, y, T, part, ybuf, rbuf, y_s, y_r, z_s, z_r)
    sum_qkv = DpSum(gqkv, gqkv.shape[0] // 4, qa, qb, qa_s, qa_r, qb_s, qb_r)
    sum_o = DpSum(go_part, go_part.shape[0] // 4, oa, ob, oa_s, oa_r, ob_s, ob_r)
    exchange = Exchange(
        me, lambda p: rows_of(gsum, p * rows, rows), lambda p: got_ref.at[p], ex_s, ex_r, ex_own
    )
    exchange_gu = Exchange(
        me, lambda p: rows_of(ggu_ref, p * rows, rows), lambda p: got_gu_ref.at[p], gx_s, gx_r, gx_own
    )
    gather.start()
    exchange_gu.own().start()
    dk[...] = jnp.zeros_like(dk)
    dv[...] = jnp.zeros_like(dv)
    gather.own_ready()
    U = 2 * T
    low_lanes = lax.broadcasted_iota(jnp.int32, (U, 128), 1) < HEAD
    scale = HEAD ** (-0.5)

    def both(product, table):
        turned = product * table
        return turned + pltpu.roll(turned, HEAD, 1)

    def unit(i, carry):
        for h in range(1, 4):

            @pl.when(i == h - 1)
            def _():
                gather.hop(h)

        @pl.when(i == 2)
        def _():
            exchange_gu.start(1, 2, 3)

        @pl.when(i == 3)
        def _():
            exchange_gu.start(4, 5, 6, 7)

        u = line_rank(i, z)
        gather.pair_ready(u)
        r = pl.ds(pl.multiple_of(u * U, U), U)
        d_att = mm_nt(full[r, :], wo_ref[...]).astype(bf16)
        for h in range(heads):
            grads[h] = d_att[:, h * 128 : (h + 1) * 128]
        g = grads[...].reshape(heads * U, 128)
        q = q_ref[:, r, :].reshape(heads * U, 128)
        lse = lse_ref[:, r, :].reshape(heads * U, 1)

        def scores(j, inner):
            c = pl.ds(pl.multiple_of(j * U, U), U)
            s = mm_nt(q, kz_ref[c, :]) * scale
            row = lax.broadcasted_iota(jnp.int32, (heads, U, U), 1).reshape(heads * U, U)
            col = lax.broadcasted_iota(jnp.int32, (heads * U, U), 1)
            s = jnp.where(col + (j - u) * U <= row, s, masked)
            p = jnp.exp(s - lse)
            dp_ = mm_nt(g, vz_ref[c, :])
            probs[j] = p
            dprobs[j] = dp_
            return inner + jnp.sum(p * dp_, axis=1, keepdims=True)

        inner = lax.fori_loop(0, u + 1, scores, jnp.zeros((heads * U, 1), f32))

        def products(j, dq):
            c = pl.ds(pl.multiple_of(j * U, U), U)
            p = probs[j]
            ds = (p * (dprobs[j] - inner)).astype(bf16)
            dk[c, :] += mm_tn(ds, q)
            dv[c, :] += mm_tn(p.astype(bf16), g)
            return dq + mm(ds, k_ref[c, :])

        dq = lax.fori_loop(0, u + 1, products, jnp.zeros((heads * U, 128), f32))
        table = table_ref[r, :]
        for h in range(0, heads, 2):
            first = both(dq[h * U : (h + 1) * U], table)
            second = both(dq[(h + 1) * U : (h + 2) * U], table)
            dqkv[r, h * HEAD : (h + 2) * HEAD] = jnp.where(low_lanes, first, second).astype(bf16)
        return carry

    lax.fori_loop(0, 4, unit, 0)

    def part_rows(i):
        u = line_rank(i, z)
        r = pl.ds(pl.multiple_of(u * U, U), U)
        d_key = both(dk[r, :], table_ref[r, :])
        dqkv[r, heads * HEAD :] = jnp.where(low_lanes, d_key, pltpu.roll(dv[r, :], HEAD, 1)).astype(bf16)
        part[r, :] = mm_nt(dqkv[r, :], wqkv_ref[...]).astype(bf16)
        scatter.start(u)

    def part_loop(i, carry):
        part_rows(3 - i)
        return carry

    lax.fori_loop(0, 4, part_loop, 0)

    def qkv_tile(i, carry):
        r = pl.ds(pl.multiple_of(i * 256, 256), 256)
        gqkv[r, :] = mm_tn(s1_ref[:, r], dqkv[...]).astype(bf16)
        return carry

    lax.fori_loop(0, gqkv.shape[0] // 256, qkv_tile, 0)
    sum_qkv.start()
    scatter.pass_on(line_rank(3, z))
    sum_qkv.middle()
    go_part[...] = mm_tn(att_ref[...], full[...]).astype(bf16)
    sum_o.start()
    scatter.pass_on(line_rank(2, z))
    sum_qkv.finish(gsum)

    exchange.own().start()
    exchange.start(*range(1, 8))
    sum_o.middle()
    scatter.pass_on(line_rank(1, z))
    sum_o.finish(go_ref)
    scatter.finish(e1_ref)
    for moved in (exchange, exchange_gu):
        moved.ready()
        moved.finish()
    gather.finish()


def attention_back(dm, q2, k2, kz, vz, lse, attended, s1_all, w_qkv, w_o2, table, g_gu, rows, cid=4):
    T, width = dm.shape
    heads, L, _ = q2.shape
    cols = w_qkv.shape[1]
    vmem = pl.BlockSpec(memory_space=pltpu.VMEM)
    U = 2 * T
    return pl.pallas_call(
        functools.partial(attention_back_kernel, T, heads),
        out_shape=(
            jax.ShapeDtypeStruct((T, width), f32),
            jax.ShapeDtypeStruct((8, rows, cols), bf16),
            jax.ShapeDtypeStruct((rows, width), bf16),
            jax.ShapeDtypeStruct((8, rows, g_gu.shape[1]), bf16),
        ),
        in_specs=[vmem] * 12,
        out_specs=(vmem,) * 4,
        scratch_shapes=[
            pltpu.VMEM((L, width), bf16),
            pltpu.VMEM((heads, U, 128), bf16),
            pltpu.VMEM((L // U, heads * U, U), f32),
            pltpu.VMEM((L // U, heads * U, U), f32),
            pltpu.VMEM((L, 128), f32),
            pltpu.VMEM((L, 128), f32),
            pltpu.VMEM((L, cols), bf16),
            pltpu.VMEM((L, width), bf16),
            pltpu.VMEM((width, cols), bf16),
            pltpu.VMEM((heads * HEAD, width), bf16),
            pltpu.VMEM((width // 4, cols), bf16),
        ]
        + line_sems(4)
        + sum_scratch(T, width)
        + dp_scratch(width // 4, cols)
        + dp_scratch(rows, width)
        + [pltpu.SemaphoreType.DMA((8,))] * 4
        + [pltpu.SemaphoreType.DMA] * 2,
        compiler_params=pltpu.CompilerParams(
            collective_id=cid, has_side_effects=True, vmem_limit_bytes=67000000
        ),
        name="attention_back",
    )(dm, q2, k2, kz, vz, lse, attended, s1_all, w_qkv, w_o2, table, g_gu)


def spread_kernel(
    down_rows, repeats, gu_ref, qkv_ref, wg_ref, wu_ref, wq_ref, wk_ref, wv_ref, one_ref, two_ref,
    gate_ref, up_ref, query_ref, key_ref, value_ref, gain1_ref, gain2_ref,
):
    S, rows, wide = gu_ref.shape
    F = wide // 2
    Dp = gate_ref.shape[1] // (S * down_rows)
    q_cols = query_ref.shape[1] // S
    for s in range(S):
        for d in range(Dp):
            to = pl.ds((d * S + s) * down_rows, down_rows)
            gate_ref[:, to] = gu_ref[s, :, d * down_rows : (d + 1) * down_rows].astype(f32)
            up_ref[:, to] = gu_ref[s, :, F + d * down_rows : F + (d + 1) * down_rows].astype(f32)
        query_ref[:, s * q_cols : (s + 1) * q_cols] = qkv_ref[s, :, :q_cols].astype(f32)
    for j in range(S // repeats):
        total = qkv_ref[j * repeats, :, q_cols:].astype(f32)
        for s in range(j * repeats + 1, (j + 1) * repeats):
            total = total + qkv_ref[s, :, q_cols:].astype(f32)
        key_ref[:, j * HEAD : (j + 1) * HEAD] = total[:, :HEAD]
        value_ref[:, j * HEAD : (j + 1) * HEAD] = total[:, HEAD:]

    def close(pairs, gain_ref, out_ref):
        total = jnp.zeros((rows, 1), f32)
        for weight_ref, grad_ref in pairs:
            grad = grad_ref[...]
            total = total + jnp.sum(weight_ref[...].astype(f32) * grad, axis=1, keepdims=True)
            grad_ref[...] = grad * gain_ref[...]
        out_ref[...] = total

    close(((wg_ref, gate_ref), (wu_ref, up_ref)), two_ref, gain2_ref)
    close(((wq_ref, query_ref), (wk_ref, key_ref), (wv_ref, value_ref)), one_ref, gain1_ref)


def spread(gu, qkv, weights, gains, down_rows, repeats):
    rows = gu.shape[1]
    outs = [jax.ShapeDtypeStruct(w.shape, f32) for w in weights]
    outs += [jax.ShapeDtypeStruct((rows, 1), f32)] * 2
    vmem = pl.BlockSpec(memory_space=pltpu.VMEM)
    return pl.pallas_call(
        functools.partial(spread_kernel, down_rows, repeats),
        out_shape=tuple(outs),
        in_specs=[vmem] * 9,
        out_specs=(vmem,) * 7,
        compiler_params=pltpu.CompilerParams(vmem_limit_bytes=40 << 20),
        name="spread",
    )(gu, qkv, *weights, *gains)


def gather_seq(rows):
    if lax.axis_size("seq") == 8:
        return gather_line(rows)
    return lax.all_gather(rows, "seq", axis=0, tiled=True)


def scatter_seq(rows):
    if lax.axis_size("seq") == 8:
        return scatter_line(rows)
    return lax.psum_scatter(rows, "seq", scatter_dimension=0, tiled=True).astype(f32)


def feedforward_plain(x, dy_all, w_gu, w_d):
    hidden = w_d.shape[0]
    s2_all = gather_seq(x)
    gate_up = mm(s2_all, w_gu)
    gate, up = gate_up[:, :hidden], gate_up[:, hidden:]
    sig = jax.nn.sigmoid(gate)
    hid = (gate * sig * up).astype(bf16)
    d_hid = mm_nt(dy_all, w_d)
    d_gate = (d_hid * up * sig * (1.0 + gate * (1.0 - sig))).astype(bf16)
    d_up = (d_hid * (gate * sig)).astype(bf16)
    d_gu = jnp.concatenate([d_gate, d_up], axis=1)
    return (
        scatter_seq(mm(hid, w_d).astype(bf16)),
        scatter_seq(mm_nt(d_gu, w_gu).astype(bf16)),
        scatter_dp(mm_tn(s2_all, d_gu).astype(bf16)),
        scatter_dp(mm_tn(hid, dy_all).astype(bf16)).astype(f32),
    )


def gather_dp(rows):
    return lax.all_gather(rows, "dp", axis=0, tiled=True)


def scatter_dp(rows):
    return lax.psum_scatter(rows, "dp", scatter_dimension=0, tiled=True)


def exchange_seq(pieces):
    return lax.all_to_all(pieces, "seq", split_axis=0, concat_axis=0, tiled=True)


def causal_mask(offset, block_rows, block_end):
    return jnp.arange(block_end)[None, :] <= (offset + jnp.arange(block_rows))[:, None]


def attention_forward(queries, keys, values, block_rows):
    outputs, totals = [], []
    for offset in range(0, queries.shape[1], block_rows):
        end = offset + block_rows
        scores = jnp.einsum(
            "hqd,kd->hqk", queries[:, offset:end], keys[:end], preferred_element_type=f32
        ) * HEAD ** (-0.5)
        scores = jnp.where(causal_mask(offset, block_rows, end), scores, masked)
        row_max = jnp.max(scores, axis=-1, keepdims=True)
        total = row_max + jnp.log(jnp.sum(jnp.exp(scores - row_max), axis=-1, keepdims=True))
        probs_low = jnp.exp(scores - total).astype(bf16)
        outputs.append(
            jnp.einsum("hqk,kd->hqd", probs_low, values[:end], preferred_element_type=f32).astype(
                bf16
            )
        )
        totals.append(total)
    return jnp.concatenate(outputs, axis=1), jnp.concatenate(totals, axis=1)


def attention_backward(queries, keys, values, grads, totals, block_rows):
    length = keys.shape[0]
    scale = HEAD ** (-0.5)
    key_sum = jnp.zeros((length, HEAD), f32)
    value_sum = jnp.zeros((length, HEAD), f32)
    query_parts = []
    for offset in range(0, length, block_rows):
        end = offset + block_rows
        query_block, grad_block = queries[:, offset:end], grads[:, offset:end]
        key_block, value_block = keys[:end], values[:end]
        scores = (
            jnp.einsum("hqd,kd->hqk", query_block, key_block, preferred_element_type=f32) * scale
        )
        scores = jnp.where(causal_mask(offset, block_rows, end), scores, masked)
        probs = jnp.exp(scores - totals[:, offset:end])
        probs_low = probs.astype(bf16)
        grad_probs = jnp.einsum(
            "hqd,kd->hqk", grad_block, value_block, preferred_element_type=f32
        )
        inner = jnp.sum(probs * grad_probs, axis=-1, keepdims=True)
        grad_scores = (probs * (grad_probs - inner)).astype(bf16)
        query_parts.append(
            jnp.einsum("hqk,kd->hqd", grad_scores, key_block, preferred_element_type=f32) * scale
        )
        padding = ((0, length - end), (0, 0))
        key_sum = key_sum + jnp.pad(
            jnp.einsum("hqk,hqd->kd", grad_scores, query_block, preferred_element_type=f32)
            * scale,
            padding,
        )
        value_sum = value_sum + jnp.pad(
            jnp.einsum("hqk,hqd->kd", probs_low, grad_block, preferred_element_type=f32), padding
        )
    return jnp.concatenate(query_parts, axis=1), key_sum, value_sum


def heads_first(flat, heads):
    return jnp.transpose(flat.reshape(flat.shape[0], heads, HEAD), (1, 0, 2))


def heads_last(stacked):
    return jnp.transpose(stacked, (1, 0, 2)).reshape(stacked.shape[1], -1)


def shards(
    inputs,
    attention_gain,
    query_weight,
    key_weight,
    value_weight,
    output_weight,
    feedforward_gain,
    gate_weight,
    up_weight,
    down_weight,
    cotangent,
):
    S, Dp = lax.axis_size("seq"), lax.axis_size("dp")
    sequences, tokens, width = inputs.shape
    length = tokens * S
    rows = query_weight.shape[0]
    heads = H // S
    q_cols = heads * HEAD
    repeats = S // KV
    down_rows = down_weight.shape[0]
    hidden = down_rows * Dp
    block_rows = min(length, max(512, length // 8))

    gain_one = attention_gain.astype(f32)[:, None]
    gain_two = feedforward_gain.astype(f32)[:, None]

    def folded(weight, gain):
        return (weight.astype(f32) * gain).astype(bf16)

    def per_group_kv(weight):
        return jnp.repeat(weight.reshape(rows, KV, HEAD), repeats, axis=1)

    def per_group_hidden(weight):
        return jnp.transpose(weight.reshape(rows, Dp, S, down_rows), (2, 0, 1, 3)).reshape(
            S, rows, hidden
        )

    packed = jnp.concatenate(
        [
            folded(query_weight, gain_one).reshape(rows, S, q_cols),
            per_group_kv(folded(key_weight, gain_one)),
            per_group_kv(folded(value_weight, gain_one)),
        ],
        axis=2,
    )
    packed_qkv = jnp.transpose(packed, (1, 0, 2))
    forward_perm = [(Dp * s + d, d * S + s) for s in range(S) for d in range(Dp)]
    backward_perm = [(b, a) for a, b in forward_perm]
    line = S == 8 and Dp == 4
    width_f = -(-hidden // 256) * 256 if line else hidden

    def padded(part, axis):
        pads = [(0, 0)] * part.ndim
        pads[axis] = (0, width_f - hidden)
        return jnp.pad(part, pads)

    packed_gu = jnp.concatenate(
        [
            padded(per_group_hidden(folded(gate_weight, gain_two)), 2),
            padded(per_group_hidden(folded(up_weight, gain_two)), 2),
        ],
        axis=2,
    )

    flat = inputs.reshape(tokens, width).astype(f32)
    r1 = rms_scale(flat)
    s1 = flat * r1
    cosine, sine = rope_tables(length)
    dy = cotangent.reshape(tokens, width)
    if line:
        lane = jnp.arange(128)[None, :]
        frequency = 10000.0 ** (-((lane % (HEAD // 2)).astype(f32) * 2.0) / HEAD)
        angles = jnp.arange(length, dtype=f32)[:, None] * frequency
        turn_cos = jnp.cos(angles)
        turn_sin = jnp.where(lane % HEAD < HEAD // 2, -1.0, 1.0) * jnp.sin(angles)
        outs = attention_front(
            s1.astype(bf16),
            (query_weight, key_weight, value_weight, gate_weight, up_weight),
            (gain_one, gain_two),
            output_weight,
            down_weight,
            dy,
            turn_cos,
            turn_sin,
            width_f,
            repeats,
        )
        summed, s1_all, dy_all, w_qkv, w_gu, w_d, w_o, q2, k2, kz, vz, totals, attended = outs
    else:
        w_qkv = gather_dp(exchange_seq(packed_qkv).reshape(S * rows, q_cols + 2 * HEAD))
        w_gu = gather_dp(exchange_seq(packed_gu).reshape(S * rows, 2 * hidden))
        w_o = gather_dp(lax.ppermute(output_weight, ("dp", "seq"), forward_perm))
        w_d = gather_dp(down_weight)
        s1_all = gather_seq(s1.astype(bf16))
        qkv = mm(s1_all, w_qkv)
        queries = rotate(qkv[:, :q_cols].reshape(length, heads, HEAD), cosine, sine).astype(bf16)
        queries = jnp.transpose(queries, (1, 0, 2))
        keys = rotate(qkv[:, None, q_cols : q_cols + HEAD], cosine, sine).astype(bf16)[:, 0]
        values = qkv[:, q_cols + HEAD :].astype(bf16)
        attended, totals = attention_forward(queries, keys, values, block_rows)
        attended = heads_last(attended)
        summed = scatter_seq(mm(attended, w_o).astype(bf16))
        dy_all = gather_seq(dy)
    middle = flat + summed
    r2 = rms_scale(middle)
    s2 = middle * r2
    if line:
        out_sum, e2, g_gu, down_grad = feedforward(
            s2.astype(bf16), dy_all, w_gu, w_d, down_rows
        )
    else:
        out_sum, e2, g_gu, down_grad = feedforward_plain(s2.astype(bf16), dy_all, w_gu, w_d)

    d_middle = dy.astype(f32) + r2 * (e2 - s2 * jnp.mean(e2 * s2, axis=-1, keepdims=True))
    if line:
        table = jnp.where(lane < HEAD, turn_cos, -turn_sin) * HEAD ** (-0.5)

        def with_zeros(u):
            return jnp.concatenate([u, jnp.zeros_like(u)], axis=-1)

        w_o2 = with_zeros(w_o.reshape(heads, 1, HEAD, width).swapaxes(2, 3)).swapaxes(2, 3)
        e1, g_qkv, g_o, g_gu = attention_back(
            d_middle.astype(bf16),
            q2,
            k2,
            kz,
            vz,
            totals,
            attended,
            s1_all,
            w_qkv,
            w_o2.reshape(2 * q_cols, width),
            table,
            g_gu,
            rows,
        )
    else:
        g_gu = exchange_seq(g_gu.reshape(S, rows, 2 * width_f))
        dm_all = gather_seq(d_middle.astype(bf16))
        d_att = heads_first(mm_nt(dm_all, w_o).astype(bf16), heads)
        d_q, d_k, d_v = attention_backward(queries, keys, values, d_att, totals, block_rows)
        d_q = jnp.transpose(d_q, (1, 0, 2))
        d_qkv = jnp.concatenate(
            [
                rotate(d_q, cosine, -sine).reshape(length, q_cols).astype(bf16),
                rotate(d_k[:, None], cosine, -sine)[:, 0].astype(bf16),
                d_v.astype(bf16),
            ],
            axis=1,
        )
        e1 = scatter_seq(mm_nt(d_qkv, w_qkv).astype(bf16))
        g_o = scatter_dp(mm_tn(attended, dm_all).astype(bf16))
        g_qkv = scatter_dp(mm_tn(s1_all, d_qkv).astype(bf16))
        g_qkv = exchange_seq(g_qkv.reshape(S, rows, q_cols + 2 * HEAD))
    output = (middle + out_sum).astype(bf16)
    input_grad = d_middle + r1 * (e1 - s1 * jnp.mean(e1 * s1, axis=-1, keepdims=True))
    output_grad = lax.ppermute(g_o, ("dp", "seq"), backward_perm).astype(f32)

    if line:
        g_gate, g_up, g_query, g_key, g_value, gain_one_grad, gain_two_grad = spread(
            g_gu,
            g_qkv,
            (gate_weight, up_weight, query_weight, key_weight, value_weight),
            (gain_one, gain_two),
            down_rows,
            repeats,
        )
        return (
            output.reshape(sequences, tokens, width),
            input_grad.reshape(sequences, tokens, width),
            gain_one_grad[:, 0],
            g_query,
            g_key,
            g_value,
            output_grad,
            gain_two_grad[:, 0],
            g_gate,
            g_up,
            down_grad,
        )

    g_gu, g_qkv = g_gu.astype(f32), g_qkv.astype(f32)

    def back_hidden(part):
        return jnp.transpose(part.reshape(S, rows, Dp, down_rows), (1, 2, 0, 3)).reshape(rows, -1)

    def back_kv(part):
        part = jnp.sum(part.reshape(KV, repeats, rows, HEAD), axis=1)
        return jnp.transpose(part, (1, 0, 2)).reshape(rows, KV * HEAD)

    g_gate, g_up = back_hidden(g_gu[..., :hidden]), back_hidden(g_gu[..., hidden:])
    g_query = jnp.transpose(g_qkv[..., :q_cols], (1, 0, 2)).reshape(rows, width)
    g_key = back_kv(g_qkv[..., q_cols : q_cols + HEAD])
    g_value = back_kv(g_qkv[..., q_cols + HEAD :])

    def row_dot(weight, grad):
        return jnp.sum(weight.astype(f32) * grad, axis=1)

    gain_two_grad = row_dot(gate_weight, g_gate) + row_dot(up_weight, g_up)
    gain_one_grad = (
        row_dot(query_weight, g_query) + row_dot(key_weight, g_key) + row_dot(value_weight, g_value)
    )
    return (
        output.reshape(sequences, tokens, width),
        input_grad.reshape(sequences, tokens, width),
        gain_one_grad,
        g_query * gain_one,
        g_key * gain_one,
        g_value * gain_one,
        output_grad,
        gain_two_grad,
        g_gate * gain_two,
        g_up * gain_two,
        down_grad,
    )


def solution(mesh):
    both = ("dp", "seq")
    tok, vec, mat = P("dp", "seq", None), P(both), P(both, None)
    in_specs = (tok, vec, mat, mat, mat, mat, vec, mat, mat, mat, tok)
    out_specs = (tok, tok, vec, mat, mat, mat, mat, vec, mat, mat, mat)
    return jax.shard_map(shards, mesh=mesh, in_specs=in_specs, out_specs=out_specs, check_vma=False)
```
